32 devices in a mesh: dp: 8 (over z, core), tensor: 4 (over y, x).
Axes of the slice: x: 2, y: 2, z: 4, core: 2. Of those that a mesh axis runs over, the one named last changes fastest.
Arguments:
- tokens: bfloat16 [16384, 1024], P(('dp', 'tensor')), may hold values from -6 to 6
- first_values: bfloat16 [16384, 1024], P(('dp', 'tensor')), may hold values from -10 to 10
- doc_lengths: int32 [8, 8], P('dp'), may hold values from 1 to 1024, 2048 in all within a row
- attention_norm_gain: float32 [1024], replicated, may hold values from 0.5 to 1.5
- w_qkv: bfloat16 [1024, 3072], P(None, 'tensor'), may hold values from -0.1875 to 0.1875
- w_out: bfloat16 [1024, 1024], P('tensor'), may hold values from -2 to 2
- feedforward_norm_gain: float32 [1024], replicated, may hold values from 0.5 to 1.5
- w_gate: bfloat16 [1024, 2816], P(None, 'tensor'), may hold values from -0.1875 to 0.1875
- w_up: bfloat16 [1024, 2816], P(None, 'tensor'), may hold values from -0.1875 to 0.1875
- w_down: bfloat16 [2816, 1024], P('tensor'), may hold values from -0.109375 to 0.109375
- out_grad: bfloat16 [16384, 1024], P(('dp', 'tensor')), may hold values from -6 to 6
Outputs:
- out: bfloat16 [16384, 1024], P(('dp', 'tensor'))
- tokens_grad: float32 [16384, 1024], P(('dp', 'tensor'))
- first_values_grad: float32 [16384, 1024], P(('dp', 'tensor'))
- attn_gain_grad: float32 [1024], replicated
- w_qkv_grad: float32 [1024, 3072], P('dp', 'tensor')
- w_out_grad: float32 [1024, 1024], P('tensor', 'dp')
- ffn_gain_grad: float32 [1024], replicated
- w_gate_grad: float32 [1024, 2816], P('dp', 'tensor')
- w_up_grad: float32 [1024, 2816], P('dp', 'tensor')
- w_down_grad: float32 [2816, 1024], P('tensor', 'dp')
- first_values_rms: float32 [], replicated
- values_rms: float32 [], replicated
The draws below stay inside these ranges and needn't reach their ends.
Inputs may be any that keep to these rules, and one draw needn't show every extreme that they name: `doc_lengths`: the lengths of a row sum to 2048, and its longest document has 1024 tokens.
All inputs are finite; a program needn't handle non-finite values.
Results may differ from the reference program's by a relative error of at most 0.023.
Values may be sent and summed in bfloat16 or wider, within the bound.
No kernel may reach another device: no remote copies, remote signals or barrier semaphores. Data moves between devices by JAX's collectives and lax.ppermute only.
A program may use at most 192 MiB of HBM per device.

```python
import math
import jax
import jax.numpy as jnp
import numpy as np
from jax import lax

D = 1024
H = 16
HD = 64
FF = 2816
LEN = 2048
DOCS = 8
MOST_DOC = 1024
SEQS = 8
TOKENS = 16384


def draw_first_values(key, part):
    places = jnp.arange(TOKENS, dtype=jnp.float32)[:, None] / TOKENS
    row_scale = 0.4 + 1.6 * places
    noise = jnp.clip(jax.random.normal(key, (TOKENS, H * HD), jnp.float32), -5.0, 5.0)
    return (noise * row_scale).astype(jnp.bfloat16)


def raised(values, own_key, source, target, shards_of, factor):
    def block_of(axis_at):
        return (jnp.arange(values.shape[axis_at]) // (values.shape[axis_at] // shards_of)).reshape((-1,) + (1,) * (values.ndim - 1 - axis_at))

    one_side = jax.random.permutation(own_key, shards_of)[block_of(target)]
    far = (block_of(target) + shards_of // 2) % shards_of
    return jnp.where((block_of(source) == one_side) | (block_of(source) == far), factor * values, values)


def level_of(own_key, dims, cuts, smallest, high):
    level, own = 1.0, jax.random.fold_in(own_key, 6)
    for axis_at, parts in cuts:
        heights = jnp.exp(jax.random.uniform(jax.random.fold_in(own, axis_at), (parts,), jnp.float32, smallest / len(cuts), high / len(cuts)))
        level = level * jnp.repeat(heights, dims[axis_at] // parts).reshape([-1 if axis == axis_at else 1 for axis in range(len(dims))])
    return level


def length_profile(count, total, reach, lean):
    loads = [(1 << 20) // math.isqrt(standing ** lean) + 1 for standing in range(2, count + 1)]
    surplus, holding = total - reach - (count - 1), [1] * (count - 1)
    while surplus > 0:
        movable = [i for i in range(count - 1) if holding[i] < reach]
        whole, remaining = sum([loads[i] for i in movable]), surplus
        for i in movable:
            more = min(reach - holding[i], max(1, remaining * loads[i] // whole), surplus)
            holding[i] = holding[i] + more
            surplus = surplus - more
    return np.array([reach] + holding)


def uneven_parts(stream_key, amount, total, reach, slope):
    if amount == 2:
        one = jax.random.randint(stream_key, (), max(1, total - reach), min(reach, total - 1) + 1)
        return jnp.stack([one, total - one])
    sizes = jnp.asarray(length_profile(amount, total, reach, slope), jnp.int32)
    twos = (amount - 1) // 2
    giver, taker = sizes[1:1 + 2 * twos:2], sizes[2:2 + 2 * twos:2]
    room = jnp.minimum(giver - 1, reach - taker)
    passed = jax.random.randint(jax.random.fold_in(stream_key, 1), (twos,), 0, 1 << 20) % (room + 1)
    sizes = sizes.at[1:1 + 2 * twos:2].set(giver - passed).at[2:2 + 2 * twos:2].set(taker + passed)
    return sizes[jax.random.permutation(jax.random.fold_in(stream_key, 2), amount)]


def bell_draw(rng, shape, scale, bound, split=(), kind=jnp.bfloat16):
    factor_of = level_of(rng, shape, split, -0.22, 0.18) if split else 1.0
    values = jax.random.normal(rng, shape, jnp.float32) * scale * factor_of
    return jnp.minimum(jnp.maximum(values, -bound), bound).astype(kind)


def bell_draw_with(rng, shape, scale, limit, pieces, heavy, kind=jnp.bfloat16):
    drawn = scale * jax.random.normal(rng, shape, jnp.float32)
    if pieces:
        drawn = drawn * level_of(rng, shape, pieces, -0.22, 0.18)
    return jnp.clip(raised(drawn, jax.random.fold_in(rng, 3), *heavy), -limit, limit).astype(kind)


def setup_inputs(seed: int = 0) -> dict:
    arg_keys = jax.random.split(jax.random.key(seed), 12)
    tokens = bell_draw(arg_keys[0], (TOKENS, D), 1.0, 6.0, ((0, 32),))
    first_values = draw_first_values(jax.random.fold_in(arg_keys[11], 71), 0)
    doc_lengths = jax.vmap(lambda own: uneven_parts(own, DOCS, LEN, MOST_DOC, 2))(jax.random.split(arg_keys[2], SEQS)).reshape((SEQS, DOCS)).astype(jnp.int32)
    attention_norm_gain = jnp.clip(1.0 + 0.1 * jax.random.normal(arg_keys[3], (D,), jnp.float32), 0.5, 1.5)
    w_qkv = bell_draw(arg_keys[4], (D, 3 * H * HD), D ** -0.5, 0.1875, ((1, 4),))
    w_out = bell_draw(arg_keys[5], (H * HD, D), (max(H * HD // 128, 1)) ** -0.5, 2.0, ((0, 4),))
    feedforward_norm_gain = jnp.clip(1.0 + 0.1 * jax.random.normal(arg_keys[6], (D,), jnp.float32), 0.5, 1.5)
    w_gate = bell_draw(arg_keys[7], (D, FF), D ** -0.5, 0.1875, ((1, 4),))
    w_up = bell_draw(arg_keys[8], (D, FF), D ** -0.5, 0.1875, ((1, 4),))
    w_down = bell_draw(arg_keys[9], (FF, D), FF ** -0.5, 0.109375, ((0, 4),))
    out_grad = bell_draw_with(arg_keys[10], (TOKENS, D), 1.0, 6.0, ((0, 32),), (0, 1, 32, 2.75))
    return dict(tokens=tokens, first_values=first_values, doc_lengths=doc_lengths, attention_norm_gain=attention_norm_gain, w_qkv=w_qkv, w_out=w_out, feedforward_norm_gain=feedforward_norm_gain, w_gate=w_gate, w_up=w_up, w_down=w_down, out_grad=out_grad)


EPS = 1e-06

@jax.custom_vjp
def low(v):
    return lax.optimization_barrier(v.astype(jnp.bfloat16)).astype(jnp.float32)

@jax.custom_vjp
def low_back(v):
    return v

def low_keep(v):
    return (low(v), None)

def low_pass(kept, grad):
    return (grad,)

def back_keep(v):
    return (v, None)

def back_low(kept, grad):
    return (low(grad),)
low.defvjp(low_keep, low_pass)
low_back.defvjp(back_keep, back_low)

def matmul_hi(left, right):
    return jnp.dot(left, right, precision=lax.Precision.HIGHEST)

def rope_tables(length, head_width):
    half_width = head_width // 2
    inverse = jnp.exp(-math.log(10000.0) * jnp.arange(half_width, dtype=jnp.float32) / half_width)
    angles = jnp.arange(length, dtype=jnp.float32)[:, None] * inverse[None, :]
    return (jnp.cos(angles), jnp.sin(angles))

def rotate(vectors, cosine, sine_table):
    half_width = vectors.shape[-1] // 2
    first_half = vectors[..., :half_width]
    second_half = vectors[..., half_width:]
    cos_b = cosine[:, None, :]
    sin_b = sine_table[:, None, :]
    return jnp.concatenate([first_half * cos_b - second_half * sin_b, first_half * sin_b + second_half * cos_b], axis=-1)

def document_ids(lengths, length):
    doc_ends = jnp.cumsum(lengths, axis=-1).astype(jnp.int32)
    places = jnp.arange(length, dtype=jnp.int32)
    return lax.optimization_barrier(jnp.sum((places[None, :, None] >= doc_ends[:, None, :]).astype(jnp.int32), axis=-1))

def both_ways(value):
    return low_back(low(value))

def attend_heads(queries, key_rows, value_rows, allowed):

    def one_head(head_items):
        query_head, key_head, value_head = head_items
        scores = low_back(matmul_hi(query_head, key_head.T) * HD ** (-0.5))
        scores = jnp.where(allowed, scores, -1e+30)
        row_max = lax.optimization_barrier(jnp.max(scores, axis=-1, keepdims=True))
        weights = jnp.exp(scores - row_max)
        probabilities = weights / lax.optimization_barrier(jnp.sum(weights, axis=-1, keepdims=True))
        return matmul_hi(low(probabilities), value_head)
    outputs = lax.map(jax.checkpoint(one_head), (queries.transpose(1, 0, 2), key_rows.transpose(1, 0, 2), value_rows.transpose(1, 0, 2)))
    return outputs.transpose(1, 0, 2).reshape(queries.shape[0], H * HD)

def layer(params, row_in, first_row, doc_row):
    attention_norm_gain, w_qkv, w_out, feedforward_norm_gain, w_gate, w_up, w_down = params
    length = row_in.shape[0]
    cosine, sine_table = rope_tables(length, HD)
    first_inverse_rms = lax.rsqrt(lax.optimization_barrier(jnp.mean(row_in * row_in, axis=-1, keepdims=True)) + EPS)
    first_normed_rows = low(row_in * first_inverse_rms * attention_norm_gain)
    projected = low_back(matmul_hi(first_normed_rows, w_qkv)).reshape(length, H, 3, HD)
    queries = low(rotate(projected[:, :, 0], cosine, sine_table))
    key_rows = low(rotate(projected[:, :, 1], cosine, sine_table))
    mixed_values = 0.5 * projected[:, :, 2] + 0.5 * first_row.reshape(length, H, HD)
    value_rows = both_ways(mixed_values)
    places = jnp.arange(length, dtype=jnp.int32)
    allowed = (doc_row[:, None] == doc_row[None, :]) & (places[:, None] >= places[None, :])
    attended = both_ways(attend_heads(queries, key_rows, value_rows, allowed))
    middle_stream = row_in + low_back(matmul_hi(attended, w_out))
    second_inverse_rms = lax.rsqrt(lax.optimization_barrier(jnp.mean(middle_stream * middle_stream, axis=-1, keepdims=True)) + EPS)
    second_normed_rows = low(middle_stream * second_inverse_rms * feedforward_norm_gain)
    gate_act = low_back(matmul_hi(second_normed_rows, w_gate))
    up_act = low_back(matmul_hi(second_normed_rows, w_up))
    hidden = low(jax.nn.silu(gate_act) * up_act)
    result = middle_stream + low_back(matmul_hi(hidden, w_down))
    return (result, jnp.sum(mixed_values * mixed_values))

def reference(tokens, first_values, doc_lengths, attention_norm_gain, w_qkv, w_out, feedforward_norm_gain, w_gate, w_up, w_down, out_grad):
    row_count = doc_lengths.shape[0]
    params = (attention_norm_gain.astype(jnp.float32), w_qkv.astype(jnp.float32), w_out.astype(jnp.float32), feedforward_norm_gain.astype(jnp.float32), w_gate.astype(jnp.float32), w_up.astype(jnp.float32), w_down.astype(jnp.float32))
    rows_in = tokens.astype(jnp.float32).reshape(row_count, LEN, D)
    first_rows = first_values.astype(jnp.float32).reshape(row_count, LEN, H * HD)
    grad_rows = out_grad.astype(jnp.float32).reshape(row_count, LEN, D)
    doc_table = document_ids(doc_lengths, LEN)

    def row_step(scan_state, row_items):
        summed, squares = scan_state
        row_in, first_row, doc_row, grad_row = row_items
        result, pull_back, square_part = jax.vjp(lambda p_set, a_row, b_row: layer(p_set, a_row, b_row, doc_row), params, row_in, first_row, has_aux=True)
        param_grads, input_grad, first_grad = pull_back(grad_row)
        summed = jax.tree.map(lambda left, right: left + right, summed, param_grads)
        return ((summed, squares + square_part), (result.astype(jnp.bfloat16), input_grad, first_grad))
    start_state = (jax.tree.map(jnp.zeros_like, params), jnp.zeros((), jnp.float32))
    (summed, squares), (results, input_grads, first_grads) = lax.scan(row_step, start_state, (rows_in, first_rows, doc_table, grad_rows))
    entry_count = TOKENS * H * HD
    first_all = first_values.astype(jnp.float32)
    first_rms = jnp.sqrt(jnp.mean(first_all * first_all))
    return (results.reshape(TOKENS, D), input_grads.reshape(TOKENS, D), first_grads.reshape(TOKENS, H * HD), summed[0], summed[1], summed[2], summed[3], summed[4], summed[5], summed[6], first_rms, jnp.sqrt(squares / entry_count))
```

```python
import functools
import math

import jax
import jax.numpy as jnp
import numpy as np
from jax import lax
from jax.experimental import pallas as pl
from jax.experimental.pallas import tpu as pltpu
from jax.sharding import PartitionSpec as P

HD = 64
HALF = HD // 2
LANES = 128
GROUP = LANES // HALF
EPS = 1e-06
NEG = -1e30
f32 = jnp.float32
bf16 = jnp.bfloat16


def rope_tables(length):
    inverse = jnp.exp(-math.log(10000.0) * jnp.arange(HALF, dtype=f32) / HALF)
    angles = jnp.arange(length, dtype=f32)[:, None] * inverse[None, :]
    tile = lambda t: jnp.concatenate([t] * GROUP, axis=1)
    return tile(jnp.cos(angles)), tile(jnp.sin(angles))


def column_order(heads):
    value_width = max(LANES, heads * HD)
    order = np.full((4 * LANES + value_width,), -1, np.int32)
    for h in range(heads):
        for part in range(2):
            for half in range(2):
                at = (2 * part + half) * LANES + h * HALF
                src = h * 3 * HD + part * HD + half * HALF
                order[at : at + HALF] = np.arange(src, src + HALF)
        order[4 * LANES + h * HD : 4 * LANES + (h + 1) * HD] = np.arange(
            h * 3 * HD + 2 * HD, (h + 1) * 3 * HD
        )
    return order


def column_selector(heads):
    order = jnp.asarray(column_order(heads))
    rows = jnp.arange(3 * heads * HD, dtype=jnp.int32)
    return (rows[:, None] == order[None, :]).astype(bf16)


def dot_nt(a, b):
    return lax.dot_general(a, b, (((1,), (1,)), ((), ())), preferred_element_type=f32)


def dot_tn(a, b):
    return lax.dot_general(a, b, (((0,), (0,)), ((), ())), preferred_element_type=f32)


def dot_nn(a, b):
    return jnp.dot(a, b, preferred_element_type=f32)


def project_kernel(
    heads, x_ref, w_ref, fv_ref, cos_ref, sin_ref, lim_ref, q_ref, k_ref, v_ref, sq_ref
):
    rows = x_ref.shape[0]
    at = pl.program_id(0)
    acc = dot_nn(x_ref[...], w_ref[...])
    c, s = cos_ref[...], sin_ref[...]
    lane = lax.broadcasted_iota(jnp.int32, (rows, LANES), 1)
    place = at * rows + lax.broadcasted_iota(jnp.int32, (rows, LANES), 0)
    inside = (place >= lim_ref[0:1, :]) & (place < lim_ref[1:2, :])
    doc_lane = (lane >= HD) & (lane < HD + 8)
    q_extra = jnp.where(doc_lane & jnp.logical_not(inside), NEG, 0.0)
    k_extra = jnp.where(inside, 1.0, jnp.where((lane >= HD + 8) & (lane < HD + 11), 1.0, 0.0))
    for ref, base, extra, scale in ((q_ref, 0, q_extra, HD**-0.5), (k_ref, 2, k_extra, 1.0)):
        u1 = acc[:, base * LANES : (base + 1) * LANES]
        u2 = acc[:, (base + 1) * LANES : (base + 2) * LANES]
        r1 = (u1 * c - u2 * s) * scale
        r2 = (u1 * s + u2 * c) * scale
        for h in range(heads):
            a = r1 if h == 0 else pltpu.roll(r1, LANES - HALF * h, 1)
            b = r2 if h == 1 else pltpu.roll(r2, (LANES + HALF - HALF * h) % LANES, 1)
            both = jnp.where(lane < HALF, a, jnp.where(lane < HD, b, extra))
            ref[:, h * LANES : (h + 1) * LANES] = both.astype(bf16)

    @pl.when(at == 0)
    def _():
        sq_ref[...] = jnp.zeros_like(sq_ref)

    width = fv_ref.shape[1]
    first = fv_ref[...].astype(f32)
    mixed = 0.5 * acc[:, 4 * LANES :] + 0.5 * first
    sq_ref[0:1, :] += jnp.sum(mixed * mixed, axis=0, keepdims=True)
    sq_ref[1:2, :] += jnp.sum(first * first, axis=0, keepdims=True)
    for h in range(heads):
        t = (h // 2) * LANES
        own = (lane < HD) if h % 2 == 0 else (lane >= HD)
        v_ref[:, h * LANES : (h + 1) * LANES] = jnp.where(
            own, mixed[:, t : t + LANES], 1.0
        ).astype(bf16)


def project(heads, x, w, fv, cos, sin, limits, rows=512):
    length = x.shape[0]
    width = fv.shape[1]
    row = lambda i: (i, 0)
    whole = lambda i: (0, 0)
    ext = heads * LANES
    return pl.pallas_call(
        functools.partial(project_kernel, heads),
        name="project",
        grid=(length // rows,),
        in_specs=[
            pl.BlockSpec((rows, x.shape[1]), row),
            pl.BlockSpec(w.shape, whole),
            pl.BlockSpec((rows, width), row),
            pl.BlockSpec((rows, LANES), row),
            pl.BlockSpec((rows, LANES), row),
            pl.BlockSpec((8, LANES), whole),
        ],
        out_specs=[
            pl.BlockSpec((rows, ext), row),
            pl.BlockSpec((rows, ext), row),
            pl.BlockSpec((rows, ext), row),
            pl.BlockSpec((8, width), whole),
        ],
        out_shape=[
            jax.ShapeDtypeStruct((length, ext), bf16),
            jax.ShapeDtypeStruct((length, ext), bf16),
            jax.ShapeDtypeStruct((length, ext), bf16),
            jax.ShapeDtypeStruct((8, width), f32),
        ],
        compiler_params=pltpu.CompilerParams(vmem_limit_bytes=40 << 20),
        cost_estimate=pl.CostEstimate(
            flops=2 * length * x.shape[1] * w.shape[1],
            bytes_accessed=2 * (x.size + w.size + fv.size + 3 * length * ext),
            transcendentals=0,
        ),
    )(x, w, fv, cos, sin, limits)


def pieces(x):
    hi = x.astype(bf16).astype(f32)
    mid = (x - hi).astype(bf16).astype(f32)
    return hi, mid, x - hi - mid


def attend_kernel(heads, block, begin_ref, q_ref, k_ref, v_ref, o_ref, qo_ref, m_ref, acc_ref):
    at = pl.program_id(0)
    lane = lax.broadcasted_iota(jnp.int32, (block, LANES), 1)
    r = lax.broadcasted_iota(jnp.int32, (block, block), 0)
    c = lax.broadcasted_iota(jnp.int32, (block, block), 1)
    causal = c <= r
    here = pl.ds(pl.multiple_of(at * block, block), block)
    col = [slice(h * LANES, (h + 1) * LANES) for h in range(heads)]
    for h in range(heads):
        s = dot_nt(q_ref[:, col[h]], k_ref[here, col[h]])
        s = jnp.where(causal, s, NEG)
        m = jnp.max(s, axis=1, keepdims=True)
        p = jnp.exp(s - m).astype(bf16)
        m_ref[:, col[h]] = jnp.broadcast_to(m, (block, LANES))
        acc_ref[:, col[h]] = dot_nn(p, v_ref[here, col[h]])

    def step(kb, carry):
        there = pl.ds(pl.multiple_of(kb * block, block), block)
        for h in range(heads):
            s = dot_nt(q_ref[:, col[h]], k_ref[there, col[h]])
            old = m_ref[:, col[h]]
            new = jnp.maximum(old, jnp.max(s, axis=1, keepdims=True))
            p = jnp.exp(s - jnp.concatenate([new] * (block // LANES), axis=1)).astype(bf16)
            m_ref[:, col[h]] = new
            acc_ref[:, col[h]] = acc_ref[:, col[h]] * jnp.exp(old - new) + dot_nn(
                p, v_ref[there, col[h]]
            )
        return carry

    lax.fori_loop(begin_ref[at], at, step, 0)
    low = lane < HD
    for t in range((heads + 1) // 2):
        a = acc_ref[:, col[2 * t]]
        b = acc_ref[:, col[2 * t + 1]] if 2 * t + 1 < heads else a
        total = pltpu.roll(jnp.where(low, b, a), HD, 1)
        o_ref[:, t * LANES : (t + 1) * LANES] = (jnp.where(low, a, b) / total).astype(bf16)
    for h in range(heads):
        a = acc_ref[:, col[h]]
        total = a if h % 2 == 0 else pltpu.roll(a, HD, 1)
        hi, mid, lo = pieces(-(m_ref[:, col[h]] + jnp.log(jnp.where(low, 1.0, total))))
        extra = jnp.where(
            lane == HD + 8, hi, jnp.where(lane == HD + 9, mid, jnp.where(lane == HD + 10, lo, 0.0))
        )
        fill = (lane >= HD + 8) & (lane < HD + 11)
        qo_ref[:, col[h]] = jnp.where(fill, extra, q_ref[:, col[h]].astype(f32)).astype(bf16)


def attend(heads, q, k, v, begins, block):
    length = q.shape[0]
    ext = heads * LANES
    width = max(LANES, heads * HD)
    row = lambda i, b: (i, 0)
    whole = lambda i, b: (0, 0)
    return pl.pallas_call(
        functools.partial(attend_kernel, heads, block),
        name="attend",
        grid_spec=pltpu.PrefetchScalarGridSpec(
            num_scalar_prefetch=1,
            grid=(length // block,),
            in_specs=[
                pl.BlockSpec((block, ext), row),
                pl.BlockSpec((length, ext), whole),
                pl.BlockSpec((length, ext), whole),
            ],
            out_specs=[pl.BlockSpec((block, width), row), pl.BlockSpec((block, ext), row)],
            scratch_shapes=[pltpu.VMEM((block, ext), f32), pltpu.VMEM((block, ext), f32)],
        ),
        out_shape=[
            jax.ShapeDtypeStruct((length, width), bf16),
            jax.ShapeDtypeStruct((length, ext), bf16),
        ],
        compiler_params=pltpu.CompilerParams(vmem_limit_bytes=40 << 20),
        cost_estimate=pl.CostEstimate(
            flops=2 * heads * length * length * LANES,
            bytes_accessed=2 * 5 * length * ext,
            transcendentals=heads * length * length // 2,
        ),
    )(begins, q, k, v)


def attend_back_kernel(
    heads, block, begin_ref, q_ref, k_ref, v_ref, do_ref, o_ref, cos_ref, sin_ref, g_ref,
    dk_ref, dv_ref, dq_ref, de_ref,
):
    at = pl.program_id(0)
    lane = lax.broadcasted_iota(jnp.int32, (block, LANES), 1)
    r = lax.broadcasted_iota(jnp.int32, (block, block), 0)
    c = lax.broadcasted_iota(jnp.int32, (block, block), 1)
    causal = r <= c
    low = lane < HD
    here = pl.ds(pl.multiple_of(at * block, block), block)
    col = [slice(h * LANES, (h + 1) * LANES) for h in range(heads)]

    for h in range(heads):
        t = slice((h // 2) * LANES, (h // 2 + 1) * LANES)
        own = low if h % 2 == 0 else jnp.logical_not(low)
        grad = do_ref[:, t].astype(f32)
        centre = jnp.sum(jnp.where(own, grad * o_ref[:, t].astype(f32), 0.0), axis=1, keepdims=True)
        hi, mid, lo = pieces(-jnp.broadcast_to(centre, (block, LANES)))
        spot = lane - (HD if h % 2 == 0 else 0)
        extra = jnp.where(spot == 0, hi, jnp.where(spot == 1, mid, jnp.where(spot == 2, lo, 0.0)))
        de_ref[:, col[h]] = jnp.where(own, grad, extra).astype(bf16)

    def pair(there, h, mask, first):
        st = dot_nt(k_ref[there, col[h]], q_ref[:, col[h]])
        p = jnp.exp(st)
        if mask is not None:
            p = jnp.where(mask, p, 0.0)
        dpt = dot_nt(v_ref[there, col[h]], de_ref[:, col[h]])
        ds = (p * dpt).astype(bf16)
        dv = dot_nn(p.astype(bf16), de_ref[:, col[h]])
        dk = dot_nn(ds, q_ref[:, col[h]])
        dq = dot_tn(ds, k_ref[there, col[h]])
        if first:
            dv_ref[there, col[h]] = dv
            dk_ref[there, col[h]] = dk
            dq_ref[:, col[h]] = dq
        else:
            dv_ref[there, col[h]] += dv
            dk_ref[there, col[h]] += dk
            dq_ref[:, col[h]] += dq

    for h in range(heads):
        pair(here, h, causal, True)

    def step(kb, carry):
        there = pl.ds(pl.multiple_of(kb * block, block), block)
        for h in range(heads):
            pair(there, h, None, False)
        return carry

    lax.fori_loop(begin_ref[at], at, step, 0)

    def turn_back(ref, rows, base, scale):
        u1 = u2 = None
        quarter = lane // HALF
        for h in range(heads):
            u = ref[rows, col[h]]
            a = u if h == 0 else pltpu.roll(u, HALF * h, 1)
            b = u if h == 1 else pltpu.roll(u, (LANES + HALF * h - HALF) % LANES, 1)
            u1 = a if h == 0 else jnp.where(quarter == h, a, u1)
            u2 = b if h == 0 else jnp.where(quarter == h, b, u2)
        if heads < GROUP:
            u1 = jnp.where(quarter < heads, u1, 0.0)
            u2 = jnp.where(quarter < heads, u2, 0.0)
        u1, u2 = u1 * scale, u2 * scale
        cs, sn = cos_ref[rows, :], sin_ref[rows, :]
        return (u1 * cs + u2 * sn).astype(bf16), (u2 * cs - u1 * sn).astype(bf16)

    def finish(i, carry):
        rows = pl.ds(pl.multiple_of(i * block, block), block)
        d1, d2 = turn_back(dk_ref, rows, 2, 1.0)
        g_ref[rows, 2 * LANES : 3 * LANES] = d1
        g_ref[rows, 3 * LANES : 4 * LANES] = d2
        for t in range((heads + 1) // 2):
            a = dv_ref[rows, col[2 * t]]
            b = dv_ref[rows, col[2 * t + 1]] if 2 * t + 1 < heads else jnp.zeros_like(a)
            d_mix = jnp.where(low, a, b).astype(bf16)
            g_ref[rows, (4 + t) * LANES : (5 + t) * LANES] = (d_mix.astype(f32) * 0.5).astype(bf16)
        return carry

    u1 = u2 = None
    quarter = lane // HALF
    for h in range(heads):
        u = dq_ref[:, col[h]]
        a = u if h == 0 else pltpu.roll(u, HALF * h, 1)
        b = u if h == 1 else pltpu.roll(u, (LANES + HALF * h - HALF) % LANES, 1)
        u1 = a if h == 0 else jnp.where(quarter == h, a, u1)
        u2 = b if h == 0 else jnp.where(quarter == h, b, u2)
    if heads < GROUP:
        u1 = jnp.where(quarter < heads, u1, 0.0)
        u2 = jnp.where(quarter < heads, u2, 0.0)
    u1, u2 = u1 * HD**-0.5, u2 * HD**-0.5
    cs, sn = cos_ref[here, :], sin_ref[here, :]
    g_ref[here, 0:LANES] = (u1 * cs + u2 * sn).astype(bf16)
    g_ref[here, LANES : 2 * LANES] = (u2 * cs - u1 * sn).astype(bf16)

    @pl.when(at == pl.num_programs(0) - 1)
    def _():
        lax.fori_loop(0, pl.num_programs(0), finish, 0)


def attend_back(heads, q, k, v, d_out, out, cos, sin, begins, block):
    length = q.shape[0]
    ext = heads * LANES
    width = out.shape[1]
    row = lambda i, b: (i, 0)
    whole = lambda i, b: (0, 0)
    return pl.pallas_call(
        functools.partial(attend_back_kernel, heads, block),
        name="attend_back",
        grid_spec=pltpu.PrefetchScalarGridSpec(
            num_scalar_prefetch=1,
            grid=(length // block,),
            in_specs=[
                pl.BlockSpec((block, ext), row),
                pl.BlockSpec((length, ext), whole),
                pl.BlockSpec((length, ext), whole),
                pl.BlockSpec((block, width), row),
                pl.BlockSpec((block, width), row),
                pl.BlockSpec((length, LANES), whole),
                pl.BlockSpec((length, LANES), whole),
            ],
            out_specs=pl.BlockSpec((length, 4 * LANES + width), whole),
            scratch_shapes=[
                pltpu.VMEM((length, ext), f32),
                pltpu.VMEM((length, ext), f32),
                pltpu.VMEM((block, ext), f32),
                pltpu.VMEM((block, ext), bf16),
            ],
        ),
        out_shape=jax.ShapeDtypeStruct((length, 4 * LANES + width), bf16),
        compiler_params=pltpu.CompilerParams(vmem_limit_bytes=48 << 20),
        cost_estimate=pl.CostEstimate(
            flops=5 * heads * length * length * LANES,
            bytes_accessed=2 * 8 * length * ext,
            transcendentals=heads * length * length // 2,
        ),
    )(begins, q, k, v, d_out, out, cos, sin)


def rms_normalize(row_block):
    inverse = lax.rsqrt(jnp.mean(row_block * row_block, axis=-1, keepdims=True) + EPS)
    return (row_block * inverse, inverse)


def rms_normalize_backward(normed, inverse, gain_vec, incoming):
    scaled = incoming * gain_vec
    inner_mean = jnp.mean(scaled * normed, axis=-1, keepdims=True)
    return (inverse * (scaled - normed * inner_mean), jnp.sum(incoming * normed, axis=0))


def shards(
    tokens,
    first_values,
    doc_lengths,
    attention_norm_gain,
    w_qkv,
    w_out,
    feedforward_norm_gain,
    w_gate,
    w_up,
    w_down,
    out_grad,
):
    local_rows = tokens.shape[0]
    heads = w_out.shape[0] // HD
    width = max(LANES, heads * HD)
    length = local_rows * lax.axis_size("tensor")
    block = 256
    cosine, sine_table = rope_tables(length)
    ends = jnp.cumsum(doc_lengths[0])
    starts = ends - doc_lengths[0]
    limits = jnp.zeros((8, LANES), jnp.int32)
    docs = doc_lengths.shape[1]
    limits = limits.at[0, HD : HD + docs].set(starts).at[1, HD : HD + docs].set(ends)
    heads_at = jnp.arange(length // block, dtype=jnp.int32) * block
    begins = jnp.max(jnp.where(starts[None, :] <= heads_at[:, None], starts[None, :], 0), axis=1)
    begins = (begins // block).astype(jnp.int32)
    select = column_selector(heads)
    w_cols = jnp.dot(w_qkv, select, preferred_element_type=f32).astype(bf16)

    residual_input = tokens.astype(f32)
    first_unit_rows, first_inverse_rms = rms_normalize(residual_input)
    first_normed_rows = (first_unit_rows * attention_norm_gain).astype(bf16)
    normed_all = lax.all_gather(first_normed_rows, "tensor", axis=0, tiled=True)
    first_local = lax.all_to_all(first_values, "tensor", split_axis=1, concat_axis=0, tiled=True)
    if width > heads * HD:
        first_local = jnp.pad(first_local, ((0, 0), (0, width - heads * HD)))
    q, k, v, squares = project(
        heads, normed_all, w_cols, first_local, cosine, sine_table, limits
    )
    attended_wide, q = attend(heads, q, k, v, begins, block)
    attended = attended_wide[:, : heads * HD]
    middle_stream = residual_input + lax.psum_scatter(
        jnp.dot(attended, w_out, preferred_element_type=f32).astype(bf16),
        "tensor",
        scatter_dimension=0,
        tiled=True,
    ).astype(f32)
    second_unit_rows, second_inverse_rms = rms_normalize(middle_stream)
    second_normed_rows = (second_unit_rows * feedforward_norm_gain).astype(bf16)
    gate_full, up_full, down_full = (w_gate, w_up, w_down)
    ffn_input = lax.all_gather(second_normed_rows, "tensor", axis=0, tiled=True)
    gate_act = jnp.dot(ffn_input, gate_full, preferred_element_type=f32)
    up_act = jnp.dot(ffn_input, up_full, preferred_element_type=f32)
    sigmoid_gate = jax.nn.sigmoid(gate_act)
    hidden = (gate_act * sigmoid_gate * up_act).astype(bf16)
    ffn_out = lax.psum_scatter(
        jnp.dot(hidden, down_full, preferred_element_type=f32).astype(bf16),
        "tensor",
        scatter_dimension=0,
        tiled=True,
    ).astype(f32)
    out = (middle_stream + ffn_out).astype(bf16)
    out_rows = lax.all_gather(out_grad, "tensor", axis=0, tiled=True)
    down_grad = jnp.einsum("tf,td->fd", hidden, out_rows, preferred_element_type=f32)
    d_hidden = jnp.einsum("td,fd->tf", out_rows, down_full, preferred_element_type=f32)
    d_up = (d_hidden * gate_act * sigmoid_gate).astype(bf16)
    d_gate = (d_hidden * up_act * sigmoid_gate * (1.0 + gate_act * (1.0 - sigmoid_gate))).astype(
        bf16
    )
    gate_grad = jnp.einsum("td,tf->df", ffn_input, d_gate, preferred_element_type=f32)
    up_grad = jnp.einsum("td,tf->df", ffn_input, d_up, preferred_element_type=f32)
    second_normed_cotangent = lax.psum_scatter(
        (
            jnp.einsum("tf,df->td", d_gate, gate_full, preferred_element_type=f32)
            + jnp.einsum("tf,df->td", d_up, up_full, preferred_element_type=f32)
        ).astype(bf16),
        "tensor",
        scatter_dimension=0,
        tiled=True,
    ).astype(f32)
    middle_norm_cotangent, feedforward_gain_share = rms_normalize_backward(
        second_unit_rows, second_inverse_rms, feedforward_norm_gain, second_normed_cotangent
    )
    d_middle = out_grad.astype(f32) + middle_norm_cotangent
    d_branch = lax.all_gather(d_middle.astype(bf16), "tensor", axis=0, tiled=True)
    out_weight_grad = jnp.einsum("te,td->ed", attended, d_branch, preferred_element_type=f32)
    d_attended = jnp.einsum("td,ed->te", d_branch, w_out, preferred_element_type=f32).astype(bf16)
    if width > heads * HD:
        d_attended = jnp.pad(d_attended, ((0, 0), (0, width - heads * HD)))
    d_qkv = attend_back(
        heads, q, k, v, d_attended, attended_wide, cosine, sine_table, begins, block
    )
    d_half = d_qkv[:, 4 * LANES : 4 * LANES + heads * HD]
    qkv_grad = jnp.einsum("tc,te->ce", normed_all, d_qkv, preferred_element_type=f32).astype(bf16)
    qkv_grad = jnp.einsum("ce,fe->cf", qkv_grad, select, preferred_element_type=f32)
    first_normed_cotangent = lax.psum_scatter(
        jnp.einsum("te,ce->tc", d_qkv, w_cols, preferred_element_type=f32).astype(bf16),
        "tensor",
        scatter_dimension=0,
        tiled=True,
    ).astype(f32)
    first_grad = lax.all_to_all(
        d_half, "tensor", split_axis=0, concat_axis=1, tiled=True
    ).astype(f32)
    input_norm_cotangent, attention_gain_share = rms_normalize_backward(
        first_unit_rows, first_inverse_rms, attention_norm_gain, first_normed_cotangent
    )
    tokens_grad = d_middle + input_norm_cotangent
    scatter = lambda g, dim: lax.psum_scatter(
        g.astype(bf16), "dp", scatter_dimension=dim, tiled=True
    ).astype(f32)
    reduced = (
        scatter(qkv_grad, 0),
        scatter(out_weight_grad, 1),
        scatter(gate_grad, 0),
        scatter(up_grad, 0),
        scatter(down_grad, 1),
    )
    attn_gain_grad, ffn_gain_grad, mixed_total, first_total = lax.psum(
        (attention_gain_share, feedforward_gain_share, jnp.sum(squares[0]), jnp.sum(squares[1])),
        ("dp", "tensor"),
    )
    entry_count = first_values.size * lax.axis_size("dp") * lax.axis_size("tensor")
    return (
        out,
        tokens_grad,
        first_grad,
        attn_gain_grad,
        reduced[0],
        reduced[1],
        ffn_gain_grad,
        reduced[2],
        reduced[3],
        reduced[4],
        jnp.sqrt(first_total / entry_count),
        jnp.sqrt(mixed_total / entry_count),
    )


def solution(mesh):
    token_spec = P(("dp", "tensor"), None)
    return jax.shard_map(
        shards,
        mesh=mesh,
        in_specs=(
            token_spec,
            token_spec,
            P("dp", None),
            P(),
            P(None, "tensor"),
            P("tensor", None),
            P(),
            P(None, "tensor"),
            P(None, "tensor"),
            P("tensor", None),
            token_spec,
        ),
        out_specs=(
            token_spec,
            token_spec,
            token_spec,
            P(),
            P("dp", "tensor"),
            P("tensor", "dp"),
            P(),
            P("dp", "tensor"),
            P("dp", "tensor"),
            P("tensor", "dp"),
            P(),
            P(),
        ),
        check_vma=False,
    )
```

```python
import functools
import math

import jax
import jax.numpy as jnp
import numpy as np
from jax import lax
from jax.experimental import pallas as pl
from jax.experimental.pallas import tpu as pltpu
from jax.sharding import PartitionSpec as P

HD = 64
HALF = HD // 2
LANES = 128
GROUP = LANES // HALF
EPS = 1e-06
NEG = -1e30
VMEM = 60 << 20
f32 = jnp.float32
bf16 = jnp.bfloat16


def rope_tables(length):
    inverse = jnp.exp(-math.log(10000.0) * jnp.arange(HALF, dtype=f32) / HALF)
    angles = jnp.arange(length, dtype=f32)[:, None] * inverse[None, :]
    tile = lambda t: jnp.concatenate([t] * GROUP, axis=1)
    return tile(jnp.cos(angles)), tile(jnp.sin(angles))


def column_order(heads):
    value_width = max(LANES, heads * HD)
    order = np.full((4 * LANES + value_width,), -1, np.int32)
    for h in range(heads):
        for part in range(2):
            for half in range(2):
                at = (2 * part + half) * LANES + h * HALF
                src = h * 3 * HD + part * HD + half * HALF
                order[at : at + HALF] = np.arange(src, src + HALF)
        order[4 * LANES + h * HD : 4 * LANES + (h + 1) * HD] = np.arange(
            h * 3 * HD + 2 * HD, (h + 1) * 3 * HD
        )
    return order


def column_selector(heads):
    order = jnp.asarray(column_order(heads))
    rows = jnp.arange(3 * heads * HD, dtype=jnp.int32)
    return (rows[:, None] == order[None, :]).astype(bf16)


def dot_nt(a, b):
    return lax.dot_general(a, b, (((1,), (1,)), ((), ())), preferred_element_type=f32)


def dot_tn(a, b):
    return lax.dot_general(a, b, (((0,), (0,)), ((), ())), preferred_element_type=f32)


def dot_nn(a, b):
    return jnp.dot(a, b, preferred_element_type=f32)


def project_kernel(heads, n, rows, placed, info_ref, *refs):
    count = len(placed)
    pieces, values = refs[:count], refs[count : count + n]
    w_ref, cos_ref, sin_ref, lim_ref = refs[count + n : count + n + 4]
    q_ref, k_ref, v_ref, sq_ref, x_ref, fv_ref, sem = refs[count + n + 4 :]
    at = pl.program_id(0)
    block = q_ref.shape[0]

    @pl.when(at == 0)
    def _():
        sq_ref[...] = jnp.zeros_like(sq_ref)
        copies = []
        for i, (ref, (j, first)) in enumerate(zip(pieces, placed)):
            size = ref.shape[0]
            place = pl.multiple_of((info_ref[0] ^ j) * rows + first, size)
            copies.append(pltpu.make_async_copy(ref, x_ref.at[pl.ds(place, size)], sem.at[i]))
        for j, ref in enumerate(values):
            place = pl.multiple_of((info_ref[0] ^ j) * rows, rows)
            copies.append(
                pltpu.make_async_copy(ref, fv_ref.at[pl.ds(place, rows)], sem.at[count + j])
            )
        for copy in copies:
            copy.start()
        for copy in copies:
            copy.wait()

    here = pl.ds(pl.multiple_of(at * block, block), block)
    acc = dot_nn(x_ref[here, :], w_ref[...])
    c, s = cos_ref[...], sin_ref[...]
    lane = lax.broadcasted_iota(jnp.int32, (block, LANES), 1)
    place = at * block + lax.broadcasted_iota(jnp.int32, (block, LANES), 0)
    inside = (place >= lim_ref[0:1, :]) & (place < lim_ref[1:2, :])
    doc_lane = (lane >= HD) & (lane < HD + 8)
    q_extra = jnp.where(doc_lane & jnp.logical_not(inside), NEG, 0.0)
    k_extra = jnp.where(inside, 1.0, jnp.where((lane >= HD + 8) & (lane < HD + 11), 1.0, 0.0))
    for ref, base, extra, scale in ((q_ref, 0, q_extra, HD**-0.5), (k_ref, 2, k_extra, 1.0)):
        u1 = acc[:, base * LANES : (base + 1) * LANES]
        u2 = acc[:, (base + 1) * LANES : (base + 2) * LANES]
        r1 = (u1 * c - u2 * s) * scale
        r2 = (u1 * s + u2 * c) * scale
        for h in range(heads):
            a = r1 if h == 0 else pltpu.roll(r1, LANES - HALF * h, 1)
            b = r2 if h == 1 else pltpu.roll(r2, (LANES + HALF - HALF * h) % LANES, 1)
            both = jnp.where(lane < HALF, a, jnp.where(lane < HD, b, extra))
            ref[:, h * LANES : (h + 1) * LANES] = both.astype(bf16)

    first = fv_ref[here, :].astype(f32)
    mixed = 0.5 * acc[:, 4 * LANES :] + 0.5 * first
    sq_ref[0:1, :] += jnp.sum(mixed * mixed, axis=0, keepdims=True)
    sq_ref[1:2, :] += jnp.sum(first * first, axis=0, keepdims=True)
    for h in range(heads):
        t = (h // 2) * LANES
        own = (lane < HD) if h % 2 == 0 else (lane >= HD)
        v_ref[:, h * LANES : (h + 1) * LANES] = jnp.where(
            own, mixed[:, t : t + LANES], 1.0
        ).astype(bf16)


def project(heads, info, parts, values, w, cos, sin, limits, rows):
    n = len(values)
    length = rows * n
    depth = parts[0][0].shape[1]
    width = values[0].shape[1]
    block = min(length, 512)
    row = lambda i, info: (i, 0)
    whole = lambda i, info: (0, 0)
    ext = heads * LANES
    placed = tuple((j, first) for _, j, first in parts)
    anywhere = pl.BlockSpec(memory_space=pl.ANY)
    return pl.pallas_call(
        functools.partial(project_kernel, heads, n, rows, placed),
        name="project",
        grid_spec=pltpu.PrefetchScalarGridSpec(
            num_scalar_prefetch=1,
            grid=(length // block,),
            in_specs=[anywhere] * (len(parts) + n)
            + [
                pl.BlockSpec(w.shape, whole),
                pl.BlockSpec((block, LANES), row),
                pl.BlockSpec((block, LANES), row),
                pl.BlockSpec((8, LANES), whole),
            ],
            out_specs=[
                pl.BlockSpec((block, ext), row),
                pl.BlockSpec((block, ext), row),
                pl.BlockSpec((block, ext), row),
                pl.BlockSpec((8, width), whole),
                pl.BlockSpec((length, depth), whole),
            ],
            scratch_shapes=[
                pltpu.VMEM((length, width), bf16),
                pltpu.SemaphoreType.DMA((len(parts) + n,)),
            ],
        ),
        out_shape=[
            jax.ShapeDtypeStruct((length, ext), bf16),
            jax.ShapeDtypeStruct((length, ext), bf16),
            jax.ShapeDtypeStruct((length, ext), bf16),
            jax.ShapeDtypeStruct((8, width), f32),
            jax.ShapeDtypeStruct((length, depth), bf16),
        ],
        compiler_params=pltpu.CompilerParams(vmem_limit_bytes=VMEM),
        cost_estimate=pl.CostEstimate(
            flops=2 * length * depth * w.shape[1],
            bytes_accessed=2 * (2 * length * depth + w.size + length * width + 3 * length * ext),
            transcendentals=0,
        ),
    )(info, *[p for p, _, _ in parts], *values, w, cos, sin, limits)


def pieces(x):
    hi = x.astype(bf16).astype(f32)
    mid = (x - hi).astype(bf16).astype(f32)
    return hi, mid, x - hi - mid


def attend_kernel(
    heads, block, offset, steps, info_ref, begin_ref, q_ref, k_ref, v_ref, o_ref, qo_ref, m_ref,
    acc_ref,
):
    at = (info_ref[0] ^ offset) * steps + pl.program_id(0)
    lane = lax.broadcasted_iota(jnp.int32, (block, LANES), 1)
    r = lax.broadcasted_iota(jnp.int32, (block, block), 0)
    c = lax.broadcasted_iota(jnp.int32, (block, block), 1)
    causal = c <= r
    here = pl.ds(pl.multiple_of(at * block, block), block)
    col = [slice(h * LANES, (h + 1) * LANES) for h in range(heads)]
    for h in range(heads):
        s = dot_nt(q_ref[:, col[h]], k_ref[here, col[h]])
        s = jnp.where(causal, s, NEG)
        m = jnp.max(s, axis=1, keepdims=True)
        p = jnp.exp(s - m).astype(bf16)
        m_ref[:, col[h]] = jnp.broadcast_to(m, (block, LANES))
        acc_ref[:, col[h]] = dot_nn(p, v_ref[here, col[h]])

    def step(kb, carry):
        there = pl.ds(pl.multiple_of(kb * block, block), block)
        for h in range(heads):
            s = dot_nt(q_ref[:, col[h]], k_ref[there, col[h]])
            old = m_ref[:, col[h]]
            new = jnp.maximum(old, jnp.max(s, axis=1, keepdims=True))
            p = jnp.exp(s - jnp.concatenate([new] * (block // LANES), axis=1)).astype(bf16)
            m_ref[:, col[h]] = new
            acc_ref[:, col[h]] = acc_ref[:, col[h]] * jnp.exp(old - new) + dot_nn(
                p, v_ref[there, col[h]]
            )
        return carry

    lax.fori_loop(begin_ref[at], at, step, 0)
    low = lane < HD
    for t in range((heads + 1) // 2):
        a = acc_ref[:, col[2 * t]]
        b = acc_ref[:, col[2 * t + 1]] if 2 * t + 1 < heads else a
        total = pltpu.roll(jnp.where(low, b, a), HD, 1)
        result = jnp.where(low, a, b) / total
        if 2 * t + 1 >= heads:
            result = jnp.where(low, result, 0.0)
        o_ref[:, t * LANES : (t + 1) * LANES] = result.astype(bf16)
    for h in range(heads):
        a = acc_ref[:, col[h]]
        total = a if h % 2 == 0 else pltpu.roll(a, HD, 1)
        hi, mid, lo = pieces(-(m_ref[:, col[h]] + jnp.log(jnp.where(low, 1.0, total))))
        extra = jnp.where(
            lane == HD + 8, hi, jnp.where(lane == HD + 9, mid, jnp.where(lane == HD + 10, lo, 0.0))
        )
        fill = (lane >= HD + 8) & (lane < HD + 11)
        qo_ref[:, col[h]] = jnp.where(fill, extra, q_ref[:, col[h]].astype(f32)).astype(bf16)


def attend(heads, info, offset, q, k, v, begins, block, rows):
    length = q.shape[0]
    ext = heads * LANES
    width = max(LANES, heads * HD)
    steps = rows // block
    row = lambda i, info, b: (i, 0)
    whole = lambda i, info, b: (0, 0)
    return pl.pallas_call(
        functools.partial(attend_kernel, heads, block, offset, steps),
        name="attend",
        grid_spec=pltpu.PrefetchScalarGridSpec(
            num_scalar_prefetch=2,
            grid=(steps,),
            in_specs=[
                pl.BlockSpec((block, ext), lambda i, info, b: ((info[0] ^ offset) * steps + i, 0)),
                pl.BlockSpec((length, ext), whole),
                pl.BlockSpec((length, ext), whole),
            ],
            out_specs=[pl.BlockSpec((block, width), row), pl.BlockSpec((block, ext), row)],
            scratch_shapes=[pltpu.VMEM((block, ext), f32), pltpu.VMEM((block, ext), f32)],
        ),
        out_shape=[
            jax.ShapeDtypeStruct((rows, width), bf16),
            jax.ShapeDtypeStruct((rows, ext), bf16),
        ],
        compiler_params=pltpu.CompilerParams(vmem_limit_bytes=VMEM),
        cost_estimate=pl.CostEstimate(
            flops=2 * heads * rows * length * LANES,
            bytes_accessed=4 * length * ext,
            transcendentals=heads * rows * length // 2,
        ),
    )(info, begins, q, k, v)


def attend_back_kernel(heads, block, n, info_ref, begin_ref, *refs):
    q_parts, do_parts, o_parts = refs[:n], refs[n : 2 * n], refs[2 * n : 3 * n]
    k_ref, v_ref, cos_ref, sin_ref, g_ref = refs[3 * n : 3 * n + 5]
    sends = refs[3 * n + 5 : 4 * n + 5]
    q_all, do_all, o_all, dk_ref, dv_ref, dq_ref, de_ref, sem = refs[4 * n + 5 :]
    at = pl.program_id(0)
    rows = q_parts[0].shape[0]

    def moves(pairs):
        copies = []
        for i, (make, j) in enumerate(pairs):
            place = pl.ds(pl.multiple_of((info_ref[0] ^ j) * rows, rows), rows)
            copies.append(make(place, sem.at[i]))
        for copy in copies:
            copy.start()
        for copy in copies:
            copy.wait()

    @pl.when(at == 0)
    def _():
        moves(
            [
                (functools.partial(lambda src, dst, p, s: pltpu.make_async_copy(src, dst.at[p], s), part, whole), j)
                for parts, whole in ((q_parts, q_all), (do_parts, do_all), (o_parts, o_all))
                for j, part in enumerate(parts)
            ]
        )

    lane = lax.broadcasted_iota(jnp.int32, (block, LANES), 1)
    r = lax.broadcasted_iota(jnp.int32, (block, block), 0)
    c = lax.broadcasted_iota(jnp.int32, (block, block), 1)
    causal = r <= c
    low = lane < HD
    here = pl.ds(pl.multiple_of(at * block, block), block)
    col = [slice(h * LANES, (h + 1) * LANES) for h in range(heads)]

    for h in range(heads):
        t = slice((h // 2) * LANES, (h // 2 + 1) * LANES)
        own = low if h % 2 == 0 else jnp.logical_not(low)
        grad = do_all[here, t].astype(f32)
        product = grad * o_all[here, t].astype(f32)
        centre = jnp.sum(jnp.where(own, product, 0.0), axis=1, keepdims=True)
        hi, mid, lo = pieces(-jnp.broadcast_to(centre, (block, LANES)))
        spot = lane - (HD if h % 2 == 0 else 0)
        extra = jnp.where(spot == 0, hi, jnp.where(spot == 1, mid, jnp.where(spot == 2, lo, 0.0)))
        de_ref[:, col[h]] = jnp.where(own, grad, extra).astype(bf16)

    def pair(there, h, mask, first):
        st = dot_nt(k_ref[there, col[h]], q_all[here, col[h]])
        p = jnp.exp(st)
        if mask is not None:
            p = jnp.where(mask, p, 0.0)
        dpt = dot_nt(v_ref[there, col[h]], de_ref[:, col[h]])
        ds = (p * dpt).astype(bf16)
        dv = dot_nn(p.astype(bf16), de_ref[:, col[h]])
        dk = dot_nn(ds, q_all[here, col[h]])
        dq = dot_tn(ds, k_ref[there, col[h]])
        if first:
            dv_ref[there, col[h]] = dv
            dk_ref[there, col[h]] = dk
            dq_ref[:, col[h]] = dq
        else:
            dv_ref[there, col[h]] += dv
            dk_ref[there, col[h]] += dk
            dq_ref[:, col[h]] += dq

    for h in range(heads):
        pair(here, h, causal, True)

    def step(kb, carry):
        there = pl.ds(pl.multiple_of(kb * block, block), block)
        for h in range(heads):
            pair(there, h, None, False)
        return carry

    lax.fori_loop(begin_ref[at], at, step, 0)

    def turn_back(ref, rows, scale):
        u1 = u2 = None
        quarter = lane // HALF
        for h in range(heads):
            u = ref[rows, col[h]]
            a = u if h == 0 else pltpu.roll(u, HALF * h, 1)
            b = u if h == 1 else pltpu.roll(u, (LANES + HALF * h - HALF) % LANES, 1)
            u1 = a if h == 0 else jnp.where(quarter == h, a, u1)
            u2 = b if h == 0 else jnp.where(quarter == h, b, u2)
        if heads < GROUP:
            u1 = jnp.where(quarter < heads, u1, 0.0)
            u2 = jnp.where(quarter < heads, u2, 0.0)
        u1, u2 = u1 * scale, u2 * scale
        cs, sn = cos_ref[rows, :], sin_ref[rows, :]
        return (u1 * cs + u2 * sn).astype(bf16), (u2 * cs - u1 * sn).astype(bf16)

    def finish_block(i, carry):
        rows = pl.ds(pl.multiple_of(i * block, block), block)
        d1, d2 = turn_back(dk_ref, rows, 1.0)
        g_ref[rows, 2 * LANES : 3 * LANES] = d1
        g_ref[rows, 3 * LANES : 4 * LANES] = d2
        for t in range((heads + 1) // 2):
            a = dv_ref[rows, col[2 * t]]
            b = dv_ref[rows, col[2 * t + 1]] if 2 * t + 1 < heads else jnp.zeros_like(a)
            d_mix = jnp.where(low, a, b).astype(bf16)
            g_ref[rows, (4 + t) * LANES : (5 + t) * LANES] = (d_mix.astype(f32) * 0.5).astype(bf16)
        return carry

    u1 = u2 = None
    quarter = lane // HALF
    for h in range(heads):
        u = dq_ref[:, col[h]]
        a = u if h == 0 else pltpu.roll(u, HALF * h, 1)
        b = u if h == 1 else pltpu.roll(u, (LANES + HALF * h - HALF) % LANES, 1)
        u1 = a if h == 0 else jnp.where(quarter == h, a, u1)
        u2 = b if h == 0 else jnp.where(quarter == h, b, u2)
    if heads < GROUP:
        u1 = jnp.where(quarter < heads, u1, 0.0)
        u2 = jnp.where(quarter < heads, u2, 0.0)
    u1, u2 = u1 * HD**-0.5, u2 * HD**-0.5
    cs, sn = cos_ref[here, :], sin_ref[here, :]
    g_ref[here, 0:LANES] = (u1 * cs + u2 * sn).astype(bf16)
    g_ref[here, LANES : 2 * LANES] = (u2 * cs - u1 * sn).astype(bf16)

    @pl.when(at == pl.num_programs(0) - 1)
    def _():
        lax.fori_loop(0, pl.num_programs(0), finish_block, 0)
        moves(
            [
                (functools.partial(lambda dst, p, s: pltpu.make_async_copy(g_ref.at[p], dst, s), dst), j)
                for j, dst in enumerate(sends)
            ]
        )


def attend_back(heads, info, q_parts, k, v, do_parts, o_parts, cos, sin, begins, block):
    n = len(q_parts)
    rows = q_parts[0].shape[0]
    length = n * rows
    ext = heads * LANES
    width = o_parts[0].shape[1]
    whole = lambda i, info, b: (0, 0)
    anywhere = pl.BlockSpec(memory_space=pl.ANY)
    columns = 4 * LANES + width
    return pl.pallas_call(
        functools.partial(attend_back_kernel, heads, block, n),
        name="attend_back",
        grid_spec=pltpu.PrefetchScalarGridSpec(
            num_scalar_prefetch=2,
            grid=(length // block,),
            in_specs=[anywhere] * (3 * n)
            + [
                pl.BlockSpec((length, ext), whole),
                pl.BlockSpec((length, ext), whole),
                pl.BlockSpec((length, LANES), whole),
                pl.BlockSpec((length, LANES), whole),
            ],
            out_specs=[pl.BlockSpec((length, columns), whole)] + [anywhere] * n,
            scratch_shapes=[
                pltpu.VMEM((length, ext), bf16),
                pltpu.VMEM((length, width), bf16),
                pltpu.VMEM((length, width), bf16),
                pltpu.VMEM((length, ext), f32),
                pltpu.VMEM((length, ext), f32),
                pltpu.VMEM((block, ext), f32),
                pltpu.VMEM((block, ext), bf16),
                pltpu.SemaphoreType.DMA((3 * n,)),
            ],
        ),
        out_shape=[jax.ShapeDtypeStruct((length, columns), bf16)]
        + [jax.ShapeDtypeStruct((rows, columns), bf16)] * n,
        compiler_params=pltpu.CompilerParams(vmem_limit_bytes=VMEM),
        cost_estimate=pl.CostEstimate(
            flops=5 * heads * length * length * LANES,
            bytes_accessed=2 * 8 * length * ext,
            transcendentals=heads * length * length // 2,
        ),
    )(info, begins, *q_parts, *do_parts, *o_parts, k, v, cos, sin)


def split_axis(n):
    low = 1 << ((n.bit_length() - 1) // 2)
    return n // low, low


def swap(axis, value, offset):
    n = lax.axis_size(axis)
    return lax.ppermute(value, axis, [(i, i ^ offset) for i in range(n)])


def gather_rows(value, n):
    high, low = split_axis(n)
    rows = value.shape[0]
    half = rows // 2
    parts = {0: value}
    for b in range(1, low):
        parts[b] = swap("tensor", value, b)
    for a in range(1, high):
        parts[a * low] = swap("tensor", value, a * low)
    listed = [(parts[j], j, 0) for j in sorted(parts)]
    for a in range(1, high):
        for b in range(1, low):
            j = a * low + b
            listed.append((swap("tensor", parts[b][:half], a * low), j, 0))
            listed.append((swap("tensor", parts[a * low][half:], b), j, half))
    return listed


def after(value, *others):
    return lax.optimization_barrier((value,) + others)[0]


def add_up(first, *others):
    total = first.astype(f32)
    for other in others:
        total = total + other.astype(f32)
    return total


def halve_over_z(parts, z, count):
    step = 1
    while step < count:
        pairs = parts.reshape((-1, 2) + parts.shape[1:])
        side = (z // step) % 2
        pick = lambda which: lax.dynamic_index_in_dim(pairs, which, 1, keepdims=False)
        parts = add_up(pick(side), swap("dp", pick(1 - side), 2 * step))
        parts = parts.astype(bf16) if 2 * step < count else parts
        given = yield parts
        parts = parts if given is None else given
        step *= 2


def all_sum(value, axis):
    n = lax.axis_size(axis)
    step = 1
    while step < n:
        value = value + swap(axis, value, step)
        step *= 2
    return value


def anywhere():
    return pl.BlockSpec(memory_space=pl.ANY)


def norm_kernel(x_ref, gain_ref, o_ref):
    x = x_ref[...].astype(f32)
    inverse = lax.rsqrt(jnp.mean(x * x, axis=-1, keepdims=True) + EPS)
    o_ref[...] = (x * inverse * gain_ref[...]).astype(bf16)


def norm_rows(x, gain):
    rows, depth = x.shape
    block = min(rows, 128)
    return pl.pallas_call(
        norm_kernel,
        name="norm_rows",
        grid=(rows // block,),
        in_specs=[
            pl.BlockSpec((block, depth), lambda i: (i, 0)),
            pl.BlockSpec((1, depth), lambda i: (0, 0)),
        ],
        out_specs=pl.BlockSpec((block, depth), lambda i: (i, 0)),
        out_shape=jax.ShapeDtypeStruct((rows, depth), bf16),
        compiler_params=pltpu.CompilerParams(vmem_limit_bytes=VMEM),
        cost_estimate=pl.CostEstimate(
            flops=5 * x.size, bytes_accessed=4 * x.size, transcendentals=rows
        ),
    )(x, gain)


def branch_kernel(n, first, info_ref, *refs):
    att = refs[:n]
    w_ref, tok_ref, gain_ref, mid_ref, h_ref, all_ref, sem = refs[n:]
    size = tok_ref.shape[0]
    width = att[0].shape[1]
    copies = []
    for j in range(n):
        lanes = pl.ds(pl.multiple_of((info_ref[0] ^ j) * width, width), width)
        copies.append(
            pltpu.make_async_copy(att[j].at[first : first + size, :], all_ref.at[:, lanes], sem.at[j])
        )
    for copy in copies:
        copy.start()
    for copy in copies:
        copy.wait()
    x = tok_ref[...].astype(f32) + dot_nn(all_ref[...], w_ref[...])
    mid_ref[...] = x
    inverse = lax.rsqrt(jnp.mean(x * x, axis=-1, keepdims=True) + EPS)
    h_ref[...] = (x * inverse * gain_ref[...]).astype(bf16)


def branch(info, att, w_all, tokens, gain, first, size):
    n = len(att)
    width = att[0].shape[1]
    depth = tokens.shape[1]
    at = first // size
    whole = lambda i, info: (0, 0)
    return pl.pallas_call(
        functools.partial(branch_kernel, n, first),
        name="branch",
        grid_spec=pltpu.PrefetchScalarGridSpec(
            num_scalar_prefetch=1,
            grid=(1,),
            in_specs=[anywhere()] * n
            + [
                pl.BlockSpec(w_all.shape, whole),
                pl.BlockSpec((size, depth), lambda i, info: (at, 0)),
                pl.BlockSpec((1, depth), whole),
            ],
            out_specs=[pl.BlockSpec((size, depth), whole)] * 2,
            scratch_shapes=[pltpu.VMEM((size, n * width), bf16), pltpu.SemaphoreType.DMA((n,))],
        ),
        out_shape=[
            jax.ShapeDtypeStruct((size, depth), f32),
            jax.ShapeDtypeStruct((size, depth), bf16),
        ],
        compiler_params=pltpu.CompilerParams(vmem_limit_bytes=VMEM),
        cost_estimate=pl.CostEstimate(
            flops=2 * size * depth * n * width,
            bytes_accessed=2 * n * width * depth + 8 * size * depth,
            transcendentals=size,
        ),
    )(info, *att, w_all, tokens, gain)


def feed_kernel(shards_in, joined, send, info_ref, h_ref, g_ref, *refs):
    flat = [ref for shard in shards_in for ref in range(shard)]
    weights, refs = refs[: len(flat)], refs[len(flat) :]
    if joined:
        (out_in, dh_in), refs = refs[:2], refs[2:]
    out_ref, dh_ref, act_ref, w_ref, sem = refs[:5]
    out_acc, dh_acc = refs[5:] if send else (out_ref, dh_ref)
    high, rows_w, depth = w_ref.shape
    units = rows_w // 3
    copies, at = [], 0
    for a, count in enumerate(shards_in):
        group = []
        for i in range(count):
            ref = weights[at]
            if count == 3:
                group.append(
                    pltpu.make_async_copy(ref, w_ref.at[a, pl.ds(i * units, units)], sem.at[at])
                )
            elif len(ref.shape) == 3:
                size = ref.shape[2]
                for d in range(ref.shape[0]):
                    group.append(
                        pltpu.make_async_copy(
                            ref.at[d],
                            w_ref.at[a, :, d * size : (d + 1) * size],
                            sem.at[len(flat) + a * ref.shape[0] + d],
                        )
                    )
            else:
                group.append(pltpu.make_async_copy(ref, w_ref.at[a], sem.at[at]))
            at += 1
        copies.append(group)
    first = pl.program_id(0) == 0

    @pl.when(first)
    def _():
        for group in copies:
            for copy in group:
                copy.start()

    for a in range(high):

        @pl.when(first)
        def _():
            for copy in copies[a]:
                copy.wait()

        gate_w, up_w, down_w = (w_ref.at[a, pl.ds(m * units, units)] for m in range(3))
        gate = dot_nt(h_ref[...], gate_w[...])
        up = dot_nt(h_ref[...], up_w[...])
        back = dot_nt(g_ref[...], down_w[...])
        s = 1.0 / (1.0 + jnp.exp(-gate))
        gs = gate * s
        hidden = (gs * up).astype(bf16)
        d_up = (back * gs).astype(bf16)
        d_gate = (back * up * (s + gs * (1.0 - s))).astype(bf16)
        act_ref[a, 0] = d_gate
        act_ref[a, 1] = d_up
        act_ref[a, 2] = hidden
        part = dot_nn(hidden, down_w[...])
        d_part = dot_nn(d_gate, gate_w[...]) + dot_nn(d_up, up_w[...])
        if a == 0 and joined:
            out_acc[...] = out_in[...] + part
            dh_acc[...] = dh_in[...] + d_part
        elif a == 0:
            out_acc[...] = part
            dh_acc[...] = d_part
        else:
            out_acc[...] += part
            dh_acc[...] += d_part
    if send:
        out_ref[...] = out_acc[...].astype(bf16)
        dh_ref[...] = dh_acc[...].astype(bf16)


def feed(info, h, g, g_first, weights, sums, send):
    rows, depth = h.shape
    high = len(weights)
    flat = [w for shard in weights for w in shard]
    units = weights[0][0].shape[0] if len(weights[0]) == 3 else weights[0][0].shape[-2] // 3
    block = min(rows, 256)
    at = g_first // block
    row = lambda i, info: (i, 0)
    kind = bf16 if send else f32
    slices = max(w.shape[0] if w.ndim == 3 else 0 for w in flat)
    return pl.pallas_call(
        functools.partial(feed_kernel, tuple(len(shard) for shard in weights), bool(sums), send),
        name="feed",
        grid_spec=pltpu.PrefetchScalarGridSpec(
            num_scalar_prefetch=1,
            grid=(rows // block,),
            in_specs=[
                pl.BlockSpec((block, depth), row),
                pl.BlockSpec((block, depth), lambda i, info: (at + i, 0)),
            ]
            + [anywhere()] * len(flat)
            + [pl.BlockSpec((block, depth), row)] * len(sums),
            out_specs=[pl.BlockSpec((block, depth), row)] * 2
            + [pl.BlockSpec((high, 3, block, units), lambda i, info: (0, 0, i, 0))],
            scratch_shapes=[
                pltpu.VMEM((high, 3 * units, depth), bf16),
                pltpu.SemaphoreType.DMA((len(flat) + high * slices,)),
            ]
            + ([pltpu.VMEM((block, depth), f32)] * 2 if send else []),
        ),
        out_shape=[
            jax.ShapeDtypeStruct((rows, depth), kind),
            jax.ShapeDtypeStruct((rows, depth), kind),
            jax.ShapeDtypeStruct((high, 3, rows, units), bf16),
        ],
        compiler_params=pltpu.CompilerParams(vmem_limit_bytes=VMEM),
        cost_estimate=pl.CostEstimate(
            flops=12 * rows * depth * high * units,
            bytes_accessed=6 * depth * high * units + 12 * rows * depth,
            transcendentals=2 * rows * high * units,
        ),
    )(info, h, g, *flat, *sums)


def feed_grad_kernel(parts, members, info_ref, *refs):
    h, g, acts = refs[:parts], refs[parts : 2 * parts], refs[2 * parts : 3 * parts]
    keep_ref, send_ref, acc_ref = refs[3 * parts :]
    core = info_ref[1]

    def product(sources):
        return sum(dot_tn(acts[p][0, 0], sources[p][...]) for p in range(parts))

    @pl.when(pl.program_id(1) < 2)
    def _():
        acc_ref[...] = product(h)

    @pl.when(pl.program_id(1) == 2)
    def _():
        acc_ref[...] = product(g)

    size = acc_ref.shape[1] // (2 * members)
    for z in range(members):
        for ref, side in ((keep_ref, core), (send_ref, 1 - core)):
            pair = acc_ref[:, 2 * z * size : 2 * (z + 1) * size]
            ref[0, z, 0] = jnp.where(side == 0, pair[:, :size], pair[:, size:]).astype(bf16)


def feed_grads(info, h, g, g_at, acts, firsts, high, members):
    parts = len(h)
    depth = h[0].shape[1]
    units = acts[0].shape[3]
    size = depth // (2 * members)
    whole = lambda a, m, info: (0, 0)
    out = jax.ShapeDtypeStruct((high, members, 3, units, size), bf16)
    return pl.pallas_call(
        functools.partial(feed_grad_kernel, parts, members),
        name="feed_grads",
        grid_spec=pltpu.PrefetchScalarGridSpec(
            num_scalar_prefetch=1,
            grid=(high, 3),
            in_specs=[pl.BlockSpec(v.shape, whole) for v in h]
            + [
                pl.BlockSpec(v.shape, lambda a, m, info, at=at: (at, 0)) for v, at in zip(h, g_at)
            ]
            + [
                pl.BlockSpec((1, 1, v.shape[2], units), lambda a, m, info, f=f: (a + f, m, 0, 0))
                for v, f in zip(acts, firsts)
            ],
            out_specs=[
                pl.BlockSpec((1, members, 1, units, size), lambda a, m, info: (a, 0, m, 0, 0))
            ]
            * 2,
            scratch_shapes=[pltpu.VMEM((units, depth), f32)],
        ),
        out_shape=[out, out],
        compiler_params=pltpu.CompilerParams(vmem_limit_bytes=VMEM),
        cost_estimate=pl.CostEstimate(
            flops=6 * high * sum(v.shape[0] for v in h) * depth * units,
            bytes_accessed=12 * high * depth * units,
            transcendentals=0,
        ),
    )(info, *h, *g, *acts)


def branch_back_kernel(n, parts, info_ref, *refs):
    dh, far = refs[:parts], refs[parts : 2 * parts]
    mid = refs[2 * parts : 3 * parts]
    first_ref, g_ref, gain_ref, w_ref = refs[3 * parts : 3 * parts + 4]
    dm_ref, db_ref, gg_ref = refs[3 * parts + 4 : 3 * parts + 7]
    da = refs[3 * parts + 7 :]
    rows = mid[0].shape[0]
    width = da[0].shape[1]
    for p in range(parts):
        at = slice(p * rows, (p + 1) * rows)
        x = mid[p][...]
        inverse = lax.rsqrt(jnp.mean(x * x, axis=-1, keepdims=True) + EPS)
        unit = x * inverse
        cotangent = dh[p][...] + far[p][...].astype(f32)
        e = cotangent * gain_ref[...]
        inner = jnp.mean(e * unit, axis=-1, keepdims=True)
        d_mid = g_ref[at, :].astype(f32) + inverse * (e - unit * inner)
        share = jnp.sum(cotangent * unit, axis=0, keepdims=True)
        gg_ref[...] = share if p == 0 else gg_ref[...] + share
        dm_ref[at, :] = d_mid
        db_ref[at, :] = d_mid.astype(bf16)
    for j in range(n):
        place = pl.ds(pl.multiple_of((info_ref[0] ^ j) * width, width), width)
        da[j][...] = dot_nt(db_ref[...], w_ref[place, :]).astype(bf16)


def branch_back(info, d_h, d_far, middle, g, gain, w_all, width):
    n = w_all.shape[0] // width
    parts = len(middle)
    rows, depth = middle[0].shape
    whole = lambda i, info: (0, 0)
    part = lambda p: pl.BlockSpec((rows, depth), lambda i, info, p=p: (p, 0))
    shapes = [((parts * rows, depth), f32), ((parts * rows, depth), bf16), ((1, depth), f32)]
    shapes += [((parts * rows, width), bf16)] * n
    return pl.pallas_call(
        functools.partial(branch_back_kernel, n, parts),
        name="branch_back",
        grid_spec=pltpu.PrefetchScalarGridSpec(
            num_scalar_prefetch=1,
            grid=(1,),
            in_specs=[part(p) for p in range(parts)]
            + [pl.BlockSpec((rows, depth), whole)] * (2 * parts)
            + [
                pl.BlockSpec((1, LANES), whole),
                pl.BlockSpec(g.shape, whole),
                pl.BlockSpec(gain.shape, whole),
                pl.BlockSpec(w_all.shape, whole),
            ],
            out_specs=[pl.BlockSpec(s, whole) for s, _ in shapes],
        ),
        out_shape=[jax.ShapeDtypeStruct(s, d) for s, d in shapes],
        compiler_params=pltpu.CompilerParams(vmem_limit_bytes=VMEM),
        cost_estimate=pl.CostEstimate(
            flops=2 * parts * rows * depth * n * width,
            bytes_accessed=20 * parts * rows * depth + 2 * n * width * depth,
            transcendentals=parts * rows,
        ),
    )(info, *[d_h] * parts, *d_far, *middle, jnp.zeros((1, LANES), f32), g, gain, w_all)


def out_grad_kernel(n, info_ref, *refs):
    db_ref = refs[0]
    att = refs[1 : 1 + n]
    o_ref = refs[1 + n]
    width = att[0].shape[1]
    for j in range(n):
        place = pl.ds(pl.multiple_of((info_ref[0] ^ j) * width, width), width)
        o_ref[place, :] = dot_tn(att[j][...], db_ref[...]).astype(bf16)


def out_grads(info, d_branch, att):
    n = len(att)
    rows, depth = d_branch.shape
    width = att[0].shape[1]
    whole = lambda i, info: (0, 0)
    return pl.pallas_call(
        functools.partial(out_grad_kernel, n),
        name="out_grads",
        grid_spec=pltpu.PrefetchScalarGridSpec(
            num_scalar_prefetch=1,
            grid=(1,),
            in_specs=[pl.BlockSpec(d_branch.shape, whole)]
            + [pl.BlockSpec(a.shape, whole) for a in att],
            out_specs=pl.BlockSpec((n * width, depth), whole),
        ),
        out_shape=jax.ShapeDtypeStruct((n * width, depth), bf16),
        compiler_params=pltpu.CompilerParams(vmem_limit_bytes=VMEM),
        cost_estimate=pl.CostEstimate(
            flops=2 * rows * depth * n * width,
            bytes_accessed=2 * rows * depth + 4 * n * width * depth,
            transcendentals=0,
        ),
    )(info, d_branch, *att)


def qkv_grad_kernel(x_ref, d_ref, w_ref, sel_ref, o_ref, share_ref):
    g = dot_tn(x_ref[...], d_ref[...])
    share_ref[...] = jnp.sum(g * w_ref[...].astype(f32), axis=1, keepdims=True)
    o_ref[...] = dot_nt(g.astype(bf16), sel_ref[...]).astype(bf16)


def qkv_grads(x, d, w, select):
    length, depth = x.shape
    columns = select.shape[0]
    block = 512
    whole = lambda i: (0, 0)
    return pl.pallas_call(
        qkv_grad_kernel,
        name="qkv_grads",
        grid=(depth // block,),
        in_specs=[
            pl.BlockSpec((length, block), lambda i: (0, i)),
            pl.BlockSpec(d.shape, whole),
            pl.BlockSpec((block, w.shape[1]), lambda i: (i, 0)),
            pl.BlockSpec(select.shape, whole),
        ],
        out_specs=[
            pl.BlockSpec((block, columns), lambda i: (i, 0)),
            pl.BlockSpec((block, 1), lambda i: (i, 0)),
        ],
        out_shape=[
            jax.ShapeDtypeStruct((depth, columns), bf16),
            jax.ShapeDtypeStruct((depth, 1), f32),
        ],
        compiler_params=pltpu.CompilerParams(vmem_limit_bytes=VMEM),
        cost_estimate=pl.CostEstimate(
            flops=2 * length * depth * d.shape[1],
            bytes_accessed=2 * (x.size + d.size + 2 * w.size),
            transcendentals=0,
        ),
    )(x, d, w, select)


def finish_kernel(n, wide, info_ref, *refs):
    d = refs[:n]
    cols_ref, tok_ref, gain_ref, dm_ref, o_ref = refs[n : n + 5]
    w_ref, sem = refs[-2:]
    t = info_ref[0]
    members, _, size, columns = cols_ref.shape
    depth = members * size
    first = pl.program_id(0) == 0
    copies = [
        pltpu.make_async_copy(cols_ref.at[:, j], w_ref.at[j], sem.at[j]) for j in range(n)
    ]

    @pl.when(first)
    def _():
        for copy in copies:
            copy.start()

    for j in range(n):

        @pl.when(first)
        def _():
            copies[j].wait()

        part = dot_nt(d[j][...], w_ref[j].reshape(depth, columns))
        o_ref[...] = part if j == 0 else o_ref[...] + part
    x = tok_ref[...].astype(f32)
    inverse = lax.rsqrt(jnp.mean(x * x, axis=-1, keepdims=True) + EPS)
    unit = x * inverse
    e = o_ref[...] * gain_ref[...]
    inner = jnp.mean(e * unit, axis=-1, keepdims=True)
    o_ref[...] = dm_ref[...] + inverse * (e - unit * inner)
    if wide:
        first_ref = refs[n + 5]
        width = depth // n
        for j in range(n):
            at = pl.ds(pl.multiple_of((t ^ j) * width, width), width)
            first_ref[:, at] = d[j][:, 4 * LANES :].astype(f32)


def finish(info, d_parts, cols, tokens, gain, d_middle):
    n = len(d_parts)
    rows, depth = tokens.shape
    block = min(rows, 256)
    wide = (depth // n) % LANES == 0
    row = lambda i, info: (i, 0)
    whole = lambda i, info: (0, 0)
    count = 2 if wide else 1
    members, _, size, columns = cols.shape
    out = pl.pallas_call(
        functools.partial(finish_kernel, n, wide),
        name="finish",
        grid_spec=pltpu.PrefetchScalarGridSpec(
            num_scalar_prefetch=1,
            grid=(rows // block,),
            in_specs=[pl.BlockSpec((block, d.shape[1]), row) for d in d_parts]
            + [
                anywhere(),
                pl.BlockSpec((block, depth), row),
                pl.BlockSpec((1, depth), whole),
                pl.BlockSpec((block, depth), row),
            ],
            out_specs=[pl.BlockSpec((block, depth), row)] * count,
            scratch_shapes=[
                pltpu.VMEM((n, members, size, columns), bf16),
                pltpu.SemaphoreType.DMA((n,)),
            ],
        ),
        out_shape=[jax.ShapeDtypeStruct((rows, depth), f32)] * count,
        compiler_params=pltpu.CompilerParams(vmem_limit_bytes=VMEM),
        cost_estimate=pl.CostEstimate(
            flops=2 * rows * cols.size,
            bytes_accessed=2 * cols.size + 16 * rows * depth,
            transcendentals=rows,
        ),
    )(info, *d_parts, cols, tokens, gain, d_middle)
    if wide:
        return out
    heads_width = depth // n
    pieces_ = jnp.stack([d[:, 4 * LANES : 4 * LANES + heads_width] for d in d_parts])
    ordered = jnp.take(pieces_, info[0] ^ jnp.arange(n), axis=0)
    return out[0], ordered.transpose(1, 0, 2).reshape(rows, depth).astype(f32)


def shards(
    tokens,
    first_values,
    doc_lengths,
    attention_norm_gain,
    w_qkv,
    w_out,
    feedforward_norm_gain,
    w_gate,
    w_up,
    w_down,
    out_grad,
):
    n = lax.axis_size("tensor")
    high, low = split_axis(n)
    members = lax.axis_size("dp") // 2
    t = lax.axis_index("tensor")
    z, core = lax.axis_index("dp") // 2, lax.axis_index("dp") % 2
    info = jnp.stack([t, core]).astype(jnp.int32)
    rows, depth = tokens.shape
    heads = w_out.shape[0] // HD
    own_width = heads * HD
    width = max(LANES, own_width)
    length = rows * n
    block = min(256, rows)
    gain_one = attention_norm_gain[None, :]
    gain_two = feedforward_norm_gain[None, :]
    missing = width - own_width
    widen = lambda v: jnp.pad(v, ((0, 0), (0, missing))) if missing else v
    replicas = 2 * members
    size_d = depth // replicas
    mine = lambda w, axis: lax.dynamic_slice_in_dim(w, lax.axis_index("dp") * size_d, size_d, axis)

    together = lax.optimization_barrier
    cosine, sine_table = rope_tables(length)
    ends = jnp.cumsum(doc_lengths[0])
    starts = ends - doc_lengths[0]
    docs = doc_lengths.shape[1]
    limits = jnp.pad(jnp.stack([starts, ends]), ((0, 6), (HD, LANES - HD - docs)))
    heads_at = jnp.arange(length // block, dtype=jnp.int32) * block
    begins = jnp.max(jnp.where(starts[None, :] <= heads_at[:, None], starts[None, :], 0), axis=1)
    begins = (begins // block).astype(jnp.int32)
    select = column_selector(heads)
    w_cols = jnp.dot(w_qkv, select, preferred_element_type=f32).astype(bf16)

    own_weights = (w_gate.T, w_up.T, w_down)
    weight_slice = jnp.concatenate([mine(w, 1) for w in own_weights])
    normed = norm_rows(tokens, gain_one)
    normed_parts = gather_rows(normed, n)
    value_part = lambda j: widen(
        lax.dynamic_slice_in_dim(first_values, (t ^ j) * own_width, own_width, 1)
    )
    value_parts = [value_part(0)] + [swap("tensor", value_part(j), j) for j in range(1, n)]
    w_out_wide = jnp.pad(w_out, ((0, missing), (0, 0))) if missing else w_out
    placed = [(j, first) for _, j, first in normed_parts]
    pieces_in = [piece for piece, _, _ in normed_parts]
    cols_slice = mine(w_cols, 0)
    (
        pieces_in, value_parts, weight_slice, w_cols, cols_slice, cosine, sine_table, limits,
        w_out_late, grad_late,
    ) = together(
        (
            pieces_in, value_parts, weight_slice, w_cols, cols_slice, cosine, sine_table, limits,
            w_out_wide, out_grad,
        )
    )

    w_out_all = lax.all_gather(w_out_late, "tensor", axis=0, tiled=True)
    far_slices = [swap("tensor", weight_slice, a * low) for a in range(1, high)]
    cols_far = [cols_slice] + [swap("tensor", cols_slice, j) for j in range(1, n)]
    grad_rows = [out_grad] + [swap("tensor", grad_late, b) for b in range(1, low)]
    normed_parts = [(piece, j, first) for piece, (j, first) in zip(pieces_in, placed)]
    q, k, v, squares, normed_all = project(
        heads, info, normed_parts, value_parts, w_cols, cosine, sine_table, limits, rows
    )
    q, far_slices, cols_far = together((q, far_slices, cols_far))
    if size_d % LANES == 0:
        feed_far = [(lax.all_gather(w, "dp", axis=0),) for w in far_slices]
    else:
        feed_far = [(lax.all_gather(w, "dp", axis=1, tiled=True),) for w in far_slices]
    seen = {}
    for j in range(n - 1, -1, -1):
        if j == 0:
            w_out_all, q, *grad_rows = together((w_out_all, q, *grad_rows))
        seen[j] = attend(heads, info, j, q, k, v, begins, block, rows)
    heads_rows = [seen[0][0]] + [swap("tensor", seen[j][0], j) for j in range(1, n)]
    heads_rows, cols = together((heads_rows, jnp.stack(cols_far)))

    cols = lax.all_gather(cols, "dp", axis=0)
    parts = 2 if rows >= 512 else 1
    size = rows // parts
    middle, second = zip(
        *[
            branch(info, heads_rows, w_out_all, tokens, gain_two, p * size, size)
            for p in range(parts)
        ]
    )
    far_keys = [(b, p) for b in range(1, low) for p in range(parts)]
    inputs = {key: swap("tensor", second[key[1]], key[0]) for key in far_keys}
    second_all = jnp.concatenate(second) if parts > 1 else second[0]
    *own_sums, own_acts = feed(info, second_all, out_grad, 0, [own_weights], [], False)
    own_out, own_back, far_acts = feed(info, second_all, out_grad, 0, feed_far, own_sums, False)
    fed = {}
    last = own_out
    for b, p in far_keys:
        arrived, last = together((inputs[b, p], last))
        fed[b, p] = feed(
            info, arrived, grad_rows[b], p * size, [own_weights] + feed_far, [], True
        )
        inputs[b, p] = arrived
    own_out = last
    d_far = [[swap("tensor", fed[b, p][1], b) for b in range(1, low)] for p in range(parts)]
    d_far = [d[0] if low == 2 else add_up(*d) for d in d_far]
    sources = (
        [second_all] + [inputs[key] for key in far_keys],
        [out_grad] + [grad_rows[b] for b, p in far_keys],
        [0] + [p for b, p in far_keys],
    )
    far_parts = [fed[key][2] for key in far_keys]
    count = len(far_keys)
    far_keep, far_send = feed_grads(
        info, *sources, [far_acts] + far_parts, [0] + [1] * count, high - 1, members
    )
    own_keep, own_send = feed_grads(
        info, *sources, [own_acts] + far_parts, [0] * (count + 1), 1, members
    )
    d_far, far_send, own_send, far_keep, own_keep = together(
        (d_far, far_send, own_send, far_keep, own_keep)
    )

    far_got, own_got = swap("dp", far_send, 1), swap("dp", own_send, 1)
    d_middle, d_branch, feed_share, *d_att = branch_back(
        info, own_back, d_far, middle, out_grad, gain_two, w_out_all, width
    )
    d_att = [d_att[0]] + [swap("tensor", d_att[j], j) for j in range(1, n)]
    pair = lambda a, lo, hi: (
        (own_keep[0, :, lo:hi], own_got[0, :, lo:hi])
        if a == 0
        else (far_keep[a - 1, :, lo:hi], far_got[a - 1, :, lo:hi])
    )
    gate_sums = jnp.concatenate(
        [add_up(*pair(a, 0, 1)).astype(bf16) for a in range(high)], axis=1
    )
    rest_sums = [add_up(*pair(a, 1, 3)).astype(bf16) for a in range(high)]
    out_grad_w = out_grads(info, d_branch, heads_rows)
    out_parts = [
        jnp.concatenate([fed[b, p][0] for p in range(parts)]) if parts > 1 else fed[b, 0][0]
        for b in range(1, low)
    ]
    d_att, gate_sums, rest_sums, out_parts, out_grad_w = together(
        (d_att, gate_sums, rest_sums, out_parts, out_grad_w)
    )

    gate_z = [
        swap("dp", lax.dynamic_index_in_dim(gate_sums, z ^ k, 0, keepdims=False), 2 * k)
        for k in range(1, members)
    ]
    rest_got = [swap("tensor", rest_sums[a], a * low) for a in range(1, high)]
    out_got = [swap("tensor", v_, b) for b, v_ in zip(range(1, low), out_parts)]
    out_sum = lax.psum_scatter(out_grad_w, "dp", scatter_dimension=1, tiled=True)
    d_cols = attend_back(
        heads, info, [seen[j][1] for j in range(n)], k, v, d_att, [seen[j][0] for j in range(n)],
        cosine, sine_table, begins, block,
    )
    d_cols, gate_z, rest_got, out_got, cols, rest_own = together(
        (d_cols, gate_z, rest_got, out_got, cols, rest_sums[0])
    )

    d_all, *d_parts = d_cols
    rest_sum = add_up(rest_own, *rest_got).astype(bf16)
    d_parts, d_all, rest_sum = together((d_parts, d_all, rest_sum))
    d_parts = [d_parts[0]] + [swap("tensor", d_parts[j], j) for j in range(1, n)]
    rest_steps = halve_over_z(rest_sum, z, members)
    rest_sum = next(rest_steps)
    qkv_grad, share = qkv_grads(normed_all, d_all, w_cols, select)
    qkv_sum = lax.psum_scatter(qkv_grad, "dp", scatter_dimension=0, tiled=True)
    gate_sum = add_up(
        lax.dynamic_index_in_dim(gate_sums, z, 0, keepdims=False), *gate_z
    ).astype(bf16)
    gate_sum = add_up(
        gate_sum[0], *[swap("tensor", gate_sum[a], a * low) for a in range(1, high)]
    )
    middle_all = jnp.concatenate(middle) if parts > 1 else middle[0]
    out = add_up(middle_all, own_out, *out_got).astype(bf16)
    totals = jnp.sum(squares[:2], axis=1)
    scalars = jnp.pad(totals[None, :], ((0, 0), (0, depth - 2)))
    shares = jnp.concatenate([share.reshape(1, depth) / gain_one, feed_share, scalars])
    d_parts, shares, rest_sum, gate_sum, out = together((d_parts, shares, rest_sum, gate_sum, out))
    rest_sum = rest_steps.send(rest_sum)
    for rest_sum in rest_steps:
        pass
    sums = all_sum(all_sum(shares, "tensor"), "dp")
    out_sum = lax.psum_scatter(out_sum, "tensor", scatter_dimension=0, tiled=True)
    tokens_grad, first_grad = finish(info, d_parts, cols, tokens, gain_one, d_middle)
    entry_count = first_values.size * lax.axis_size("dp") * n
    return (
        out,
        tokens_grad,
        first_grad,
        sums[0],
        qkv_sum.astype(f32),
        out_sum[:own_width].astype(f32),
        sums[1],
        gate_sum.T,
        rest_sum[0, 0].T,
        rest_sum[0, 1],
        jnp.sqrt(sums[2, 1] / entry_count),
        jnp.sqrt(sums[2, 0] / entry_count),
    )


def solution(mesh):
    token_spec = P(("dp", "tensor"), None)
    return jax.shard_map(
        shards,
        mesh=mesh,
        in_specs=(
            token_spec,
            token_spec,
            P("dp", None),
            P(),
            P(None, "tensor"),
            P("tensor", None),
            P(),
            P(None, "tensor"),
            P(None, "tensor"),
            P("tensor", None),
            token_spec,
        ),
        out_specs=(
            token_spec,
            token_spec,
            token_spec,
            P(),
            P("dp", "tensor"),
            P("tensor", "dp"),
            P(),
            P("dp", "tensor"),
            P("dp", "tensor"),
            P("tensor", "dp"),
            P(),
            P(),
        ),
        check_vma=False,
    )
```

```python
import functools
import math

import jax
import jax.numpy as jnp
import numpy as np
from jax import lax
from jax.experimental import pallas as pl
from jax.experimental.pallas import tpu as pltpu
from jax.sharding import PartitionSpec as P

HD = 64
HALF = HD // 2
LANES = 128
GROUP = LANES // HALF
EPS = 1e-06
NEG = -1e30
VMEM = 60 << 20
f32 = jnp.float32
bf16 = jnp.bfloat16


def rope_tables(length):
    inverse = jnp.exp(-math.log(10000.0) * jnp.arange(HALF, dtype=f32) / HALF)
    angles = jnp.arange(length, dtype=f32)[:, None] * inverse[None, :]
    tile = lambda t: jnp.concatenate([t] * GROUP, axis=1)
    return tile(jnp.cos(angles)), tile(jnp.sin(angles))


def column_order(heads):
    value_width = max(LANES, heads * HD)
    order = np.full((4 * LANES + value_width,), -1, np.int32)
    for h in range(heads):
        for part in range(2):
            for half in range(2):
                at = (2 * part + half) * LANES + h * HALF
                src = h * 3 * HD + part * HD + half * HALF
                order[at : at + HALF] = np.arange(src, src + HALF)
        order[4 * LANES + h * HD : 4 * LANES + (h + 1) * HD] = np.arange(
            h * 3 * HD + 2 * HD, (h + 1) * 3 * HD
        )
    return order


def column_selector(heads):
    order = jnp.asarray(column_order(heads))
    rows = jnp.arange(3 * heads * HD, dtype=jnp.int32)
    return (rows[:, None] == order[None, :]).astype(bf16)


def dot_nt(a, b):
    return lax.dot_general(a, b, (((1,), (1,)), ((), ())), preferred_element_type=f32)


def dot_tn(a, b):
    return lax.dot_general(a, b, (((0,), (0,)), ((), ())), preferred_element_type=f32)


def dot_nn(a, b):
    return jnp.dot(a, b, preferred_element_type=f32)


def anywhere():
    return pl.BlockSpec(memory_space=pl.ANY)


def project_kernel(heads, placed, info_ref, *refs):
    count = len(placed)
    n = len({j for j, _ in placed})
    pieces, values = refs[:count], refs[count : count + n]
    w_ref, cos_ref, sin_ref, lim_ref = refs[count + n : count + n + 4]
    q_ref, k_ref, v_ref, sq_ref, x_ref, fv_ref, sem = refs[count + n + 4 :]
    at = pl.program_id(0)
    block = q_ref.shape[0]
    copies = []
    for i, (ref, (j, first)) in enumerate(zip(pieces, placed)):
        into = x_ref.at[j, first : first + ref.shape[0]]
        copies.append((j, pltpu.make_async_copy(ref, into, sem.at[i])))
    for j, ref in enumerate(values):
        copies.append((j, pltpu.make_async_copy(ref, fv_ref.at[j], sem.at[count + j])))

    @pl.when(at == 0)
    def _():
        sq_ref[...] = jnp.zeros_like(sq_ref)
        for _, copy in copies:
            copy.start()

    for j in range(n):

        @pl.when(at == j)
        def _():
            for owner, copy in copies:
                if owner == j:
                    copy.wait()

    acc = dot_nn(x_ref[at], w_ref[...])
    c, s = cos_ref[...], sin_ref[...]
    lane = lax.broadcasted_iota(jnp.int32, (block, LANES), 1)
    place = (info_ref[0] ^ at) * block + lax.broadcasted_iota(jnp.int32, (block, LANES), 0)
    inside = (place >= lim_ref[0:1, :]) & (place < lim_ref[1:2, :])
    doc_lane = (lane >= HD) & (lane < HD + 8)
    q_extra = jnp.where(doc_lane & jnp.logical_not(inside), NEG, 0.0)
    k_extra = jnp.where(inside, 1.0, jnp.where((lane >= HD + 8) & (lane < HD + 11), 1.0, 0.0))
    for ref, base, extra, scale in ((q_ref, 0, q_extra, HD**-0.5), (k_ref, 2, k_extra, 1.0)):
        u1 = acc[:, base * LANES : (base + 1) * LANES]
        u2 = acc[:, (base + 1) * LANES : (base + 2) * LANES]
        r1 = (u1 * c - u2 * s) * scale
        r2 = (u1 * s + u2 * c) * scale
        for h in range(heads):
            a = r1 if h == 0 else pltpu.roll(r1, LANES - HALF * h, 1)
            b = r2 if h == 1 else pltpu.roll(r2, (LANES + HALF - HALF * h) % LANES, 1)
            both = jnp.where(lane < HALF, a, jnp.where(lane < HD, b, extra))
            ref[:, h * LANES : (h + 1) * LANES] = both.astype(bf16)
    first = fv_ref[at].astype(f32)
    mixed = 0.5 * acc[:, 4 * LANES :] + 0.5 * first
    sq_ref[0:1, :] += jnp.sum(mixed * mixed, axis=0, keepdims=True)
    sq_ref[1:2, :] += jnp.sum(first * first, axis=0, keepdims=True)
    for h in range(heads):
        t = (h // 2) * LANES
        own = (lane < HD) if h % 2 == 0 else (lane >= HD)
        v_ref[:, h * LANES : (h + 1) * LANES] = jnp.where(
            own, mixed[:, t : t + LANES], 1.0
        ).astype(bf16)


def project(heads, info, parts, values, w, cos, sin, limits, rows):
    n = len(values)
    length = rows * n
    depth = parts[0][0].shape[1]
    width = values[0].shape[1]
    row = lambda i, info: (info[0] ^ i, 0)
    whole = lambda i, info: (0, 0)
    ext = heads * LANES
    placed = tuple((j, first) for _, j, first in parts)
    return pl.pallas_call(
        functools.partial(project_kernel, heads, placed),
        name="project",
        grid_spec=pltpu.PrefetchScalarGridSpec(
            num_scalar_prefetch=1,
            grid=(n,),
            in_specs=[anywhere()] * (len(parts) + n)
            + [
                pl.BlockSpec(w.shape, whole),
                pl.BlockSpec((rows, LANES), row),
                pl.BlockSpec((rows, LANES), row),
                pl.BlockSpec((8, LANES), whole),
            ],
            out_specs=[
                pl.BlockSpec((rows, ext), row),
                pl.BlockSpec((rows, ext), row),
                pl.BlockSpec((rows, ext), row),
                pl.BlockSpec((8, width), whole),
            ],
            scratch_shapes=[
                pltpu.VMEM((n, rows, depth), bf16),
                pltpu.VMEM((n, rows, width), bf16),
                pltpu.SemaphoreType.DMA((len(parts) + n,)),
            ],
        ),
        out_shape=[jax.ShapeDtypeStruct((length, ext), bf16)] * 3
        + [jax.ShapeDtypeStruct((8, width), f32)],
        compiler_params=pltpu.CompilerParams(vmem_limit_bytes=VMEM),
        cost_estimate=pl.CostEstimate(
            flops=2 * length * depth * w.shape[1],
            bytes_accessed=2 * (length * depth + w.size + 3 * length * ext),
            transcendentals=0,
        ),
    )(info, *[p for p, _, _ in parts], *values, w, cos, sin, limits)


def pieces(x):
    hi = x.astype(bf16).astype(f32)
    mid = (x - hi).astype(bf16).astype(f32)
    return hi, mid, x - hi - mid


def attend_kernel(
    heads, offset, bk, info_ref, begin_ref, q_ref, k_ref, v_ref, o_ref, qo_ref, m_ref, acc_ref
):
    bq = q_ref.shape[0]
    at = info_ref[0] ^ offset
    lane = lax.broadcasted_iota(jnp.int32, (bq, LANES), 1)
    r = lax.broadcasted_iota(jnp.int32, (bq, bk), 0)
    c = lax.broadcasted_iota(jnp.int32, (bq, bk), 1)
    col = [slice(h * LANES, (h + 1) * LANES) for h in range(heads)]
    spread = lambda m: jnp.concatenate([m] * (bk // LANES), axis=1)

    def visit(kb, mask, first):
        there = pl.ds(pl.multiple_of(kb * bk, bk), bk)
        for h in range(heads):
            s = dot_nt(q_ref[:, col[h]], k_ref[there, col[h]])
            if mask is not None:
                s = jnp.where(mask, s, NEG)
            new = jnp.broadcast_to(jnp.max(s, axis=1, keepdims=True), (bq, LANES))
            if not first:
                old = m_ref[:, col[h]]
                new = jnp.maximum(old, new)
            p = jnp.exp(s - spread(new)).astype(bf16)
            part = dot_nn(p, v_ref[there, col[h]])
            m_ref[:, col[h]] = new
            acc_ref[:, col[h]] = part if first else acc_ref[:, col[h]] * jnp.exp(old - new) + part

    for d in range(bq // bk):
        visit(at * (bq // bk) + d, c + d * bk <= r, d == 0)

    def step(kb, carry):
        visit(kb, None, False)
        return carry

    lax.fori_loop(begin_ref[at * (bq // bk)], at * (bq // bk), step, 0)
    low = lane < HD
    for t in range((heads + 1) // 2):
        a = acc_ref[:, col[2 * t]]
        b = acc_ref[:, col[2 * t + 1]] if 2 * t + 1 < heads else a
        total = pltpu.roll(jnp.where(low, b, a), HD, 1)
        result = jnp.where(low, a, b) / total
        if 2 * t + 1 >= heads:
            result = jnp.where(low, result, 0.0)
        o_ref[:, t * LANES : (t + 1) * LANES] = result.astype(bf16)
    for h in range(heads):
        a = acc_ref[:, col[h]]
        total = a if h % 2 == 0 else pltpu.roll(a, HD, 1)
        hi, mid, lo = pieces(-(m_ref[:, col[h]] + jnp.log(jnp.where(low, 1.0, total))))
        extra = jnp.where(
            lane == HD + 8, hi, jnp.where(lane == HD + 9, mid, jnp.where(lane == HD + 10, lo, 0.0))
        )
        fill = (lane >= HD + 8) & (lane < HD + 11)
        qo_ref[:, col[h]] = jnp.where(fill, extra, q_ref[:, col[h]].astype(f32)).astype(bf16)


def attend(heads, info, offset, q, k, v, begins, block, rows):
    length = q.shape[0]
    ext = heads * LANES
    width = max(LANES, heads * HD)
    whole = lambda i, info, b: (0, 0)
    return pl.pallas_call(
        functools.partial(attend_kernel, heads, offset, block),
        name="attend",
        grid_spec=pltpu.PrefetchScalarGridSpec(
            num_scalar_prefetch=2,
            grid=(1,),
            in_specs=[
                pl.BlockSpec((rows, ext), lambda i, info, b: (info[0] ^ offset, 0)),
                pl.BlockSpec((length, ext), whole),
                pl.BlockSpec((length, ext), whole),
            ],
            out_specs=[pl.BlockSpec((rows, width), whole), pl.BlockSpec((rows, ext), whole)],
            scratch_shapes=[pltpu.VMEM((rows, ext), f32), pltpu.VMEM((rows, ext), f32)],
        ),
        out_shape=[
            jax.ShapeDtypeStruct((rows, width), bf16),
            jax.ShapeDtypeStruct((rows, ext), bf16),
        ],
        compiler_params=pltpu.CompilerParams(vmem_limit_bytes=VMEM),
        cost_estimate=pl.CostEstimate(
            flops=2 * heads * rows * length * LANES,
            bytes_accessed=4 * length * ext,
            transcendentals=heads * rows * length // 2,
        ),
    )(info, begins, q, k, v)


def attend_back_kernel(heads, block, n, info_ref, begin_ref, *refs):
    q_parts, do_parts, o_parts = refs[:n], refs[n : 2 * n], refs[2 * n : 3 * n]
    k_ref, v_ref, cos_ref, sin_ref, g_ref = refs[3 * n : 3 * n + 5]
    sends = refs[3 * n + 5 : 4 * n + 5]
    q_all, do_all, o_all, dk_ref, dv_ref, dq_ref, de_ref, sem = refs[4 * n + 5 :]
    at = pl.program_id(0)
    rows = q_parts[0].shape[0]

    def moves(pairs):
        copies = []
        for i, (make, j) in enumerate(pairs):
            place = pl.ds(pl.multiple_of((info_ref[0] ^ j) * rows, rows), rows)
            copies.append(make(place, sem.at[i]))
        for copy in copies:
            copy.start()
        for copy in copies:
            copy.wait()

    @pl.when(at == 0)
    def _():
        moves(
            [
                (functools.partial(lambda src, dst, p, s: pltpu.make_async_copy(src, dst.at[p], s), part, whole), j)
                for parts, whole in ((q_parts, q_all), (do_parts, do_all), (o_parts, o_all))
                for j, part in enumerate(parts)
            ]
        )

    lane = lax.broadcasted_iota(jnp.int32, (block, LANES), 1)
    r = lax.broadcasted_iota(jnp.int32, (block, block), 0)
    c = lax.broadcasted_iota(jnp.int32, (block, block), 1)
    causal = r <= c
    low = lane < HD
    here = pl.ds(pl.multiple_of(at * block, block), block)
    col = [slice(h * LANES, (h + 1) * LANES) for h in range(heads)]

    for h in range(heads):
        t = slice((h // 2) * LANES, (h // 2 + 1) * LANES)
        own = low if h % 2 == 0 else jnp.logical_not(low)
        grad = do_all[here, t].astype(f32)
        product = grad * o_all[here, t].astype(f32)
        centre = jnp.sum(jnp.where(own, product, 0.0), axis=1, keepdims=True)
        hi, mid, lo = pieces(-jnp.broadcast_to(centre, (block, LANES)))
        spot = lane - (HD if h % 2 == 0 else 0)
        extra = jnp.where(spot == 0, hi, jnp.where(spot == 1, mid, jnp.where(spot == 2, lo, 0.0)))
        de_ref[:, col[h]] = jnp.where(own, grad, extra).astype(bf16)

    def visit(there, mask, first):
        st = [dot_nt(k_ref[there, c_], q_all[here, c_]) for c_ in col]
        dpt = [dot_nt(v_ref[there, c_], de_ref[:, c_]) for c_ in col]
        p = [jnp.exp(s) for s in st]
        if mask is not None:
            p = [jnp.where(mask, x, 0.0) for x in p]
        ds = [(x * y).astype(bf16) for x, y in zip(p, dpt)]
        p = [x.astype(bf16) for x in p]
        for h, c_ in enumerate(col):
            dv = dot_nn(p[h], de_ref[:, c_])
            dk = dot_nn(ds[h], q_all[here, c_])
            dq = dot_tn(ds[h], k_ref[there, c_])
            if first:
                dv_ref[there, c_] = dv
                dk_ref[there, c_] = dk
                dq_ref[:, c_] = dq
            else:
                dv_ref[there, c_] += dv
                dk_ref[there, c_] += dk
                dq_ref[:, c_] += dq

    visit(here, causal, True)

    def step(kb, carry):
        visit(pl.ds(pl.multiple_of(kb * block, block), block), None, False)
        return carry

    lax.fori_loop(begin_ref[at], at, step, 0)

    def turn_back(ref, rows, scale):
        u1 = u2 = None
        quarter = lane // HALF
        for h in range(heads):
            u = ref[rows, col[h]]
            a = u if h == 0 else pltpu.roll(u, HALF * h, 1)
            b = u if h == 1 else pltpu.roll(u, (LANES + HALF * h - HALF) % LANES, 1)
            u1 = a if h == 0 else jnp.where(quarter == h, a, u1)
            u2 = b if h == 0 else jnp.where(quarter == h, b, u2)
        if heads < GROUP:
            u1 = jnp.where(quarter < heads, u1, 0.0)
            u2 = jnp.where(quarter < heads, u2, 0.0)
        u1, u2 = u1 * scale, u2 * scale
        cs, sn = cos_ref[rows, :], sin_ref[rows, :]
        return (u1 * cs + u2 * sn).astype(bf16), (u2 * cs - u1 * sn).astype(bf16)

    def finish_block(i, carry):
        rows = pl.ds(pl.multiple_of(i * block, block), block)
        d1, d2 = turn_back(dk_ref, rows, 1.0)
        g_ref[rows, 2 * LANES : 3 * LANES] = d1
        g_ref[rows, 3 * LANES : 4 * LANES] = d2
        for t in range((heads + 1) // 2):
            a = dv_ref[rows, col[2 * t]]
            b = dv_ref[rows, col[2 * t + 1]] if 2 * t + 1 < heads else jnp.zeros_like(a)
            d_mix = jnp.where(low, a, b).astype(bf16)
            g_ref[rows, (4 + t) * LANES : (5 + t) * LANES] = (d_mix.astype(f32) * 0.5).astype(bf16)
        return carry

    u1 = u2 = None
    quarter = lane // HALF
    for h in range(heads):
        u = dq_ref[:, col[h]]
        a = u if h == 0 else pltpu.roll(u, HALF * h, 1)
        b = u if h == 1 else pltpu.roll(u, (LANES + HALF * h - HALF) % LANES, 1)
        u1 = a if h == 0 else jnp.where(quarter == h, a, u1)
        u2 = b if h == 0 else jnp.where(quarter == h, b, u2)
    if heads < GROUP:
        u1 = jnp.where(quarter < heads, u1, 0.0)
        u2 = jnp.where(quarter < heads, u2, 0.0)
    u1, u2 = u1 * HD**-0.5, u2 * HD**-0.5
    cs, sn = cos_ref[here, :], sin_ref[here, :]
    g_ref[here, 0:LANES] = (u1 * cs + u2 * sn).astype(bf16)
    g_ref[here, LANES : 2 * LANES] = (u2 * cs - u1 * sn).astype(bf16)

    @pl.when(at == pl.num_programs(0) - 1)
    def _():
        lax.fori_loop(0, pl.num_programs(0), finish_block, 0)
        moves(
            [
                (functools.partial(lambda dst, p, s: pltpu.make_async_copy(g_ref.at[p], dst, s), dst), j)
                for j, dst in enumerate(sends)
            ]
        )


def attend_back(heads, info, q_parts, k, v, do_parts, o_parts, cos, sin, begins, block):
    n = len(q_parts)
    rows = q_parts[0].shape[0]
    length = n * rows
    ext = heads * LANES
    width = o_parts[0].shape[1]
    whole = lambda i, info, b: (0, 0)
    anywhere = pl.BlockSpec(memory_space=pl.ANY)
    columns = 4 * LANES + width
    return pl.pallas_call(
        functools.partial(attend_back_kernel, heads, block, n),
        name="attend_back",
        grid_spec=pltpu.PrefetchScalarGridSpec(
            num_scalar_prefetch=2,
            grid=(length // block,),
            in_specs=[anywhere] * (3 * n)
            + [
                pl.BlockSpec((length, ext), whole),
                pl.BlockSpec((length, ext), whole),
                pl.BlockSpec((length, LANES), whole),
                pl.BlockSpec((length, LANES), whole),
            ],
            out_specs=[pl.BlockSpec((length, columns), whole)] + [anywhere] * n,
            scratch_shapes=[
                pltpu.VMEM((length, ext), bf16),
                pltpu.VMEM((length, width), bf16),
                pltpu.VMEM((length, width), bf16),
                pltpu.VMEM((length, ext), f32),
                pltpu.VMEM((length, ext), f32),
                pltpu.VMEM((block, ext), f32),
                pltpu.VMEM((block, ext), bf16),
                pltpu.SemaphoreType.DMA((3 * n,)),
            ],
        ),
        out_shape=[jax.ShapeDtypeStruct((length, columns), bf16)]
        + [jax.ShapeDtypeStruct((rows, columns), bf16)] * n,
        compiler_params=pltpu.CompilerParams(vmem_limit_bytes=VMEM),
        cost_estimate=pl.CostEstimate(
            flops=40 * heads * length * length * LANES,
            bytes_accessed=2 * 8 * length * ext,
            transcendentals=heads * length * length // 2,
        ),
    )(info, begins, *q_parts, *do_parts, *o_parts, k, v, cos, sin)


def split_axis(n):
    low = 1 << ((n.bit_length() - 1) // 2)
    return n // low, low


def swap(axis, value, offset):
    n = lax.axis_size(axis)
    return lax.ppermute(value, axis, [(i, i ^ offset) for i in range(n)])


def gather_rows(value, n):
    high, low = split_axis(n)
    rows = value.shape[0]
    half = rows // 2
    parts = {0: value}
    for b in range(1, low):
        parts[b] = swap("tensor", value, b)
    for a in range(1, high):
        parts[a * low] = swap("tensor", value, a * low)
    listed = [(parts[j], j, 0) for j in sorted(parts)]
    for a in range(1, high):
        for b in range(1, low):
            j = a * low + b
            listed.append((swap("tensor", parts[b][:half], a * low), j, 0))
            listed.append((swap("tensor", parts[a * low][half:], b), j, half))
    return listed


def after(value, *others):
    return lax.optimization_barrier((value,) + others)[0]


def add_up(first, *others):
    total = first.astype(f32)
    for other in others:
        total = total + other.astype(f32)
    return total


def over_replicas(value):
    if value.shape[1] % LANES == 0:
        return lax.all_gather(value, "dp", axis=0)
    return lax.all_gather(value, "dp", axis=1, tiled=True)


def halve_over_z(parts, z, count):
    step = 1
    while step < count:
        pairs = parts.reshape((-1, 2) + parts.shape[1:])
        side = (z // step) % 2
        pick = lambda which: lax.dynamic_index_in_dim(pairs, which, 1, keepdims=False)
        parts = add_up(pick(side), swap("dp", pick(1 - side), 2 * step))
        parts = parts.astype(bf16) if 2 * step < count else parts
        given = yield parts
        parts = parts if given is None else given
        step *= 2


def all_sum(value, axis):
    n = lax.axis_size(axis)
    step = 1
    while step < n:
        value = value + swap(axis, value, step)
        step *= 2
    return value


def norm_kernel(x_ref, gain_ref, o_ref):
    x = x_ref[...].astype(f32)
    inverse = lax.rsqrt(jnp.mean(x * x, axis=-1, keepdims=True) + EPS)
    o_ref[...] = (x * inverse * gain_ref[...]).astype(bf16)


def norm_rows(x, gain):
    rows, depth = x.shape
    block = min(rows, 128)
    return pl.pallas_call(
        norm_kernel,
        name="norm_rows",
        grid=(rows // block,),
        in_specs=[
            pl.BlockSpec((block, depth), lambda i: (i, 0)),
            pl.BlockSpec((1, depth), lambda i: (0, 0)),
        ],
        out_specs=pl.BlockSpec((block, depth), lambda i: (i, 0)),
        out_shape=jax.ShapeDtypeStruct((rows, depth), bf16),
        compiler_params=pltpu.CompilerParams(vmem_limit_bytes=VMEM),
        cost_estimate=pl.CostEstimate(
            flops=5 * x.size, bytes_accessed=4 * x.size, transcendentals=rows
        ),
    )(x, gain)


def branch_kernel(n, parts, info_ref, *refs):
    att = refs[:n]
    slices_ref, tok_ref, gain_ref, mid_ref, h_ref, w_ref = refs[n : n + 6]
    h_parts = refs[n + 6 : n + 6 + parts]
    all_ref, sem, w_sem = refs[n + 6 + parts :]
    at = pl.program_id(0)
    size = tok_ref.shape[0]
    width = att[0].shape[1]

    @pl.when(at == 0)
    def _():
        copies = [
            pltpu.make_async_copy(
                att[j], all_ref.at[:, j * width : (j + 1) * width], sem.at[j]
            )
            for j in range(n)
        ]
        if len(slices_ref.shape) == 3:
            lanes = slices_ref.shape[2]
            copies += [
                pltpu.make_async_copy(
                    slices_ref.at[d], w_ref.at[:, d * lanes : (d + 1) * lanes], w_sem.at[d]
                )
                for d in range(slices_ref.shape[0])
            ]
        else:
            copies.append(pltpu.make_async_copy(slices_ref, w_ref, w_sem.at[0]))
        for copy in copies:
            copy.start()
        for copy in copies:
            copy.wait()

    here = pl.ds(pl.multiple_of(at * size, size), size)
    x = tok_ref[...].astype(f32) + dot_nn(all_ref[here, :], w_ref[...])
    mid_ref[...] = x
    inverse = lax.rsqrt(jnp.mean(x * x, axis=-1, keepdims=True) + EPS)
    h = (x * inverse * gain_ref[...]).astype(bf16)
    h_ref[...] = h
    for p in range(parts):

        @pl.when(at == p)
        def _():
            h_parts[p][...] = h


def branch(info, att, w_slices, tokens, gain, parts):
    n = len(att)
    rows, width = att[0].shape
    depth = tokens.shape[1]
    size = rows // parts
    whole = lambda i, info: (0, 0)
    row = lambda i, info: (i, 0)
    count = w_slices.shape[0] if w_slices.ndim == 3 else 1
    return pl.pallas_call(
        functools.partial(branch_kernel, n, parts),
        name="branch",
        grid_spec=pltpu.PrefetchScalarGridSpec(
            num_scalar_prefetch=1,
            grid=(parts,),
            in_specs=[anywhere()] * (n + 1)
            + [pl.BlockSpec((size, depth), row), pl.BlockSpec((1, depth), whole)],
            out_specs=[pl.BlockSpec((size, depth), row)] * 2
            + [pl.BlockSpec((n * width, depth), whole)]
            + [pl.BlockSpec((size, depth), whole)] * parts,
            scratch_shapes=[
                pltpu.VMEM((rows, n * width), bf16),
                pltpu.SemaphoreType.DMA((n,)),
                pltpu.SemaphoreType.DMA((count,)),
            ],
        ),
        out_shape=[
            jax.ShapeDtypeStruct((rows, depth), f32),
            jax.ShapeDtypeStruct((rows, depth), bf16),
            jax.ShapeDtypeStruct((n * width, depth), bf16),
        ]
        + [jax.ShapeDtypeStruct((size, depth), bf16)] * parts,
        compiler_params=pltpu.CompilerParams(vmem_limit_bytes=VMEM),
        cost_estimate=pl.CostEstimate(
            flops=2 * rows * depth * n * width,
            bytes_accessed=2 * n * width * depth + 8 * rows * depth,
            transcendentals=rows,
        ),
    )(info, *att, w_slices, tokens, gain)


def feed_kernel(shards_in, shared, send, act_first, info_ref, h_ref, g_ref, *refs):
    count = sum(shards_in)
    weights, refs = refs[:count], refs[count + shared :]
    out_ref, dh_ref, act_out, w_ref, sem, act_ref, act_sem = refs[:7]
    out_acc, dh_acc = refs[7:] if send else (out_ref, dh_ref)
    high, rows_w, depth = w_ref.shape
    units = rows_w // 3
    copies, at, used = [], 0, 0
    for a, pieces_in in enumerate(shards_in):
        groups = []
        for m in range(3):
            span = pl.ds(m * units, units)
            ref = weights[at + m] if pieces_in == 3 else weights[at]
            if pieces_in == 3:
                moves = [(ref, w_ref.at[a, span])]
            elif len(ref.shape) == 3:
                size = ref.shape[2]
                moves = [
                    (ref.at[d, span], w_ref.at[a, span, d * size : (d + 1) * size])
                    for d in range(ref.shape[0])
                ]
            else:
                moves = [(ref.at[span], w_ref.at[a, span])]
            groups.append(
                [
                    pltpu.make_async_copy(src, dst, sem.at[used + i])
                    for i, (src, dst) in enumerate(moves)
                ]
            )
            used += len(moves)
        at += pieces_in
        copies.append(groups)
    first = pl.program_id(0) == 0

    @pl.when(first)
    def _():
        for groups in copies:
            for group in groups:
                for copy in group:
                    copy.start()

    def products(a):
        def weight(m):
            @pl.when(first)
            def _():
                for copy in copies[a][m]:
                    copy.wait()

            return w_ref[a, m * units : (m + 1) * units, :]

        gate = dot_nt(h_ref[...], weight(0))
        up = dot_nt(h_ref[...], weight(1))
        return gate, up, dot_nt(g_ref[...], weight(2))

    leaving = []
    ahead = products(0)
    for a in range(high):
        gate, up, back = ahead
        if a + 1 < high:
            ahead = products(a + 1)
        s = 1.0 / (1.0 + jnp.exp(-gate))
        gs = gate * s
        hidden = (gs * up).astype(bf16)
        d_up = (back * gs).astype(bf16)
        d_gate = (back * up * (s + gs * (1.0 - s))).astype(bf16)
        act_ref[a, 0] = d_gate
        act_ref[a, 1] = d_up
        act_ref[a, 2] = hidden
        rows = h_ref.shape[0]
        leaving.append(
            pltpu.make_async_copy(
                act_ref.at[a], act_out.at[a, :, act_first : act_first + rows], act_sem.at[a]
            )
        )
        leaving[-1].start()
        gate_w, up_w, down_w = (w_ref[a, m * units : (m + 1) * units, :] for m in range(3))
        d_part = dot_nn(d_gate, gate_w) + dot_nn(d_up, up_w)
        part = dot_nn(hidden, down_w)
        if a == 0:
            dh_acc[...] = d_part
            out_acc[...] = part
        else:
            dh_acc[...] += d_part
            out_acc[...] += part
    if send:
        out_ref[...] = out_acc[...].astype(bf16)
        dh_ref[...] = dh_acc[...].astype(bf16)
    for copy in leaving:
        copy.wait()


def feed(info, h, g, g_first, weights, act_first, act_rows, shared, out_first, out_rows, send):
    rows, depth = h.shape
    high = len(weights)
    flat = [w for shard in weights for w in shard]
    units = weights[0][0].shape[0] if len(weights[0]) == 3 else weights[0][0].shape[-2] // 3
    block = rows
    at, out_at = g_first // block, out_first // block
    row = lambda i, info: (i, 0)
    kind = bf16 if send else f32
    moves = sum(
        3 if len(shard) == 3 else 3 * (shard[0].shape[0] if shard[0].ndim == 3 else 1)
        for shard in weights
    )
    base = 3 + len(flat)
    aliases = {} if not shared else {base: 2} if len(shared) == 1 else {base: 0, base + 1: 2}
    return pl.pallas_call(
        functools.partial(
            feed_kernel, tuple(len(shard) for shard in weights), len(shared), send, act_first
        ),
        name="feed",
        grid_spec=pltpu.PrefetchScalarGridSpec(
            num_scalar_prefetch=1,
            grid=(1,),
            in_specs=[
                pl.BlockSpec((block, depth), row),
                pl.BlockSpec((block, depth), lambda i, info: (at, 0)),
            ]
            + [anywhere()] * (len(flat) + len(shared)),
            out_specs=[
                pl.BlockSpec((block, depth), lambda i, info: (out_at, 0)),
                pl.BlockSpec((block, depth), row),
                anywhere(),
            ],
            scratch_shapes=[
                pltpu.VMEM((high, 3 * units, depth), bf16),
                pltpu.SemaphoreType.DMA((moves,)),
                pltpu.VMEM((high, 3, block, units), bf16),
                pltpu.SemaphoreType.DMA((high,)),
            ]
            + ([pltpu.VMEM((block, depth), f32)] * 2 if send else []),
        ),
        out_shape=[
            jax.ShapeDtypeStruct((out_rows, depth), kind),
            jax.ShapeDtypeStruct((rows, depth), kind),
            jax.ShapeDtypeStruct((high, 3, act_rows, units), bf16),
        ],
        input_output_aliases=aliases,
        compiler_params=pltpu.CompilerParams(vmem_limit_bytes=VMEM),
        cost_estimate=pl.CostEstimate(
            flops=12 * rows * depth * high * units,
            bytes_accessed=6 * depth * high * units + 12 * rows * depth,
            transcendentals=2 * rows * high * units,
        ),
    )(info, h, g, *flat, *shared)


def feed_grad_kernel(h_rows, g_rows, members, info_ref, list_ref, *refs):
    h, g = refs[: len(h_rows)], refs[len(h_rows) : len(h_rows) + len(g_rows)]
    act_ref, keep_ref, send_ref, h_ref, g_ref, acc_ref, h_sem, g_sem = refs[
        len(h_rows) + len(g_rows) :
    ]
    core = info_ref[1]
    at = pl.program_id(0)

    def copies(parts, rows, whole, sem):
        return [
            pltpu.make_async_copy(ref, whole.at[first : first + ref.shape[0]], sem.at[i])
            for i, (ref, first) in enumerate(zip(parts, rows))
        ]

    h_copies, g_copies = copies(h, h_rows, h_ref, h_sem), copies(g, g_rows, g_ref, g_sem)

    @pl.when(at == 0)
    def _():
        for copy in h_copies + g_copies:
            copy.start()
        for copy in h_copies:
            copy.wait()

    @pl.when(at == 1)
    def _():
        for copy in g_copies:
            copy.wait()

    @pl.when(list_ref[at, 1] < 2)
    def _():
        acc_ref[...] = dot_tn(act_ref[0, 0], h_ref[...])

    @pl.when(list_ref[at, 1] == 2)
    def _():
        acc_ref[...] = dot_tn(act_ref[0, 0], g_ref[...])

    size = acc_ref.shape[1] // (2 * members)
    for z in range(members):
        for ref, side in ((keep_ref, core), (send_ref, 1 - core)):
            if size % LANES == 0:
                lanes = pl.ds(pl.multiple_of((2 * z + side) * size, size), size)
                ref[0, z] = acc_ref[:, lanes].astype(bf16)
            else:
                pair = acc_ref[:, 2 * z * size : 2 * (z + 1) * size]
                ref[0, z] = jnp.where(side == 0, pair[:, :size], pair[:, size:]).astype(bf16)


def feed_grads(info, h, h_rows, g, g_rows, act, wanted, members):
    depth = h[0].shape[1]
    _, _, rows, units = act.shape
    size = depth // (2 * members)
    count = len(wanted)
    out = jax.ShapeDtypeStruct((count, members, units, size), bf16)
    return pl.pallas_call(
        functools.partial(feed_grad_kernel, tuple(h_rows), tuple(g_rows), members),
        name="feed_grads",
        grid_spec=pltpu.PrefetchScalarGridSpec(
            num_scalar_prefetch=2,
            grid=(count,),
            in_specs=[anywhere()] * (len(h) + len(g))
            + [pl.BlockSpec((1, 1, rows, units), lambda i, info, w: (w[i, 0], w[i, 1], 0, 0))],
            out_specs=[pl.BlockSpec((1, members, units, size), lambda i, info, w: (i, 0, 0, 0))]
            * 2,
            scratch_shapes=[
                pltpu.VMEM((rows, depth), bf16),
                pltpu.VMEM((rows, depth), bf16),
                pltpu.VMEM((units, depth), f32),
                pltpu.SemaphoreType.DMA((len(h),)),
                pltpu.SemaphoreType.DMA((len(g),)),
            ],
        ),
        out_shape=[out, out],
        compiler_params=pltpu.CompilerParams(vmem_limit_bytes=VMEM),
        cost_estimate=pl.CostEstimate(
            flops=2 * count * rows * depth * units,
            bytes_accessed=4 * count * depth * units,
            transcendentals=0,
        ),
    )(info, jnp.asarray(wanted, jnp.int32), *h, *g, act)


def branch_back_kernel(n, parts, info_ref, dh_ref, mid_ref, g_ref, gain_ref, w_ref, *refs):
    far, refs = refs[:parts], refs[parts:]
    dm_ref, db_ref, gg_ref = refs[:3]
    da = refs[3:]
    at = pl.program_id(0)
    width = da[0].shape[1]
    x = mid_ref[...]
    inverse = lax.rsqrt(jnp.mean(x * x, axis=-1, keepdims=True) + EPS)
    unit = x * inverse
    received = far[0][...]
    for p in range(1, parts):
        received = jnp.where(at == p, far[p][...], received)
    cotangent = dh_ref[...] + received.astype(f32)
    e = cotangent * gain_ref[...]
    inner = jnp.mean(e * unit, axis=-1, keepdims=True)
    d_mid = g_ref[...].astype(f32) + inverse * (e - unit * inner)
    share = jnp.sum(cotangent * unit, axis=0, keepdims=True)

    @pl.when(at == 0)
    def _():
        gg_ref[...] = jnp.zeros_like(gg_ref)

    gg_ref[...] += share
    dm_ref[...] = d_mid
    rounded = d_mid.astype(bf16)
    db_ref[...] = rounded
    for j in range(n):
        da[j][...] = dot_nt(rounded, w_ref[j * width : (j + 1) * width, :]).astype(bf16)


def branch_back(info, d_h, d_far, middle, g, gain, w_all, width):
    n = w_all.shape[0] // width
    parts = len(d_far)
    rows, depth = middle.shape
    size = rows // parts
    whole = lambda i, info: (0, 0)
    row = lambda i, info: (i, 0)
    part = pl.BlockSpec((size, depth), row)
    return pl.pallas_call(
        functools.partial(branch_back_kernel, n, parts),
        name="branch_back",
        grid_spec=pltpu.PrefetchScalarGridSpec(
            num_scalar_prefetch=1,
            grid=(parts,),
            in_specs=[part, part, part]
            + [pl.BlockSpec(gain.shape, whole), pl.BlockSpec(w_all.shape, whole)]
            + [pl.BlockSpec((size, depth), whole)] * parts,
            out_specs=[part, part, pl.BlockSpec((1, depth), whole)]
            + [pl.BlockSpec((size, width), row)] * n,
        ),
        out_shape=[
            jax.ShapeDtypeStruct((rows, depth), f32),
            jax.ShapeDtypeStruct((rows, depth), bf16),
            jax.ShapeDtypeStruct((1, depth), f32),
        ]
        + [jax.ShapeDtypeStruct((rows, width), bf16)] * n,
        compiler_params=pltpu.CompilerParams(vmem_limit_bytes=VMEM),
        cost_estimate=pl.CostEstimate(
            flops=2 * rows * depth * n * width,
            bytes_accessed=20 * rows * depth + 2 * n * width * depth,
            transcendentals=rows,
        ),
    )(info, d_h, middle, g, gain, w_all, *d_far)


def out_grad_kernel(n, info_ref, *refs):
    db_ref = refs[0]
    att = refs[1 : 1 + n]
    o_ref = refs[1 + n]
    for j in range(n):
        o_ref[info_ref[0] ^ j] = dot_tn(db_ref[...], att[j][...]).astype(bf16)


def out_grads(info, d_branch, att):
    n = len(att)
    rows, depth = d_branch.shape
    width = att[0].shape[1]
    whole = lambda i, info: (0, 0)
    return pl.pallas_call(
        functools.partial(out_grad_kernel, n),
        name="out_grads",
        grid_spec=pltpu.PrefetchScalarGridSpec(
            num_scalar_prefetch=1,
            grid=(1,),
            in_specs=[pl.BlockSpec(d_branch.shape, whole)]
            + [pl.BlockSpec(a.shape, whole) for a in att],
            out_specs=pl.BlockSpec((n, depth, width), lambda i, info: (0, 0, 0)),
        ),
        out_shape=jax.ShapeDtypeStruct((n, depth, width), bf16),
        compiler_params=pltpu.CompilerParams(vmem_limit_bytes=VMEM),
        cost_estimate=pl.CostEstimate(
            flops=2 * rows * depth * n * width,
            bytes_accessed=2 * rows * depth + 4 * n * width * depth,
            transcendentals=0,
        ),
    )(info, d_branch, *att)


def qkv_grad_kernel(rows, placed, info_ref, *refs):
    count = len(placed)
    pieces = refs[:count]
    d_ref, w_ref, sel_ref, out_ref, o_ref, share_ref, x_ref, sem = refs[count:]
    columns = sel_ref.shape[0]
    at = pl.program_id(0)
    block = o_ref.shape[0]

    @pl.when(at == 0)
    def _():
        copies = []
        for i, (ref, (j, first)) in enumerate(zip(pieces, placed)):
            size = ref.shape[0]
            place = pl.ds(pl.multiple_of((info_ref[0] ^ j) * rows + first, size), size)
            copies.append(pltpu.make_async_copy(ref, x_ref.at[place], sem.at[i]))
        for copy in copies:
            copy.start()
        for copy in copies:
            copy.wait()

    lanes = pl.ds(pl.multiple_of(at * block, block), block)
    g = dot_tn(x_ref[:, lanes], d_ref[...])
    share_ref[...] = jnp.sum(g * w_ref[...].astype(f32), axis=1, keepdims=True)
    o_ref[:, :columns] = dot_nt(g.astype(bf16), sel_ref[...]).astype(bf16)
    o_ref[:, columns:] = out_ref[...]


def qkv_grads(info, parts, d, w, select, beside, rows):
    length = d.shape[0]
    depth = w.shape[0]
    columns = select.shape[0]
    total = columns + beside.shape[1]
    block = 512
    placed = tuple((j, first) for _, j, first in parts)
    whole = lambda i, info: (0, 0)
    row = lambda i, info: (i, 0)
    return pl.pallas_call(
        functools.partial(qkv_grad_kernel, rows, placed),
        name="qkv_grads",
        grid_spec=pltpu.PrefetchScalarGridSpec(
            num_scalar_prefetch=1,
            grid=(depth // block,),
            in_specs=[anywhere()] * len(parts)
            + [
                pl.BlockSpec(d.shape, whole),
                pl.BlockSpec((block, w.shape[1]), row),
                pl.BlockSpec(select.shape, whole),
                pl.BlockSpec((block, beside.shape[1]), row),
            ],
            out_specs=[pl.BlockSpec((block, total), row), pl.BlockSpec((block, 1), row)],
            scratch_shapes=[
                pltpu.VMEM((length, depth), bf16),
                pltpu.SemaphoreType.DMA((len(parts),)),
            ],
        ),
        out_shape=[
            jax.ShapeDtypeStruct((depth, total), bf16),
            jax.ShapeDtypeStruct((depth, 1), f32),
        ],
        compiler_params=pltpu.CompilerParams(vmem_limit_bytes=VMEM),
        cost_estimate=pl.CostEstimate(
            flops=2 * length * depth * d.shape[1],
            bytes_accessed=2 * (length * depth + d.size + 2 * w.size),
            transcendentals=0,
        ),
    )(info, *[p for p, _, _ in parts], d, w, select, beside)


def finish_kernel(n, wide, info_ref, *refs):
    d = refs[:n]
    cols_ref, tok_ref, gain_ref, dm_ref, o_ref = refs[n : n + 5]
    w_ref, sem = refs[-2:]
    t = info_ref[0]
    members, _, size, columns = cols_ref.shape
    depth = members * size
    first = pl.program_id(0) == 0
    copies = [
        pltpu.make_async_copy(cols_ref.at[:, j], w_ref.at[j], sem.at[j]) for j in range(n)
    ]

    @pl.when(first)
    def _():
        for copy in copies:
            copy.start()

    for j in range(n):

        @pl.when(first)
        def _():
            copies[j].wait()

        part = dot_nt(d[j][...], w_ref[j].reshape(depth, columns))
        o_ref[...] = part if j == 0 else o_ref[...] + part
    x = tok_ref[...].astype(f32)
    inverse = lax.rsqrt(jnp.mean(x * x, axis=-1, keepdims=True) + EPS)
    unit = x * inverse
    e = o_ref[...] * gain_ref[...]
    inner = jnp.mean(e * unit, axis=-1, keepdims=True)
    o_ref[...] = dm_ref[...] + inverse * (e - unit * inner)
    if wide:
        first_ref = refs[n + 5]
        width = depth // n
        for j in range(n):
            at = pl.ds(pl.multiple_of((t ^ j) * width, width), width)
            first_ref[:, at] = d[j][:, 4 * LANES :].astype(f32)


def finish(info, d_parts, cols, tokens, gain, d_middle):
    n = len(d_parts)
    rows, depth = tokens.shape
    block = min(rows, 512)
    wide = (depth // n) % LANES == 0
    row = lambda i, info: (i, 0)
    whole = lambda i, info: (0, 0)
    count = 2 if wide else 1
    members, _, size, columns = cols.shape
    out = pl.pallas_call(
        functools.partial(finish_kernel, n, wide),
        name="finish",
        grid_spec=pltpu.PrefetchScalarGridSpec(
            num_scalar_prefetch=1,
            grid=(rows // block,),
            in_specs=[pl.BlockSpec((block, d.shape[1]), row) for d in d_parts]
            + [
                anywhere(),
                pl.BlockSpec((block, depth), row),
                pl.BlockSpec((1, depth), whole),
                pl.BlockSpec((block, depth), row),
            ],
            out_specs=[pl.BlockSpec((block, depth), row)] * count,
            scratch_shapes=[
                pltpu.VMEM((n, members, size, columns), bf16),
                pltpu.SemaphoreType.DMA((n,)),
            ],
        ),
        out_shape=[jax.ShapeDtypeStruct((rows, depth), f32)] * count,
        compiler_params=pltpu.CompilerParams(vmem_limit_bytes=VMEM),
        cost_estimate=pl.CostEstimate(
            flops=40 * rows * cols.size,
            bytes_accessed=2 * cols.size + 16 * rows * depth,
            transcendentals=rows,
        ),
    )(info, *d_parts, cols, tokens, gain, d_middle)
    if wide:
        return out
    heads_width = depth // n
    pieces_ = jnp.stack([d[:, 4 * LANES : 4 * LANES + heads_width] for d in d_parts])
    ordered = jnp.take(pieces_, info[0] ^ jnp.arange(n), axis=0)
    return out[0], ordered.transpose(1, 0, 2).reshape(rows, depth).astype(f32)


def shards(
    tokens,
    first_values,
    doc_lengths,
    attention_norm_gain,
    w_qkv,
    w_out,
    feedforward_norm_gain,
    w_gate,
    w_up,
    w_down,
    out_grad,
):
    n = lax.axis_size("tensor")
    high, low = split_axis(n)
    members = lax.axis_size("dp") // 2
    t = lax.axis_index("tensor")
    z, core = lax.axis_index("dp") // 2, lax.axis_index("dp") % 2
    info = jnp.stack([t, core]).astype(jnp.int32)
    rows, depth = tokens.shape
    heads = w_out.shape[0] // HD
    own_width = heads * HD
    width = max(LANES, own_width)
    length = rows * n
    block = min(256, rows)
    gain_one = attention_norm_gain[None, :]
    gain_two = feedforward_norm_gain[None, :]
    missing = width - own_width
    widen = lambda v: jnp.pad(v, ((0, 0), (0, missing))) if missing else v
    replicas = 2 * members
    size_d = depth // replicas
    mine = lambda w, axis: lax.dynamic_slice_in_dim(w, lax.axis_index("dp") * size_d, size_d, axis)

    together = lax.optimization_barrier
    cosine, sine_table = rope_tables(length)
    ends = jnp.cumsum(doc_lengths[0])
    starts = ends - doc_lengths[0]
    docs = doc_lengths.shape[1]
    limits = jnp.pad(jnp.stack([starts, ends]), ((0, 6), (HD, LANES - HD - docs)))
    heads_at = jnp.arange(length // block, dtype=jnp.int32) * block
    begins = jnp.max(jnp.where(starts[None, :] <= heads_at[:, None], starts[None, :], 0), axis=1)
    begins = (begins // block).astype(jnp.int32)
    select = column_selector(heads)
    w_cols = jnp.dot(w_qkv, select, preferred_element_type=f32).astype(bf16)

    own_weights = (w_gate.T, w_up.T, w_down)
    weight_slice = jnp.concatenate([mine(w, 1) for w in own_weights])
    value_parts = [
        widen(lax.dynamic_slice_in_dim(first_values, (t ^ j) * own_width, own_width, 1))
        for j in range(n)
    ]
    w_out_wide = jnp.pad(w_out, ((0, missing), (0, 0))) if missing else w_out
    out_slice = mine(w_out_wide, 1)
    value_parts, out_slice, tokens_late = together((value_parts, out_slice, tokens))
    out_slices = [out_slice] + [swap("tensor", out_slice, j) for j in range(1, n)]
    w_out_all = over_replicas(jnp.concatenate(out_slices))
    value_parts = [value_parts[0]] + [swap("tensor", value_parts[j], j) for j in range(1, n)]
    normed = norm_rows(tokens_late, gain_one)
    normed_parts = gather_rows(normed, n)
    placed = [(j, first) for _, j, first in normed_parts]
    pieces_in = [piece for piece, _, _ in normed_parts]
    cols_slice = mine(w_cols, 0)
    (
        pieces_in, value_parts, weight_slice, w_cols, cols_slice, cosine, sine_table, limits,
        w_out_all, grad_late,
    ) = together(
        (
            pieces_in, value_parts, weight_slice, w_cols, cols_slice, cosine, sine_table, limits,
            w_out_all, out_grad,
        )
    )

    far_slices = [swap("tensor", weight_slice, a * low) for a in range(1, high)]
    grad_rows = [out_grad] + [swap("tensor", grad_late, b) for b in range(1, low)]
    normed_parts = [(piece, j, first) for piece, (j, first) in zip(pieces_in, placed)]
    q, k, v, squares = project(
        heads, info, normed_parts, value_parts, w_cols, cosine, sine_table, limits, rows
    )
    q, far_slices = together((q, far_slices))
    seen = {}
    for j in range(n - 1, -1, -1):
        seen[j] = attend(heads, info, j, q, k, v, begins, block, rows)
        if j == 1:
            q, *grad_rows = together((q, *grad_rows))
    feed_far = [(over_replicas(w),) for w in far_slices]
    heads_rows = [seen[0][0]] + [swap("tensor", seen[j][0], j) for j in range(1, n)]
    heads_rows, cols_slice = together((heads_rows, cols_slice))

    parts = 2 if rows >= 512 else 1
    size = rows // parts
    middle, second, w_out_all, *second_parts = branch(
        info, heads_rows, w_out_all, tokens, gain_two, parts
    )
    second_parts, cols_slice = together((second_parts, cols_slice))
    far_keys = [(b, p) for b in range(1, low) for p in range(parts)]
    inputs = {(b, p): swap("tensor", second_parts[p], b) for b, p in far_keys}
    cols_far = [cols_slice] + [swap("tensor", cols_slice, j) for j in range(1, n)]
    shards_held = [own_weights] + feed_far
    own_out, own_back, act = feed(
        info, second, out_grad, 0, shards_held, 0, low * rows, [], 0, rows, False
    )
    shared, backs = [act], {}
    for b, p in far_keys:
        if (b, p) == far_keys[-1]:
            shared, cols_far = together((shared, cols_far))
        arrived, shared = together((inputs[b, p], shared))
        to_send, backs[b, p], act = feed(
            info, arrived, grad_rows[b], p * size, shards_held, b * rows + p * size, low * rows,
            shared, (b - 1) * rows + p * size, (low - 1) * rows, True,
        )
        inputs[b, p] = arrived
        shared = [to_send, act]
    d_far = [[swap("tensor", backs[b, p], b) for b in range(1, low)] for p in range(parts)]
    d_far = [d[0] if low == 2 else add_up(*d) for d in d_far]
    sources = (
        [second] + [inputs[key] for key in far_keys],
        [0] + [b * rows + p * size for b, p in far_keys],
        grad_rows,
        [b * rows for b in range(low)],
        act,
    )
    cols = lax.all_gather(jnp.stack(cols_far), "dp", axis=0)
    early = [(a, m) for a in range(1, high) for m in range(3)] + [(0, 0)]
    keep, send = feed_grads(info, *sources, early, members)
    d_far, keep, send, to_send = together((d_far, keep, send, to_send))

    got = swap("dp", send, 1)
    d_middle, d_branch, feed_share, *d_att = branch_back(
        info, own_back, d_far, middle, out_grad, gain_two, w_out_all, width
    )
    act, d_att[0] = together((act, d_att[0]))
    late_keep, late_send = feed_grads(info, *sources[:-1], act, [(0, 1), (0, 2)], members)
    late_got = swap("dp", late_send, 1)
    d_att = [d_att[0]] + [swap("tensor", d_att[j], j) for j in range(1, n)]
    add_two = lambda lo, hi: add_up(keep[lo:hi], got[lo:hi]).astype(bf16)
    rest_sums = [add_two(3 * a + 1, 3 * a + 3) for a in range(high - 1)]
    gate_sums = jnp.stack(
        [add_two(i, i + 1)[0] for i in [3 * (high - 1)] + [3 * a for a in range(high - 1)]], axis=1
    )
    out_grad_w = out_grads(info, d_branch, heads_rows)
    d_att, gate_sums, rest_sums, to_send, out_grad_w, late_keep, late_got = together(
        (d_att, gate_sums, rest_sums, to_send, out_grad_w, late_keep, late_got)
    )

    gate_z = [
        swap("dp", lax.dynamic_index_in_dim(gate_sums, z ^ k, 0, keepdims=False), 2 * k)
        for k in range(1, members)
    ]
    rest_got = [swap("tensor", rest_sums[a - 1], a * low) for a in range(1, high)]
    out_got = [swap("tensor", to_send[(b - 1) * rows : b * rows], b) for b in range(1, low)]
    out_sum = lax.psum_scatter(out_grad_w, "tensor", scatter_dimension=0, tiled=False)
    d_cols = attend_back(
        heads, info, [seen[j][1] for j in range(n)], k, v, d_att, [seen[j][0] for j in range(n)],
        cosine, sine_table, begins, block,
    )
    d_cols, gate_z, rest_got, out_got, cols, late_keep = together(
        (d_cols, gate_z, rest_got, out_got, cols, late_keep)
    )

    d_all, *d_parts = d_cols
    rest_sum = add_up(late_keep, late_got, *rest_got).astype(bf16).swapaxes(0, 1)
    d_parts, d_all, rest_sum = together((d_parts, d_all, rest_sum))
    d_parts = [d_parts[0]] + [swap("tensor", d_parts[j], j) for j in range(1, n)]
    rest_steps = halve_over_z(rest_sum, z, members)
    rest_sum = next(rest_steps)
    grads, share = qkv_grads(info, normed_parts, d_all, w_cols, select, out_sum, rows)
    grads = lax.psum_scatter(grads, "dp", scatter_dimension=0, tiled=True)
    gate_sum = add_up(
        lax.dynamic_index_in_dim(gate_sums, z, 0, keepdims=False), *gate_z
    ).astype(bf16)
    gate_sum = add_up(
        gate_sum[0], *[swap("tensor", gate_sum[a], a * low) for a in range(1, high)]
    )
    out = add_up(middle, own_out, *out_got).astype(bf16)
    totals = jnp.sum(squares[:2], axis=1)
    scalars = jnp.pad(totals[None, :], ((0, 0), (0, depth - 2)))
    shares = jnp.concatenate([share.reshape(1, depth) / gain_one, feed_share, scalars])
    shares = all_sum(shares, "dp")
    rest_sum, shares = together((rest_sum, shares))
    rest_sum = rest_steps.send(rest_sum)
    for rest_sum in rest_steps:
        pass
    d_parts, gate_sum, out = together((d_parts, gate_sum, out))
    tokens_grad, first_grad = finish(info, d_parts, cols, tokens, gain_one, d_middle)
    sums = all_sum(shares, "tensor")
    columns = 3 * own_width
    entry_count = first_values.size * lax.axis_size("dp") * n
    return (
        out,
        tokens_grad,
        first_grad,
        sums[0],
        grads[:, :columns].astype(f32),
        grads[:, columns : columns + own_width].T.astype(f32),
        sums[1],
        gate_sum.T,
        rest_sum[0, 0].T,
        rest_sum[0, 1],
        jnp.sqrt(sums[2, 1] / entry_count),
        jnp.sqrt(sums[2, 0] / entry_count),
    )


def solution(mesh):
    token_spec = P(("dp", "tensor"), None)
    return jax.shard_map(
        shards,
        mesh=mesh,
        in_specs=(
            token_spec,
            token_spec,
            P("dp", None),
            P(),
            P(None, "tensor"),
            P("tensor", None),
            P(),
            P(None, "tensor"),
            P(None, "tensor"),
            P("tensor", None),
            token_spec,
        ),
        out_specs=(
            token_spec,
            token_spec,
            token_spec,
            P(),
            P("dp", "tensor"),
            P("tensor", "dp"),
            P(),
            P("dp", "tensor"),
            P("dp", "tensor"),
            P("tensor", "dp"),
            P(),
            P(),
        ),
        check_vma=False,
    )
```

```python
import functools
import math

import jax
import jax.numpy as jnp
import numpy as np
from jax import lax
from jax.experimental import pallas as pl
from jax.experimental.pallas import tpu as pltpu
from jax.sharding import PartitionSpec as P

HD = 64
HALF = HD // 2
LANES = 128
GROUP = LANES // HALF
EPS = 1e-06
NEG = -1e30
VMEM = 60 << 20
SMALL = pl.CostEstimate(flops=1, bytes_accessed=1, transcendentals=0)
LARGE = pl.CostEstimate(flops=10**11, bytes_accessed=1, transcendentals=0)
f32 = jnp.float32
bf16 = jnp.bfloat16


def rope_tables(length):
    inverse = jnp.exp(-math.log(10000.0) * jnp.arange(HALF, dtype=f32) / HALF)
    angles = jnp.arange(length, dtype=f32)[:, None] * inverse[None, :]
    tile = lambda t: jnp.concatenate([t] * GROUP, axis=1)
    return tile(jnp.cos(angles)), tile(jnp.sin(angles))


def column_order(heads):
    value_width = max(LANES, heads * HD)
    order = np.full((4 * LANES + value_width,), -1, np.int32)
    for h in range(heads):
        for part in range(2):
            for half in range(2):
                at = (2 * part + half) * LANES + h * HALF
                src = h * 3 * HD + part * HD + half * HALF
                order[at : at + HALF] = np.arange(src, src + HALF)
        order[4 * LANES + h * HD : 4 * LANES + (h + 1) * HD] = np.arange(
            h * 3 * HD + 2 * HD, (h + 1) * 3 * HD
        )
    return order


def column_selector(heads):
    order = jnp.asarray(column_order(heads))
    rows = jnp.arange(3 * heads * HD, dtype=jnp.int32)
    return (rows[:, None] == order[None, :]).astype(bf16)


def dot_nt(a, b):
    return lax.dot_general(a, b, (((1,), (1,)), ((), ())), preferred_element_type=f32)


def dot_tn(a, b):
    return lax.dot_general(a, b, (((0,), (0,)), ((), ())), preferred_element_type=f32)


def dot_nn(a, b):
    return jnp.dot(a, b, preferred_element_type=f32)


def anywhere():
    return pl.BlockSpec(memory_space=pl.ANY)


def project_kernel(heads, placed, info_ref, *refs):
    count = len(placed)
    n = len({j for j, _ in placed})
    pieces, values = refs[:count], refs[count : count + n]
    w_ref, cos_ref, sin_ref, lim_ref = refs[count + n : count + n + 4]
    q_ref, k_ref, v_ref, sq_ref, x_ref, fv_ref, sem = refs[count + n + 4 :]
    at = pl.program_id(0)
    block = q_ref.shape[0]
    copies = []
    for i, (ref, (j, first)) in enumerate(zip(pieces, placed)):
        into = x_ref.at[j, first : first + ref.shape[0]]
        copies.append((j, pltpu.make_async_copy(ref, into, sem.at[i])))
    for j, ref in enumerate(values):
        copies.append((j, pltpu.make_async_copy(ref, fv_ref.at[j], sem.at[count + j])))

    @pl.when(at == 0)
    def _():
        sq_ref[...] = jnp.zeros_like(sq_ref)
        for _, copy in copies:
            copy.start()

    for j in range(n):

        @pl.when(at == j)
        def _():
            for owner, copy in copies:
                if owner == j:
                    copy.wait()

    acc = dot_nn(x_ref[at], w_ref[...])
    c, s = cos_ref[...], sin_ref[...]
    lane = lax.broadcasted_iota(jnp.int32, (block, LANES), 1)
    place = (info_ref[0] ^ at) * block + lax.broadcasted_iota(jnp.int32, (block, LANES), 0)
    inside = (place >= lim_ref[0:1, :]) & (place < lim_ref[1:2, :])
    doc_lane = (lane >= HD) & (lane < HD + 8)
    q_extra = jnp.where(doc_lane & jnp.logical_not(inside), NEG, 0.0)
    k_extra = jnp.where(inside, 1.0, jnp.where((lane >= HD + 8) & (lane < HD + 11), 1.0, 0.0))
    for ref, base, extra, scale in ((q_ref, 0, q_extra, HD**-0.5), (k_ref, 2, k_extra, 1.0)):
        u1 = acc[:, base * LANES : (base + 1) * LANES]
        u2 = acc[:, (base + 1) * LANES : (base + 2) * LANES]
        r1 = (u1 * c - u2 * s) * scale
        r2 = (u1 * s + u2 * c) * scale
        for h in range(heads):
            a = r1 if h == 0 else pltpu.roll(r1, LANES - HALF * h, 1)
            b = r2 if h == 1 else pltpu.roll(r2, (LANES + HALF - HALF * h) % LANES, 1)
            both = jnp.where(lane < HALF, a, jnp.where(lane < HD, b, extra))
            ref[:, h * LANES : (h + 1) * LANES] = both.astype(bf16)
    first = fv_ref[at].astype(f32)
    mixed = 0.5 * acc[:, 4 * LANES :] + 0.5 * first
    sq_ref[0:1, :] += jnp.sum(mixed * mixed, axis=0, keepdims=True)
    sq_ref[1:2, :] += jnp.sum(first * first, axis=0, keepdims=True)
    for h in range(heads):
        t = (h // 2) * LANES
        own = (lane < HD) if h % 2 == 0 else (lane >= HD)
        v_ref[:, h * LANES : (h + 1) * LANES] = jnp.where(
            own, mixed[:, t : t + LANES], 1.0
        ).astype(bf16)


def project(heads, info, parts, values, w, cos, sin, limits, rows):
    n = len(values)
    length = rows * n
    depth = parts[0][0].shape[1]
    width = values[0].shape[1]
    row = lambda i, info: (info[0] ^ i, 0)
    whole = lambda i, info: (0, 0)
    ext = heads * LANES
    placed = tuple((j, first) for _, j, first in parts)
    return pl.pallas_call(
        functools.partial(project_kernel, heads, placed),
        name="project",
        grid_spec=pltpu.PrefetchScalarGridSpec(
            num_scalar_prefetch=1,
            grid=(n,),
            in_specs=[anywhere()] * (len(parts) + n)
            + [
                pl.BlockSpec(w.shape, whole),
                pl.BlockSpec((rows, LANES), row),
                pl.BlockSpec((rows, LANES), row),
                pl.BlockSpec((8, LANES), whole),
            ],
            out_specs=[
                pl.BlockSpec((rows, ext), row),
                pl.BlockSpec((rows, ext), row),
                pl.BlockSpec((rows, ext), row),
                pl.BlockSpec((8, width), whole),
            ],
            scratch_shapes=[
                pltpu.VMEM((n, rows, depth), bf16),
                pltpu.VMEM((n, rows, width), bf16),
                pltpu.SemaphoreType.DMA((len(parts) + n,)),
            ],
        ),
        out_shape=[jax.ShapeDtypeStruct((length, ext), bf16)] * 3
        + [jax.ShapeDtypeStruct((8, width), f32)],
        compiler_params=pltpu.CompilerParams(vmem_limit_bytes=VMEM),
        cost_estimate=SMALL,
    )(info, *[p for p, _, _ in parts], *values, w, cos, sin, limits)


def pieces(x):
    hi = x.astype(bf16).astype(f32)
    mid = (x - hi).astype(bf16).astype(f32)
    return hi, mid, x - hi - mid


def attend_kernel(
    heads, offset, bk, info_ref, begin_ref, q_ref, k_ref, v_ref, o_ref, qo_ref, m_ref, acc_ref
):
    bq = q_ref.shape[0]
    at = info_ref[0] ^ offset
    lane = lax.broadcasted_iota(jnp.int32, (bq, LANES), 1)
    r = lax.broadcasted_iota(jnp.int32, (bq, bk), 0)
    c = lax.broadcasted_iota(jnp.int32, (bq, bk), 1)
    col = [slice(h * LANES, (h + 1) * LANES) for h in range(heads)]
    spread = lambda m: jnp.concatenate([m] * (bk // LANES), axis=1)

    def visit(kb, mask, first):
        there = pl.ds(pl.multiple_of(kb * bk, bk), bk)
        for h in range(heads):
            s = dot_nt(q_ref[:, col[h]], k_ref[there, col[h]])
            if mask is not None:
                s = jnp.where(mask, s, NEG)
            new = jnp.broadcast_to(jnp.max(s, axis=1, keepdims=True), (bq, LANES))
            if not first:
                old = m_ref[:, col[h]]
                new = jnp.maximum(old, new)
            p = jnp.exp(s - spread(new)).astype(bf16)
            part = dot_nn(p, v_ref[there, col[h]])
            m_ref[:, col[h]] = new
            acc_ref[:, col[h]] = part if first else acc_ref[:, col[h]] * jnp.exp(old - new) + part

    for d in range(bq // bk):
        visit(at * (bq // bk) + d, c + d * bk <= r, d == 0)

    def step(kb, carry):
        visit(kb, None, False)
        return carry

    lax.fori_loop(begin_ref[at * (bq // bk)], at * (bq // bk), step, 0)
    low = lane < HD
    for t in range((heads + 1) // 2):
        a = acc_ref[:, col[2 * t]]
        b = acc_ref[:, col[2 * t + 1]] if 2 * t + 1 < heads else a
        total = pltpu.roll(jnp.where(low, b, a), HD, 1)
        result = jnp.where(low, a, b) / total
        if 2 * t + 1 >= heads:
            result = jnp.where(low, result, 0.0)
        o_ref[:, t * LANES : (t + 1) * LANES] = result.astype(bf16)
    for h in range(heads):
        a = acc_ref[:, col[h]]
        total = a if h % 2 == 0 else pltpu.roll(a, HD, 1)
        hi, mid, lo = pieces(-(m_ref[:, col[h]] + jnp.log(jnp.where(low, 1.0, total))))
        extra = jnp.where(
            lane == HD + 8, hi, jnp.where(lane == HD + 9, mid, jnp.where(lane == HD + 10, lo, 0.0))
        )
        fill = (lane >= HD + 8) & (lane < HD + 11)
        qo_ref[:, col[h]] = jnp.where(fill, extra, q_ref[:, col[h]].astype(f32)).astype(bf16)


def attend(heads, info, offset, q, k, v, begins, block, rows):
    length = q.shape[0]
    ext = heads * LANES
    width = max(LANES, heads * HD)
    whole = lambda i, info, b: (0, 0)
    return pl.pallas_call(
        functools.partial(attend_kernel, heads, offset, block),
        name="attend",
        grid_spec=pltpu.PrefetchScalarGridSpec(
            num_scalar_prefetch=2,
            grid=(1,),
            in_specs=[
                pl.BlockSpec((rows, ext), lambda i, info, b: (info[0] ^ offset, 0)),
                pl.BlockSpec((length, ext), whole),
                pl.BlockSpec((length, ext), whole),
            ],
            out_specs=[pl.BlockSpec((rows, width), whole), pl.BlockSpec((rows, ext), whole)],
            scratch_shapes=[pltpu.VMEM((rows, ext), f32), pltpu.VMEM((rows, ext), f32)],
        ),
        out_shape=[
            jax.ShapeDtypeStruct((rows, width), bf16),
            jax.ShapeDtypeStruct((rows, ext), bf16),
        ],
        compiler_params=pltpu.CompilerParams(vmem_limit_bytes=VMEM),
        cost_estimate=SMALL,
    )(info, begins, q, k, v)


def attend_back_kernel(heads, block, n, info_ref, begin_ref, *refs):
    q_parts, do_parts, o_parts = refs[:n], refs[n : 2 * n], refs[2 * n : 3 * n]
    k_ref, v_ref, cos_ref, sin_ref, g_ref = refs[3 * n : 3 * n + 5]
    sends = refs[3 * n + 5 : 4 * n + 5]
    q_all, do_all, o_all, dk_ref, dv_ref, dq_ref, de_ref, sem = refs[4 * n + 5 :]
    at = pl.program_id(0)
    rows = q_parts[0].shape[0]

    def moves(pairs):
        copies = []
        for i, (make, j) in enumerate(pairs):
            place = pl.ds(pl.multiple_of((info_ref[0] ^ j) * rows, rows), rows)
            copies.append(make(place, sem.at[i]))
        for copy in copies:
            copy.start()
        for copy in copies:
            copy.wait()

    @pl.when(at == 0)
    def _():
        moves(
            [
                (functools.partial(lambda src, dst, p, s: pltpu.make_async_copy(src, dst.at[p], s), part, whole), j)
                for parts, whole in ((q_parts, q_all), (do_parts, do_all), (o_parts, o_all))
                for j, part in enumerate(parts)
            ]
        )

    lane = lax.broadcasted_iota(jnp.int32, (block, LANES), 1)
    r = lax.broadcasted_iota(jnp.int32, (block, block), 0)
    c = lax.broadcasted_iota(jnp.int32, (block, block), 1)
    causal = r <= c
    low = lane < HD
    here = pl.ds(pl.multiple_of(at * block, block), block)
    col = [slice(h * LANES, (h + 1) * LANES) for h in range(heads)]

    for h in range(heads):
        t = slice((h // 2) * LANES, (h // 2 + 1) * LANES)
        own = low if h % 2 == 0 else jnp.logical_not(low)
        grad = do_all[here, t].astype(f32)
        product = grad * o_all[here, t].astype(f32)
        centre = jnp.sum(jnp.where(own, product, 0.0), axis=1, keepdims=True)
        hi, mid, lo = pieces(-jnp.broadcast_to(centre, (block, LANES)))
        spot = lane - (HD if h % 2 == 0 else 0)
        extra = jnp.where(spot == 0, hi, jnp.where(spot == 1, mid, jnp.where(spot == 2, lo, 0.0)))
        de_ref[:, col[h]] = jnp.where(own, grad, extra).astype(bf16)

    def visit(there, mask, first):
        st = [dot_nt(k_ref[there, c_], q_all[here, c_]) for c_ in col]
        dpt = [dot_nt(v_ref[there, c_], de_ref[:, c_]) for c_ in col]
        p = [jnp.exp(s) for s in st]
        if mask is not None:
            p = [jnp.where(mask, x, 0.0) for x in p]
        ds = [(x * y).astype(bf16) for x, y in zip(p, dpt)]
        p = [x.astype(bf16) for x in p]
        for h, c_ in enumerate(col):
            dv = dot_nn(p[h], de_ref[:, c_])
            dk = dot_nn(ds[h], q_all[here, c_])
            dq = dot_tn(ds[h], k_ref[there, c_])
            if first:
                dv_ref[there, c_] = dv
                dk_ref[there, c_] = dk
                dq_ref[:, c_] = dq
            else:
                dv_ref[there, c_] += dv
                dk_ref[there, c_] += dk
                dq_ref[:, c_] += dq

    visit(here, causal, True)

    def step(kb, carry):
        visit(pl.ds(pl.multiple_of(kb * block, block), block), None, False)
        return carry

    lax.fori_loop(begin_ref[at], at, step, 0)

    def turn_back(ref, rows, scale):
        u1 = u2 = None
        quarter = lane // HALF
        for h in range(heads):
            u = ref[rows, col[h]]
            a = u if h == 0 else pltpu.roll(u, HALF * h, 1)
            b = u if h == 1 else pltpu.roll(u, (LANES + HALF * h - HALF) % LANES, 1)
            u1 = a if h == 0 else jnp.where(quarter == h, a, u1)
            u2 = b if h == 0 else jnp.where(quarter == h, b, u2)
        if heads < GROUP:
            u1 = jnp.where(quarter < heads, u1, 0.0)
            u2 = jnp.where(quarter < heads, u2, 0.0)
        u1, u2 = u1 * scale, u2 * scale
        cs, sn = cos_ref[rows, :], sin_ref[rows, :]
        return (u1 * cs + u2 * sn).astype(bf16), (u2 * cs - u1 * sn).astype(bf16)

    def finish_block(i, carry):
        rows = pl.ds(pl.multiple_of(i * block, block), block)
        d1, d2 = turn_back(dk_ref, rows, 1.0)
        g_ref[rows, 2 * LANES : 3 * LANES] = d1
        g_ref[rows, 3 * LANES : 4 * LANES] = d2
        for t in range((heads + 1) // 2):
            a = dv_ref[rows, col[2 * t]]
            b = dv_ref[rows, col[2 * t + 1]] if 2 * t + 1 < heads else jnp.zeros_like(a)
            d_mix = jnp.where(low, a, b).astype(bf16)
            g_ref[rows, (4 + t) * LANES : (5 + t) * LANES] = (d_mix.astype(f32) * 0.5).astype(bf16)
        return carry

    u1 = u2 = None
    quarter = lane // HALF
    for h in range(heads):
        u = dq_ref[:, col[h]]
        a = u if h == 0 else pltpu.roll(u, HALF * h, 1)
        b = u if h == 1 else pltpu.roll(u, (LANES + HALF * h - HALF) % LANES, 1)
        u1 = a if h == 0 else jnp.where(quarter == h, a, u1)
        u2 = b if h == 0 else jnp.where(quarter == h, b, u2)
    if heads < GROUP:
        u1 = jnp.where(quarter < heads, u1, 0.0)
        u2 = jnp.where(quarter < heads, u2, 0.0)
    u1, u2 = u1 * HD**-0.5, u2 * HD**-0.5
    cs, sn = cos_ref[here, :], sin_ref[here, :]
    g_ref[here, 0:LANES] = (u1 * cs + u2 * sn).astype(bf16)
    g_ref[here, LANES : 2 * LANES] = (u2 * cs - u1 * sn).astype(bf16)

    @pl.when(at == pl.num_programs(0) - 1)
    def _():
        lax.fori_loop(0, pl.num_programs(0), finish_block, 0)
        moves(
            [
                (functools.partial(lambda dst, p, s: pltpu.make_async_copy(g_ref.at[p], dst, s), dst), j)
                for j, dst in enumerate(sends)
            ]
        )


def attend_back(heads, info, q_parts, k, v, do_parts, o_parts, cos, sin, begins, block):
    n = len(q_parts)
    rows = q_parts[0].shape[0]
    length = n * rows
    ext = heads * LANES
    width = o_parts[0].shape[1]
    whole = lambda i, info, b: (0, 0)
    anywhere = pl.BlockSpec(memory_space=pl.ANY)
    columns = 4 * LANES + width
    return pl.pallas_call(
        functools.partial(attend_back_kernel, heads, block, n),
        name="attend_back",
        grid_spec=pltpu.PrefetchScalarGridSpec(
            num_scalar_prefetch=2,
            grid=(length // block,),
            in_specs=[anywhere] * (3 * n)
            + [
                pl.BlockSpec((length, ext), whole),
                pl.BlockSpec((length, ext), whole),
                pl.BlockSpec((length, LANES), whole),
                pl.BlockSpec((length, LANES), whole),
            ],
            out_specs=[pl.BlockSpec((length, columns), whole)] + [anywhere] * n,
            scratch_shapes=[
                pltpu.VMEM((length, ext), bf16),
                pltpu.VMEM((length, width), bf16),
                pltpu.VMEM((length, width), bf16),
                pltpu.VMEM((length, ext), f32),
                pltpu.VMEM((length, ext), f32),
                pltpu.VMEM((block, ext), f32),
                pltpu.VMEM((block, ext), bf16),
                pltpu.SemaphoreType.DMA((3 * n,)),
            ],
        ),
        out_shape=[jax.ShapeDtypeStruct((length, columns), bf16)]
        + [jax.ShapeDtypeStruct((rows, columns), bf16)] * n,
        compiler_params=pltpu.CompilerParams(vmem_limit_bytes=VMEM),
        cost_estimate=LARGE,
    )(info, begins, *q_parts, *do_parts, *o_parts, k, v, cos, sin)


def split_axis(n):
    low = 1 << ((n.bit_length() - 1) // 2)
    return n // low, low


def swap(axis, value, offset):
    n = lax.axis_size(axis)
    return lax.ppermute(value, axis, [(i, i ^ offset) for i in range(n)])


def gather_rows(value, n):
    high, low = split_axis(n)
    rows = value.shape[0]
    half = rows // 2
    parts = {0: value}
    for b in range(1, low):
        parts[b] = swap("tensor", value, b)
    for a in range(1, high):
        parts[a * low] = swap("tensor", value, a * low)
    listed = [(parts[j], j, 0) for j in sorted(parts)]
    for a in range(1, high):
        for b in range(1, low):
            j = a * low + b
            listed.append((swap("tensor", parts[b][:half], a * low), j, 0))
            listed.append((swap("tensor", parts[a * low][half:], b), j, half))
    return listed


def after(value, *others):
    return lax.optimization_barrier((value,) + others)[0]


def add_up(first, *others):
    total = first.astype(f32)
    for other in others:
        total = total + other.astype(f32)
    return total


def over_replicas(value):
    if value.shape[1] % LANES == 0:
        return lax.all_gather(value, "dp", axis=0)
    return lax.all_gather(value, "dp", axis=1, tiled=True)


def halve_over_z(parts, z, step, hold):
    pairs = parts.reshape((-1, 2) + parts.shape[1:])
    side = (z // step) % 2
    pick = lambda which: lax.dynamic_index_in_dim(pairs, which, 1, keepdims=False)
    parts = add_up(pick(side), hold(swap("dp", pick(1 - side), 2 * step)))
    return parts.astype(bf16) if parts.shape[0] > 1 else parts


def all_sum(value, axis):
    n = lax.axis_size(axis)
    step = 1
    while step < n:
        value = value + swap(axis, value, step)
        step *= 2
    return value


def norm_kernel(x_ref, gain_ref, o_ref):
    x = x_ref[...].astype(f32)
    inverse = lax.rsqrt(jnp.mean(x * x, axis=-1, keepdims=True) + EPS)
    o_ref[...] = (x * inverse * gain_ref[...]).astype(bf16)


def norm_rows(x, gain):
    rows, depth = x.shape
    block = min(rows, 128)
    return pl.pallas_call(
        norm_kernel,
        name="norm_rows",
        grid=(rows // block,),
        in_specs=[
            pl.BlockSpec((block, depth), lambda i: (i, 0)),
            pl.BlockSpec((1, depth), lambda i: (0, 0)),
        ],
        out_specs=pl.BlockSpec((block, depth), lambda i: (i, 0)),
        out_shape=jax.ShapeDtypeStruct((rows, depth), bf16),
        compiler_params=pltpu.CompilerParams(vmem_limit_bytes=VMEM),
        cost_estimate=SMALL,
    )(x, gain)


def branch_kernel(n, parts, info_ref, *refs):
    att = refs[:n]
    slices_ref, tok_ref, gain_ref, mid_ref, h_ref, w_ref = refs[n : n + 6]
    h_parts = refs[n + 6 : n + 6 + parts]
    all_ref, sem, w_sem = refs[n + 6 + parts :]
    at = pl.program_id(0)
    size = tok_ref.shape[0]
    width = att[0].shape[1]

    @pl.when(at == 0)
    def _():
        copies = [
            pltpu.make_async_copy(
                att[j], all_ref.at[:, j * width : (j + 1) * width], sem.at[j]
            )
            for j in range(n)
        ]
        if len(slices_ref.shape) == 3:
            lanes = slices_ref.shape[2]
            copies += [
                pltpu.make_async_copy(
                    slices_ref.at[d], w_ref.at[:, d * lanes : (d + 1) * lanes], w_sem.at[d]
                )
                for d in range(slices_ref.shape[0])
            ]
        else:
            copies.append(pltpu.make_async_copy(slices_ref, w_ref, w_sem.at[0]))
        for copy in copies:
            copy.start()
        for copy in copies:
            copy.wait()

    here = pl.ds(pl.multiple_of(at * size, size), size)
    x = tok_ref[...].astype(f32) + dot_nn(all_ref[here, :], w_ref[...])
    mid_ref[...] = x
    inverse = lax.rsqrt(jnp.mean(x * x, axis=-1, keepdims=True) + EPS)
    h = (x * inverse * gain_ref[...]).astype(bf16)
    h_ref[...] = h
    for p in range(parts):

        @pl.when(at == p)
        def _():
            h_parts[p][...] = h


def branch(info, att, w_slices, tokens, gain, parts):
    n = len(att)
    rows, width = att[0].shape
    depth = tokens.shape[1]
    size = rows // parts
    whole = lambda i, info: (0, 0)
    row = lambda i, info: (i, 0)
    count = w_slices.shape[0] if w_slices.ndim == 3 else 1
    return pl.pallas_call(
        functools.partial(branch_kernel, n, parts),
        name="branch",
        grid_spec=pltpu.PrefetchScalarGridSpec(
            num_scalar_prefetch=1,
            grid=(parts,),
            in_specs=[anywhere()] * (n + 1)
            + [pl.BlockSpec((size, depth), row), pl.BlockSpec((1, depth), whole)],
            out_specs=[pl.BlockSpec((size, depth), row)] * 2
            + [pl.BlockSpec((n * width, depth), whole)]
            + [pl.BlockSpec((size, depth), whole)] * parts,
            scratch_shapes=[
                pltpu.VMEM((rows, n * width), bf16),
                pltpu.SemaphoreType.DMA((n,)),
                pltpu.SemaphoreType.DMA((count,)),
            ],
        ),
        out_shape=[
            jax.ShapeDtypeStruct((rows, depth), f32),
            jax.ShapeDtypeStruct((rows, depth), bf16),
            jax.ShapeDtypeStruct((n * width, depth), bf16),
        ]
        + [jax.ShapeDtypeStruct((size, depth), bf16)] * parts,
        compiler_params=pltpu.CompilerParams(vmem_limit_bytes=VMEM),
        cost_estimate=SMALL,
    )(info, *att, w_slices, tokens, gain)


def feed_kernel(shards_in, shared, send, act_first, info_ref, h_ref, g_ref, *refs):
    count = sum(shards_in)
    weights, refs = refs[:count], refs[count + shared :]
    out_ref, dh_ref, act_out, w_ref, sem, act_ref, act_sem = refs[:7]
    out_acc, dh_acc = refs[7:] if send else (out_ref, dh_ref)
    high, rows_w, depth = w_ref.shape
    units = rows_w // 3
    copies, at, used = [], 0, 0
    for a, pieces_in in enumerate(shards_in):
        groups = []
        for m in range(3):
            span = pl.ds(m * units, units)
            ref = weights[at + m] if pieces_in == 3 else weights[at]
            if pieces_in == 3:
                moves = [(ref, w_ref.at[a, span])]
            elif len(ref.shape) == 3:
                size = ref.shape[2]
                moves = [
                    (ref.at[d, span], w_ref.at[a, span, d * size : (d + 1) * size])
                    for d in range(ref.shape[0])
                ]
            else:
                moves = [(ref.at[span], w_ref.at[a, span])]
            groups.append(
                [
                    pltpu.make_async_copy(src, dst, sem.at[used + i])
                    for i, (src, dst) in enumerate(moves)
                ]
            )
            used += len(moves)
        at += pieces_in
        copies.append(groups)
    for groups in copies:
        for group in groups:
            for copy in group:
                copy.start()

    rows = h_ref.shape[0]
    out_acc[...] = jnp.zeros_like(out_acc)
    dh_acc[...] = jnp.zeros_like(dh_acc)

    def leave(a):
        to = act_out.at[a, :, act_first : act_first + rows]
        return pltpu.make_async_copy(act_ref.at[a], to, act_sem.at[a])

    def shard(a, carry):
        def weight(m):
            for k in range(high):

                @pl.when(a == k)
                def _():
                    for copy in copies[k][m]:
                        copy.wait()

            return w_ref[a, m * units : (m + 1) * units, :]

        gate = dot_nt(h_ref[...], weight(0))
        up = dot_nt(h_ref[...], weight(1))
        back = dot_nt(g_ref[...], weight(2))
        s = 0.5 * jnp.tanh(0.5 * gate) + 0.5
        gs = gate * s
        hidden = (gs * up).astype(bf16)
        d_up = (back * gs).astype(bf16)
        d_gate = (back * up * (s + gs * (1.0 - s))).astype(bf16)
        act_ref[a, 0] = d_gate
        act_ref[a, 1] = d_up
        act_ref[a, 2] = hidden
        leave(a).start()
        gate_w, up_w, down_w = (w_ref[a, m * units : (m + 1) * units, :] for m in range(3))
        dh_acc[...] += dot_nn(d_gate, gate_w) + dot_nn(d_up, up_w)
        out_acc[...] += dot_nn(hidden, down_w)
        return carry

    lax.fori_loop(0, high, shard, 0)
    if send:
        out_ref[...] = out_acc[...].astype(bf16)
        dh_ref[...] = dh_acc[...].astype(bf16)
    for a in range(high):
        leave(a).wait()


def feed(info, h, g, g_first, weights, act_first, act_rows, shared, out_first, out_rows, send):
    rows, depth = h.shape
    high = len(weights)
    flat = [w for shard in weights for w in shard]
    units = weights[0][0].shape[0] if len(weights[0]) == 3 else weights[0][0].shape[-2] // 3
    block = rows
    at, out_at = g_first // block, out_first // block
    row = lambda i, info: (i, 0)
    kind = bf16 if send else f32
    moves = sum(
        3 if len(shard) == 3 else 3 * (shard[0].shape[0] if shard[0].ndim == 3 else 1)
        for shard in weights
    )
    base = 3 + len(flat)
    aliases = {} if not shared else {base: 2} if len(shared) == 1 else {base: 0, base + 1: 2}
    return pl.pallas_call(
        functools.partial(
            feed_kernel, tuple(len(shard) for shard in weights), len(shared), send, act_first
        ),
        name="feed",
        grid_spec=pltpu.PrefetchScalarGridSpec(
            num_scalar_prefetch=1,
            grid=(1,),
            in_specs=[
                pl.BlockSpec((block, depth), row),
                pl.BlockSpec((block, depth), lambda i, info: (at, 0)),
            ]
            + [anywhere()] * (len(flat) + len(shared)),
            out_specs=[
                pl.BlockSpec((block, depth), lambda i, info: (out_at, 0)),
                pl.BlockSpec((block, depth), row),
                anywhere(),
            ],
            scratch_shapes=[
                pltpu.VMEM((high, 3 * units, depth), bf16),
                pltpu.SemaphoreType.DMA((moves,)),
                pltpu.VMEM((high, 3, block, units), bf16),
                pltpu.SemaphoreType.DMA((high,)),
            ]
            + ([pltpu.VMEM((block, depth), f32)] * 2 if send else []),
        ),
        out_shape=[
            jax.ShapeDtypeStruct((out_rows, depth), kind),
            jax.ShapeDtypeStruct((rows, depth), kind),
            jax.ShapeDtypeStruct((high, 3, act_rows, units), bf16),
        ],
        input_output_aliases=aliases,
        compiler_params=pltpu.CompilerParams(vmem_limit_bytes=VMEM),
        cost_estimate=SMALL,
    )(info, h, g, *flat, *shared)


def feed_grad_kernel(h_rows, g_rows, members, info_ref, list_ref, *refs):
    h, g = refs[: len(h_rows)], refs[len(h_rows) : len(h_rows) + len(g_rows)]
    act_ref, keep_ref, send_ref, h_ref, g_ref, h_sem, g_sem = refs[len(h_rows) + len(g_rows) :]
    core = info_ref[1]
    at = pl.program_id(0)
    depth = h_ref.shape[1]
    half = depth // 2
    size = half // members
    aligned = size % LANES == 0

    def copies(parts, rows, whole, sem):
        out = []
        for ref, first in zip(parts, rows):
            here = slice(first, first + ref.shape[0])
            if not aligned:
                out.append(pltpu.make_async_copy(ref, whole.at[here], sem.at[len(out)]))
                continue
            for side in range(2):
                for z in range(members):
                    lanes = pl.ds(pl.multiple_of((2 * z + (core ^ side)) * size, size), size)
                    to = slice(side * half + z * size, side * half + (z + 1) * size)
                    out.append(
                        pltpu.make_async_copy(ref.at[:, lanes], whole.at[here, to], sem.at[len(out)])
                    )
        return out

    h_copies, g_copies = copies(h, h_rows, h_ref, h_sem), copies(g, g_rows, g_ref, g_sem)

    @pl.when(at == 0)
    def _():
        for copy in h_copies + g_copies:
            copy.start()
        for copy in h_copies:
            copy.wait()

    @pl.when(at == 1)
    def _():
        for copy in g_copies:
            copy.wait()

    def work(source):
        if aligned:
            for ref, side in ((keep_ref, 0), (send_ref, 1)):
                g_side = dot_tn(act_ref[0, 0], source[:, side * half : (side + 1) * half])
                for z in range(members):
                    ref[0, z] = g_side[:, z * size : (z + 1) * size].astype(bf16)
            return
        g_all = dot_tn(act_ref[0, 0], source[...])
        for z in range(members):
            even = g_all[:, 2 * z * size : (2 * z + 1) * size]
            odd = g_all[:, (2 * z + 1) * size : (2 * z + 2) * size]
            keep_ref[0, z] = jnp.where(core == 0, even, odd).astype(bf16)
            send_ref[0, z] = jnp.where(core == 0, odd, even).astype(bf16)

    @pl.when(list_ref[at, 1] < 2)
    def _():
        work(h_ref)

    @pl.when(list_ref[at, 1] == 2)
    def _():
        work(g_ref)


def feed_grads(info, h, h_rows, g, g_rows, act, wanted, members):
    depth = h[0].shape[1]
    _, _, rows, units = act.shape
    size = depth // (2 * members)
    count = len(wanted)
    out = jax.ShapeDtypeStruct((count, members, units, size), bf16)
    return pl.pallas_call(
        functools.partial(feed_grad_kernel, tuple(h_rows), tuple(g_rows), members),
        name="feed_grads",
        grid_spec=pltpu.PrefetchScalarGridSpec(
            num_scalar_prefetch=2,
            grid=(count,),
            in_specs=[anywhere()] * (len(h) + len(g))
            + [pl.BlockSpec((1, 1, rows, units), lambda i, info, w: (w[i, 0], w[i, 1], 0, 0))],
            out_specs=[pl.BlockSpec((1, members, units, size), lambda i, info, w: (i, 0, 0, 0))]
            * 2,
            scratch_shapes=[
                pltpu.VMEM((rows, depth), bf16),
                pltpu.VMEM((rows, depth), bf16),
                pltpu.SemaphoreType.DMA((2 * members * len(h),)),
                pltpu.SemaphoreType.DMA((2 * members * len(g),)),
            ],
        ),
        out_shape=[out, out],
        compiler_params=pltpu.CompilerParams(vmem_limit_bytes=VMEM),
        cost_estimate=SMALL,
    )(info, jnp.asarray(wanted, jnp.int32), *h, *g, act)


def branch_back_kernel(n, parts, info_ref, dh_ref, mid_ref, g_ref, gain_ref, w_ref, *refs):
    far, refs = refs[:parts], refs[parts:]
    dm_ref, db_ref, gg_ref = refs[:3]
    da = refs[3:]
    at = pl.program_id(0)
    width = da[0].shape[1]
    x = mid_ref[...]
    inverse = lax.rsqrt(jnp.mean(x * x, axis=-1, keepdims=True) + EPS)
    unit = x * inverse
    received = far[0][...]
    for p in range(1, parts):
        received = jnp.where(at == p, far[p][...], received)
    cotangent = dh_ref[...] + received.astype(f32)
    e = cotangent * gain_ref[...]
    inner = jnp.mean(e * unit, axis=-1, keepdims=True)
    d_mid = g_ref[...].astype(f32) + inverse * (e - unit * inner)
    share = jnp.sum(cotangent * unit, axis=0, keepdims=True)

    @pl.when(at == 0)
    def _():
        gg_ref[...] = jnp.zeros_like(gg_ref)

    gg_ref[...] += share
    dm_ref[...] = d_mid
    rounded = d_mid.astype(bf16)
    db_ref[...] = rounded
    for j in range(n):
        da[j][...] = dot_nt(rounded, w_ref[j * width : (j + 1) * width, :]).astype(bf16)


def branch_back(info, d_h, d_far, middle, g, gain, w_all, width):
    n = w_all.shape[0] // width
    parts = len(d_far)
    rows, depth = middle.shape
    size = rows // parts
    whole = lambda i, info: (0, 0)
    row = lambda i, info: (i, 0)
    part = pl.BlockSpec((size, depth), row)
    return pl.pallas_call(
        functools.partial(branch_back_kernel, n, parts),
        name="branch_back",
        grid_spec=pltpu.PrefetchScalarGridSpec(
            num_scalar_prefetch=1,
            grid=(parts,),
            in_specs=[part, part, part]
            + [pl.BlockSpec(gain.shape, whole), pl.BlockSpec(w_all.shape, whole)]
            + [pl.BlockSpec((size, depth), whole)] * parts,
            out_specs=[part, part, pl.BlockSpec((1, depth), whole)]
            + [pl.BlockSpec((size, width), row)] * n,
        ),
        out_shape=[
            jax.ShapeDtypeStruct((rows, depth), f32),
            jax.ShapeDtypeStruct((rows, depth), bf16),
            jax.ShapeDtypeStruct((1, depth), f32),
        ]
        + [jax.ShapeDtypeStruct((rows, width), bf16)] * n,
        compiler_params=pltpu.CompilerParams(vmem_limit_bytes=VMEM),
        cost_estimate=SMALL,
    )(info, d_h, middle, g, gain, w_all, *d_far)


def out_grad_kernel(n, info_ref, *refs):
    db_ref = refs[0]
    att = refs[1 : 1 + n]
    o_ref = refs[1 + n]
    for j in range(n):
        o_ref[info_ref[0] ^ j] = dot_tn(db_ref[...], att[j][...]).astype(bf16)


def out_grads(info, d_branch, att):
    n = len(att)
    rows, depth = d_branch.shape
    width = att[0].shape[1]
    whole = lambda i, info: (0, 0)
    return pl.pallas_call(
        functools.partial(out_grad_kernel, n),
        name="out_grads",
        grid_spec=pltpu.PrefetchScalarGridSpec(
            num_scalar_prefetch=1,
            grid=(1,),
            in_specs=[pl.BlockSpec(d_branch.shape, whole)]
            + [pl.BlockSpec(a.shape, whole) for a in att],
            out_specs=pl.BlockSpec((n, depth, width), lambda i, info: (0, 0, 0)),
        ),
        out_shape=jax.ShapeDtypeStruct((n, depth, width), bf16),
        compiler_params=pltpu.CompilerParams(vmem_limit_bytes=VMEM),
        cost_estimate=SMALL,
    )(info, d_branch, *att)


def qkv_grad_kernel(rows, placed, info_ref, *refs):
    count = len(placed)
    pieces = refs[:count]
    d_ref, w_ref, sel_ref, out_ref, o_ref, share_ref, x_ref, sem = refs[count:]
    columns = sel_ref.shape[0]
    at = pl.program_id(0)
    block = o_ref.shape[0]

    @pl.when(at == 0)
    def _():
        copies = []
        for i, (ref, (j, first)) in enumerate(zip(pieces, placed)):
            size = ref.shape[0]
            place = pl.ds(pl.multiple_of((info_ref[0] ^ j) * rows + first, size), size)
            copies.append(pltpu.make_async_copy(ref, x_ref.at[place], sem.at[i]))
        for copy in copies:
            copy.start()
        for copy in copies:
            copy.wait()

    lanes = pl.ds(pl.multiple_of(at * block, block), block)
    g = dot_tn(x_ref[:, lanes], d_ref[...])
    share_ref[...] = jnp.sum(g * w_ref[...].astype(f32), axis=1, keepdims=True)
    o_ref[:, :columns] = dot_nt(g.astype(bf16), sel_ref[...]).astype(bf16)
    o_ref[:, columns:] = out_ref[...]


def qkv_grads(info, parts, d, w, select, beside, rows):
    length = d.shape[0]
    depth = w.shape[0]
    columns = select.shape[0]
    total = columns + beside.shape[1]
    block = 512
    placed = tuple((j, first) for _, j, first in parts)
    whole = lambda i, info: (0, 0)
    row = lambda i, info: (i, 0)
    return pl.pallas_call(
        functools.partial(qkv_grad_kernel, rows, placed),
        name="qkv_grads",
        grid_spec=pltpu.PrefetchScalarGridSpec(
            num_scalar_prefetch=1,
            grid=(depth // block,),
            in_specs=[anywhere()] * len(parts)
            + [
                pl.BlockSpec(d.shape, whole),
                pl.BlockSpec((block, w.shape[1]), row),
                pl.BlockSpec(select.shape, whole),
                pl.BlockSpec((block, beside.shape[1]), row),
            ],
            out_specs=[pl.BlockSpec((block, total), row), pl.BlockSpec((block, 1), row)],
            scratch_shapes=[
                pltpu.VMEM((length, depth), bf16),
                pltpu.SemaphoreType.DMA((len(parts),)),
            ],
        ),
        out_shape=[
            jax.ShapeDtypeStruct((depth, total), bf16),
            jax.ShapeDtypeStruct((depth, 1), f32),
        ],
        compiler_params=pltpu.CompilerParams(vmem_limit_bytes=VMEM),
        cost_estimate=SMALL,
    )(info, *[p for p, _, _ in parts], d, w, select, beside)


def finish_kernel(n, wide, info_ref, *refs):
    d = refs[:n]
    cols_ref, tok_ref, gain_ref, dm_ref, o_ref = refs[n : n + 5]
    w_ref, sem = refs[-2:]
    t = info_ref[0]
    members, _, size, columns = cols_ref.shape
    depth = members * size
    first = pl.program_id(0) == 0
    copies = [
        pltpu.make_async_copy(cols_ref.at[:, j], w_ref.at[j], sem.at[j]) for j in range(n)
    ]

    @pl.when(first)
    def _():
        for copy in copies:
            copy.start()

    for j in range(n):

        @pl.when(first)
        def _():
            copies[j].wait()

        part = dot_nt(d[j][...], w_ref[j].reshape(depth, columns))
        o_ref[...] = part if j == 0 else o_ref[...] + part
    x = tok_ref[...].astype(f32)
    inverse = lax.rsqrt(jnp.mean(x * x, axis=-1, keepdims=True) + EPS)
    unit = x * inverse
    e = o_ref[...] * gain_ref[...]
    inner = jnp.mean(e * unit, axis=-1, keepdims=True)
    o_ref[...] = dm_ref[...] + inverse * (e - unit * inner)
    if wide:
        first_ref = refs[n + 5]
        width = depth // n
        for j in range(n):
            at = pl.ds(pl.multiple_of((t ^ j) * width, width), width)
            first_ref[:, at] = d[j][:, 4 * LANES :].astype(f32)


def finish(info, d_parts, cols, tokens, gain, d_middle):
    n = len(d_parts)
    rows, depth = tokens.shape
    block = min(rows, 512)
    wide = (depth // n) % LANES == 0
    row = lambda i, info: (i, 0)
    whole = lambda i, info: (0, 0)
    count = 2 if wide else 1
    members, _, size, columns = cols.shape
    out = pl.pallas_call(
        functools.partial(finish_kernel, n, wide),
        name="finish",
        grid_spec=pltpu.PrefetchScalarGridSpec(
            num_scalar_prefetch=1,
            grid=(rows // block,),
            in_specs=[pl.BlockSpec((block, d.shape[1]), row) for d in d_parts]
            + [
                anywhere(),
                pl.BlockSpec((block, depth), row),
                pl.BlockSpec((1, depth), whole),
                pl.BlockSpec((block, depth), row),
            ],
            out_specs=[pl.BlockSpec((block, depth), row)] * count,
            scratch_shapes=[
                pltpu.VMEM((n, members, size, columns), bf16),
                pltpu.SemaphoreType.DMA((n,)),
            ],
        ),
        out_shape=[jax.ShapeDtypeStruct((rows, depth), f32)] * count,
        compiler_params=pltpu.CompilerParams(vmem_limit_bytes=VMEM),
        cost_estimate=LARGE,
    )(info, *d_parts, cols, tokens, gain, d_middle)
    if wide:
        return out
    heads_width = depth // n
    pieces_ = jnp.stack([d[:, 4 * LANES : 4 * LANES + heads_width] for d in d_parts])
    ordered = jnp.take(pieces_, info[0] ^ jnp.arange(n), axis=0)
    return out[0], ordered.transpose(1, 0, 2).reshape(rows, depth).astype(f32)


def shards(
    tokens,
    first_values,
    doc_lengths,
    attention_norm_gain,
    w_qkv,
    w_out,
    feedforward_norm_gain,
    w_gate,
    w_up,
    w_down,
    out_grad,
):
    n = lax.axis_size("tensor")
    high, low = split_axis(n)
    members = lax.axis_size("dp") // 2
    t = lax.axis_index("tensor")
    z, core = lax.axis_index("dp") // 2, lax.axis_index("dp") % 2
    info = jnp.stack([t, core]).astype(jnp.int32)
    rows, depth = tokens.shape
    heads = w_out.shape[0] // HD
    own_width = heads * HD
    width = max(LANES, own_width)
    length = rows * n
    block = min(256, rows)
    gain_one = attention_norm_gain[None, :]
    gain_two = feedforward_norm_gain[None, :]
    missing = width - own_width
    widen = lambda v: jnp.pad(v, ((0, 0), (0, missing))) if missing else v
    replicas = 2 * members
    size_d = depth // replicas
    mine = lambda w, axis: lax.dynamic_slice_in_dim(w, lax.axis_index("dp") * size_d, size_d, axis)

    together = lax.optimization_barrier
    cosine, sine_table = rope_tables(length)
    ends = jnp.cumsum(doc_lengths[0])
    starts = ends - doc_lengths[0]
    docs = doc_lengths.shape[1]
    limits = jnp.pad(jnp.stack([starts, ends]), ((0, 6), (HD, LANES - HD - docs)))
    heads_at = jnp.arange(length // block, dtype=jnp.int32) * block
    begins = jnp.max(jnp.where(starts[None, :] <= heads_at[:, None], starts[None, :], 0), axis=1)
    begins = (begins // block).astype(jnp.int32)
    select = column_selector(heads)
    w_cols = jnp.dot(w_qkv, select, preferred_element_type=f32).astype(bf16)

    own_weights = (w_gate.T, w_up.T, w_down)
    weight_slice = jnp.concatenate([mine(w, 1) for w in own_weights])
    value_parts = [
        widen(lax.dynamic_slice_in_dim(first_values, (t ^ j) * own_width, own_width, 1))
        for j in range(n)
    ]
    w_out_wide = jnp.pad(w_out, ((0, missing), (0, 0))) if missing else w_out
    out_slice = mine(w_out_wide, 1)
    normed = norm_rows(tokens, gain_one)
    value_parts, normed = together((value_parts, normed))
    normed_parts = gather_rows(normed, n)
    out_slices = [out_slice] + [swap("tensor", out_slice, j) for j in range(1, n)]
    w_out_all = over_replicas(jnp.concatenate(after(out_slices, normed)))
    value_parts = [value_parts[0]] + [swap("tensor", value_parts[j], j) for j in range(1, n)]
    placed = [(j, first) for _, j, first in normed_parts]
    pieces_in = [piece for piece, _, _ in normed_parts]
    cols_slice = mine(w_cols, 0)
    (
        pieces_in, value_parts, weight_slice, w_cols, cols_slice, cosine, sine_table, limits,
        grad_late,
    ) = together(
        (
            pieces_in, value_parts, weight_slice, w_cols, cols_slice, cosine, sine_table, limits,
            out_grad,
        )
    )

    far_slices = [swap("tensor", weight_slice, a * low) for a in range(1, high)]
    grad_rows = [out_grad] + [swap("tensor", grad_late, b) for b in range(1, low)]
    normed_parts = [(piece, j, first) for piece, (j, first) in zip(pieces_in, placed)]
    q, k, v, squares = project(
        heads, info, normed_parts, value_parts, w_cols, cosine, sine_table, limits, rows
    )
    q, far_slices, w_out_all = together((q, far_slices, w_out_all))
    seen = {}
    for j in range(n - 1, -1, -1):
        seen[j] = attend(heads, info, j, q, k, v, begins, block, rows)
        if j == 1:
            q, *grad_rows = together((q, *grad_rows))
    feed_far = [(over_replicas(w),) for w in far_slices]
    heads_rows = [seen[0][0]] + [swap("tensor", seen[j][0], j) for j in range(1, n)]
    heads_rows, cols_slice = together((heads_rows, cols_slice))

    parts = 2 if rows >= 512 else 1
    size = rows // parts
    middle, second, w_out_all, *second_parts = branch(
        info, heads_rows, w_out_all, tokens, gain_two, parts
    )
    second_parts, cols_slice = together((second_parts, cols_slice))
    far_keys = [(b, p) for b in range(1, low) for p in range(parts)]
    inputs = {(b, p): swap("tensor", second_parts[p], b) for b, p in far_keys}
    cols_far = [cols_slice] + [swap("tensor", cols_slice, j) for j in range(1, n)]
    shards_held = [own_weights] + feed_far
    own_out, own_back, act = feed(
        info, second, out_grad, 0, shards_held, 0, low * rows, [], 0, rows, False
    )
    shared, backs = [act], {}
    for b, p in far_keys:
        if (b, p) == far_keys[0]:
            inputs, cols_far, shared = together((inputs, cols_far, shared))
        arrived = inputs[b, p]
        to_send, backs[b, p], act = feed(
            info, arrived, grad_rows[b], p * size, shards_held, b * rows + p * size, low * rows,
            shared, (b - 1) * rows + p * size, (low - 1) * rows, True,
        )
        shared = [to_send, act]
    d_far = [[swap("tensor", backs[b, p], b) for b in range(1, low)] for p in range(parts)]
    d_far = [d[0] if low == 2 else add_up(*d) for d in d_far]
    sources = (
        [second] + [inputs[key] for key in far_keys],
        [0] + [b * rows + p * size for b, p in far_keys],
        grad_rows,
        [b * rows for b in range(low)],
    )
    d_far[0], act = together((d_far[0], act))
    cols = lax.all_gather(jnp.stack(cols_far), "dp", axis=0)
    wanted = [(a, m) for a in range(1, high) for m in range(3)] + [(0, 0), (0, 1), (0, 2)]
    keep, send = feed_grads(info, *sources, act, wanted, members)
    d_far, keep, send, to_send = together((d_far, keep, send, to_send))

    got = swap("dp", send, 1)
    d_middle, d_branch, feed_share, *d_att = branch_back(
        info, own_back, d_far, middle, out_grad, gain_two, w_out_all, width
    )
    d_att = [d_att[0]] + [swap("tensor", d_att[j], j) for j in range(1, n)]
    add_two = lambda lo, hi: add_up(keep[lo:hi], got[lo:hi]).astype(bf16)
    rest_sums = [add_two(3 * a + 1, 3 * a + 3) for a in range(high - 1)]
    rest_sums, got = together((rest_sums, got))
    gate_sums = jnp.stack(
        [add_two(i, i + 1)[0] for i in [3 * (high - 1)] + [3 * a for a in range(high - 1)]], axis=1
    )
    out_grad_w = out_grads(info, d_branch, heads_rows)
    d_att, to_send, out_grad_w, keep, got, cols = together(
        (d_att, to_send, out_grad_w, keep, got, cols)
    )

    gate_z = [
        swap("dp", lax.dynamic_index_in_dim(gate_sums, z ^ k, 0, keepdims=False), 2 * k)
        for k in range(1, members)
    ]
    rest_got = [swap("tensor", rest_sums[a - 1], a * low) for a in range(1, high)]
    out_got = [swap("tensor", to_send[(b - 1) * rows : b * rows], b) for b in range(1, low)]
    out_sum = lax.psum_scatter(out_grad_w, "tensor", scatter_dimension=0, tiled=False)
    d_cols = attend_back(
        heads, info, [seen[j][1] for j in range(n)], k, v, d_att, [seen[j][0] for j in range(n)],
        cosine, sine_table, begins, block,
    )
    d_cols, gate_z, rest_got, out_got, keep = together(
        (d_cols, gate_z, rest_got, out_got, keep)
    )

    d_all, *d_parts = d_cols
    rest_sum = add_up(keep[-2:], got[-2:], *rest_got).astype(bf16).swapaxes(0, 1)
    d_parts, d_all, rest_sum = together((d_parts, d_all, rest_sum))
    d_parts = [d_parts[0]] + [swap("tensor", d_parts[j], j) for j in range(1, n)]
    grads, share = qkv_grads(info, normed_parts, d_all, w_cols, select, out_sum, rows)
    grads = lax.psum_scatter(grads, "dp", scatter_dimension=0, tiled=True)
    gate_z, out_got, share = together((gate_z, out_got, share))
    step = 1
    if members > 1:
        rest_sum = halve_over_z(rest_sum, z, step, lambda half: after(half, share))
    gate_sum = add_up(
        lax.dynamic_index_in_dim(gate_sums, z, 0, keepdims=False), *gate_z
    ).astype(bf16)
    gate_sum = add_up(
        gate_sum[0], *[swap("tensor", gate_sum[a], a * low) for a in range(1, high)]
    )
    out = add_up(middle, own_out, *out_got).astype(bf16)
    totals = jnp.sum(squares[:2], axis=1)
    scalars = jnp.pad(totals[None, :], ((0, 0), (0, depth - 2)))
    shares = jnp.concatenate([share.reshape(1, depth) / gain_one, feed_share, scalars])
    d_parts, out, rest_sum = together((d_parts, out, rest_sum))
    while 2 * step < members:
        step *= 2
        rest_sum = halve_over_z(rest_sum, z, step, lambda half: half)
    rest_sum = rest_sum[0].astype(f32)
    tokens_grad, first_grad = finish(info, d_parts, cols, tokens, gain_one, d_middle)
    shares, tokens_grad, rest_sum = together((shares, tokens_grad, rest_sum))
    sums = all_sum(all_sum(shares, "dp"), "tensor")
    columns = 3 * own_width
    entry_count = first_values.size * lax.axis_size("dp") * n
    return (
        out,
        tokens_grad,
        first_grad,
        sums[0],
        grads[:, :columns].astype(f32),
        grads[:, columns : columns + own_width].T.astype(f32),
        sums[1],
        gate_sum.T,
        rest_sum[0].T,
        rest_sum[1],
        jnp.sqrt(sums[2, 1] / entry_count),
        jnp.sqrt(sums[2, 0] / entry_count),
    )


def solution(mesh):
    token_spec = P(("dp", "tensor"), None)
    return jax.shard_map(
        shards,
        mesh=mesh,
        in_specs=(
            token_spec,
            token_spec,
            P("dp", None),
            P(),
            P(None, "tensor"),
            P("tensor", None),
            P(),
            P(None, "tensor"),
            P(None, "tensor"),
            P("tensor", None),
            token_spec,
        ),
        out_specs=(
            token_spec,
            token_spec,
            token_spec,
            P(),
            P("dp", "tensor"),
            P("tensor", "dp"),
            P(),
            P("dp", "tensor"),
            P("dp", "tensor"),
            P("tensor", "dp"),
            P(),
            P(),
        ),
        check_vma=False,
    )
```

```python
import functools
import math

import jax
import jax.numpy as jnp
import numpy as np
from jax import lax
from jax.experimental import pallas as pl
from jax.experimental.pallas import tpu as pltpu
from jax.sharding import PartitionSpec as P

HD = 64
HALF = HD // 2
LANES = 128
GROUP = LANES // HALF
EPS = 1e-06
NEG = -1e30
VMEM = 60 << 20
SMALL = pl.CostEstimate(flops=1, bytes_accessed=1, transcendentals=0)
LARGE = pl.CostEstimate(flops=10**11, bytes_accessed=1, transcendentals=0)
f32 = jnp.float32
bf16 = jnp.bfloat16


def rope_tables(length):
    inverse = jnp.exp(-math.log(10000.0) * jnp.arange(HALF, dtype=f32) / HALF)
    angles = jnp.arange(length, dtype=f32)[:, None] * inverse[None, :]
    tile = lambda t: jnp.concatenate([t] * GROUP, axis=1)
    return tile(jnp.cos(angles)), tile(jnp.sin(angles))


def column_order(heads):
    value_width = max(LANES, heads * HD)
    order = np.full((4 * LANES + value_width,), -1, np.int32)
    for h in range(heads):
        for part in range(2):
            for half in range(2):
                at = (2 * part + half) * LANES + h * HALF
                src = h * 3 * HD + part * HD + half * HALF
                order[at : at + HALF] = np.arange(src, src + HALF)
        order[4 * LANES + h * HD : 4 * LANES + (h + 1) * HD] = np.arange(
            h * 3 * HD + 2 * HD, (h + 1) * 3 * HD
        )
    return order


def column_selector(heads):
    order = jnp.asarray(column_order(heads))
    rows = jnp.arange(3 * heads * HD, dtype=jnp.int32)
    return (rows[:, None] == order[None, :]).astype(bf16)


def dot_nt(a, b):
    return lax.dot_general(a, b, (((1,), (1,)), ((), ())), preferred_element_type=f32)


def dot_tn(a, b):
    return lax.dot_general(a, b, (((0,), (0,)), ((), ())), preferred_element_type=f32)


def dot_nn(a, b):
    return jnp.dot(a, b, preferred_element_type=f32)


def anywhere():
    return pl.BlockSpec(memory_space=pl.ANY)


def project_kernel(heads, placed, info_ref, *refs):
    count = len(placed)
    n = len({j for j, _ in placed})
    pieces, values = refs[:count], refs[count : count + n]
    w_ref, cos_ref, sin_ref, lim_ref = refs[count + n : count + n + 4]
    q_ref, k_ref, v_ref, sq_ref, x_ref, fv_ref, sem = refs[count + n + 4 :]
    at = pl.program_id(0)
    block = q_ref.shape[0]
    copies = []
    for i, (ref, (j, first)) in enumerate(zip(pieces, placed)):
        into = x_ref.at[j, first : first + ref.shape[0]]
        copies.append((j, pltpu.make_async_copy(ref, into, sem.at[i])))
    for j, ref in enumerate(values):
        copies.append((j, pltpu.make_async_copy(ref, fv_ref.at[j], sem.at[count + j])))

    @pl.when(at == 0)
    def _():
        sq_ref[...] = jnp.zeros_like(sq_ref)
        for _, copy in copies:
            copy.start()

    for j in range(n):

        @pl.when(at == j)
        def _():
            for owner, copy in copies:
                if owner == j:
                    copy.wait()

    acc = dot_nn(x_ref[at], w_ref[...])
    c, s = cos_ref[...], sin_ref[...]
    lane = lax.broadcasted_iota(jnp.int32, (block, LANES), 1)
    place = (info_ref[0] ^ at) * block + lax.broadcasted_iota(jnp.int32, (block, LANES), 0)
    inside = (place >= lim_ref[0:1, :]) & (place < lim_ref[1:2, :])
    doc_lane = (lane >= HD) & (lane < HD + 8)
    q_extra = jnp.where(doc_lane & jnp.logical_not(inside), NEG, 0.0)
    k_extra = jnp.where(inside, 1.0, jnp.where((lane >= HD + 8) & (lane < HD + 11), 1.0, 0.0))
    for ref, base, extra, scale in ((q_ref, 0, q_extra, HD**-0.5), (k_ref, 2, k_extra, 1.0)):
        u1 = acc[:, base * LANES : (base + 1) * LANES]
        u2 = acc[:, (base + 1) * LANES : (base + 2) * LANES]
        r1 = (u1 * c - u2 * s) * scale
        r2 = (u1 * s + u2 * c) * scale
        for h in range(heads):
            a = r1 if h == 0 else pltpu.roll(r1, LANES - HALF * h, 1)
            b = r2 if h == 1 else pltpu.roll(r2, (LANES + HALF - HALF * h) % LANES, 1)
            both = jnp.where(lane < HALF, a, jnp.where(lane < HD, b, extra))
            ref[:, h * LANES : (h + 1) * LANES] = both.astype(bf16)
    first = fv_ref[at].astype(f32)
    mixed = 0.5 * acc[:, 4 * LANES :] + 0.5 * first
    sq_ref[0:1, :] += jnp.sum(mixed * mixed, axis=0, keepdims=True)
    sq_ref[1:2, :] += jnp.sum(first * first, axis=0, keepdims=True)
    for h in range(heads):
        t = (h // 2) * LANES
        own = (lane < HD) if h % 2 == 0 else (lane >= HD)
        v_ref[:, h * LANES : (h + 1) * LANES] = jnp.where(
            own, mixed[:, t : t + LANES], 1.0
        ).astype(bf16)


def project(heads, info, parts, values, w, cos, sin, limits, rows):
    n = len(values)
    length = rows * n
    depth = parts[0][0].shape[1]
    width = values[0].shape[1]
    row = lambda i, info: (info[0] ^ i, 0)
    whole = lambda i, info: (0, 0)
    ext = heads * LANES
    placed = tuple((j, first) for _, j, first in parts)
    return pl.pallas_call(
        functools.partial(project_kernel, heads, placed),
        name="project",
        grid_spec=pltpu.PrefetchScalarGridSpec(
            num_scalar_prefetch=1,
            grid=(n,),
            in_specs=[anywhere()] * (len(parts) + n)
            + [
                pl.BlockSpec(w.shape, whole),
                pl.BlockSpec((rows, LANES), row),
                pl.BlockSpec((rows, LANES), row),
                pl.BlockSpec((8, LANES), whole),
            ],
            out_specs=[
                pl.BlockSpec((rows, ext), row),
                pl.BlockSpec((rows, ext), row),
                pl.BlockSpec((rows, ext), row),
                pl.BlockSpec((8, width), whole),
            ],
            scratch_shapes=[
                pltpu.VMEM((n, rows, depth), bf16),
                pltpu.VMEM((n, rows, width), bf16),
                pltpu.SemaphoreType.DMA((len(parts) + n,)),
            ],
        ),
        out_shape=[jax.ShapeDtypeStruct((length, ext), bf16)] * 3
        + [jax.ShapeDtypeStruct((8, width), f32)],
        compiler_params=pltpu.CompilerParams(vmem_limit_bytes=VMEM),
        cost_estimate=SMALL,
    )(info, *[p for p, _, _ in parts], *values, w, cos, sin, limits)


def pieces(x):
    hi = x.astype(bf16).astype(f32)
    mid = (x - hi).astype(bf16).astype(f32)
    return hi, mid, x - hi - mid


def attend_kernel(
    heads, offset, bk, info_ref, begin_ref, q_ref, k_ref, v_ref, o_ref, qo_ref, m_ref, acc_ref
):
    bq = q_ref.shape[0]
    at = info_ref[0] ^ offset
    lane = lax.broadcasted_iota(jnp.int32, (bq, LANES), 1)
    r = lax.broadcasted_iota(jnp.int32, (bq, bk), 0)
    c = lax.broadcasted_iota(jnp.int32, (bq, bk), 1)
    col = [slice(h * LANES, (h + 1) * LANES) for h in range(heads)]
    spread = lambda m: jnp.concatenate([m] * (bk // LANES), axis=1)

    def visit(kb, mask, first):
        there = pl.ds(pl.multiple_of(kb * bk, bk), bk)
        for h in range(heads):
            s = dot_nt(q_ref[:, col[h]], k_ref[there, col[h]])
            if mask is not None:
                s = jnp.where(mask, s, NEG)
            new = jnp.broadcast_to(jnp.max(s, axis=1, keepdims=True), (bq, LANES))
            if not first:
                old = m_ref[:, col[h]]
                new = jnp.maximum(old, new)
            p = jnp.exp(s - spread(new)).astype(bf16)
            part = dot_nn(p, v_ref[there, col[h]])
            m_ref[:, col[h]] = new
            acc_ref[:, col[h]] = part if first else acc_ref[:, col[h]] * jnp.exp(old - new) + part

    for d in range(bq // bk):
        visit(at * (bq // bk) + d, c + d * bk <= r, d == 0)

    def step(kb, carry):
        visit(kb, None, False)
        return carry

    lax.fori_loop(begin_ref[at * (bq // bk)], at * (bq // bk), step, 0)
    low = lane < HD
    for t in range((heads + 1) // 2):
        a = acc_ref[:, col[2 * t]]
        b = acc_ref[:, col[2 * t + 1]] if 2 * t + 1 < heads else a
        total = pltpu.roll(jnp.where(low, b, a), HD, 1)
        result = jnp.where(low, a, b) / total
        if 2 * t + 1 >= heads:
            result = jnp.where(low, result, 0.0)
        o_ref[:, t * LANES : (t + 1) * LANES] = result.astype(bf16)
    for h in range(heads):
        a = acc_ref[:, col[h]]
        total = a if h % 2 == 0 else pltpu.roll(a, HD, 1)
        hi, mid, lo = pieces(-(m_ref[:, col[h]] + jnp.log(jnp.where(low, 1.0, total))))
        extra = jnp.where(
            lane == HD + 8, hi, jnp.where(lane == HD + 9, mid, jnp.where(lane == HD + 10, lo, 0.0))
        )
        fill = (lane >= HD + 8) & (lane < HD + 11)
        qo_ref[:, col[h]] = jnp.where(fill, extra, q_ref[:, col[h]].astype(f32)).astype(bf16)


def attend(heads, info, offset, q, k, v, begins, block, rows):
    length = q.shape[0]
    ext = heads * LANES
    width = max(LANES, heads * HD)
    whole = lambda i, info, b: (0, 0)
    return pl.pallas_call(
        functools.partial(attend_kernel, heads, offset, block),
        name="attend",
        grid_spec=pltpu.PrefetchScalarGridSpec(
            num_scalar_prefetch=2,
            grid=(1,),
            in_specs=[
                pl.BlockSpec((rows, ext), lambda i, info, b: (info[0] ^ offset, 0)),
                pl.BlockSpec((length, ext), whole),
                pl.BlockSpec((length, ext), whole),
            ],
            out_specs=[pl.BlockSpec((rows, width), whole), pl.BlockSpec((rows, ext), whole)],
            scratch_shapes=[pltpu.VMEM((rows, ext), f32), pltpu.VMEM((rows, ext), f32)],
        ),
        out_shape=[
            jax.ShapeDtypeStruct((rows, width), bf16),
            jax.ShapeDtypeStruct((rows, ext), bf16),
        ],
        compiler_params=pltpu.CompilerParams(vmem_limit_bytes=VMEM),
        cost_estimate=SMALL,
    )(info, begins, q, k, v)


def attend_back_kernel(heads, block, n, info_ref, begin_ref, *refs):
    q_parts, do_parts, o_parts = refs[:n], refs[n : 2 * n], refs[2 * n : 3 * n]
    k_ref, v_ref, cos_ref, sin_ref, g_ref = refs[3 * n : 3 * n + 5]
    sends = refs[3 * n + 5 : 4 * n + 5]
    q_all, do_all, o_all, dk_ref, dv_ref, dq_ref, de_ref, sem = refs[4 * n + 5 :]
    at = pl.program_id(0)
    rows = q_parts[0].shape[0]

    def moves(pairs):
        copies = []
        for i, (make, j) in enumerate(pairs):
            place = pl.ds(pl.multiple_of((info_ref[0] ^ j) * rows, rows), rows)
            copies.append(make(place, sem.at[i]))
        for copy in copies:
            copy.start()
        for copy in copies:
            copy.wait()

    @pl.when(at == 0)
    def _():
        moves(
            [
                (functools.partial(lambda src, dst, p, s: pltpu.make_async_copy(src, dst.at[p], s), part, whole), j)
                for parts, whole in ((q_parts, q_all), (do_parts, do_all), (o_parts, o_all))
                for j, part in enumerate(parts)
            ]
        )

    lane = lax.broadcasted_iota(jnp.int32, (block, LANES), 1)
    r = lax.broadcasted_iota(jnp.int32, (block, block), 0)
    c = lax.broadcasted_iota(jnp.int32, (block, block), 1)
    causal = r <= c
    low = lane < HD
    here = pl.ds(pl.multiple_of(at * block, block), block)
    col = [slice(h * LANES, (h + 1) * LANES) for h in range(heads)]

    for h in range(heads):
        t = slice((h // 2) * LANES, (h // 2 + 1) * LANES)
        own = low if h % 2 == 0 else jnp.logical_not(low)
        grad = do_all[here, t].astype(f32)
        product = grad * o_all[here, t].astype(f32)
        centre = jnp.sum(jnp.where(own, product, 0.0), axis=1, keepdims=True)
        hi, mid, lo = pieces(-jnp.broadcast_to(centre, (block, LANES)))
        spot = lane - (HD if h % 2 == 0 else 0)
        extra = jnp.where(spot == 0, hi, jnp.where(spot == 1, mid, jnp.where(spot == 2, lo, 0.0)))
        de_ref[:, col[h]] = jnp.where(own, grad, extra).astype(bf16)

    def visit(there, mask, first):
        st = [dot_nt(k_ref[there, c_], q_all[here, c_]) for c_ in col]
        dpt = [dot_nt(v_ref[there, c_], de_ref[:, c_]) for c_ in col]
        p = [jnp.exp(s) for s in st]
        if mask is not None:
            p = [jnp.where(mask, x, 0.0) for x in p]
        ds = [(x * y).astype(bf16) for x, y in zip(p, dpt)]
        p = [x.astype(bf16) for x in p]
        for h, c_ in enumerate(col):
            dv = dot_nn(p[h], de_ref[:, c_])
            dk = dot_nn(ds[h], q_all[here, c_])
            dq = dot_tn(ds[h], k_ref[there, c_])
            if first:
                dv_ref[there, c_] = dv
                dk_ref[there, c_] = dk
                dq_ref[:, c_] = dq
            else:
                dv_ref[there, c_] += dv
                dk_ref[there, c_] += dk
                dq_ref[:, c_] += dq

    visit(here, causal, True)

    def step(kb, carry):
        visit(pl.ds(pl.multiple_of(kb * block, block), block), None, False)
        return carry

    lax.fori_loop(begin_ref[at], at, step, 0)

    def turn_back(ref, rows, scale):
        u1 = u2 = None
        quarter = lane // HALF
        for h in range(heads):
            u = ref[rows, col[h]]
            a = u if h == 0 else pltpu.roll(u, HALF * h, 1)
            b = u if h == 1 else pltpu.roll(u, (LANES + HALF * h - HALF) % LANES, 1)
            u1 = a if h == 0 else jnp.where(quarter == h, a, u1)
            u2 = b if h == 0 else jnp.where(quarter == h, b, u2)
        if heads < GROUP:
            u1 = jnp.where(quarter < heads, u1, 0.0)
            u2 = jnp.where(quarter < heads, u2, 0.0)
        u1, u2 = u1 * scale, u2 * scale
        cs, sn = cos_ref[rows, :], sin_ref[rows, :]
        return (u1 * cs + u2 * sn).astype(bf16), (u2 * cs - u1 * sn).astype(bf16)

    def finish_block(i, carry):
        rows = pl.ds(pl.multiple_of(i * block, block), block)
        d1, d2 = turn_back(dk_ref, rows, 1.0)
        g_ref[rows, 2 * LANES : 3 * LANES] = d1
        g_ref[rows, 3 * LANES : 4 * LANES] = d2
        for t in range((heads + 1) // 2):
            a = dv_ref[rows, col[2 * t]]
            b = dv_ref[rows, col[2 * t + 1]] if 2 * t + 1 < heads else jnp.zeros_like(a)
            d_mix = jnp.where(low, a, b).astype(bf16)
            g_ref[rows, (4 + t) * LANES : (5 + t) * LANES] = (d_mix.astype(f32) * 0.5).astype(bf16)
        return carry

    u1 = u2 = None
    quarter = lane // HALF
    for h in range(heads):
        u = dq_ref[:, col[h]]
        a = u if h == 0 else pltpu.roll(u, HALF * h, 1)
        b = u if h == 1 else pltpu.roll(u, (LANES + HALF * h - HALF) % LANES, 1)
        u1 = a if h == 0 else jnp.where(quarter == h, a, u1)
        u2 = b if h == 0 else jnp.where(quarter == h, b, u2)
    if heads < GROUP:
        u1 = jnp.where(quarter < heads, u1, 0.0)
        u2 = jnp.where(quarter < heads, u2, 0.0)
    u1, u2 = u1 * HD**-0.5, u2 * HD**-0.5
    cs, sn = cos_ref[here, :], sin_ref[here, :]
    g_ref[here, 0:LANES] = (u1 * cs + u2 * sn).astype(bf16)
    g_ref[here, LANES : 2 * LANES] = (u2 * cs - u1 * sn).astype(bf16)

    @pl.when(at == pl.num_programs(0) - 1)
    def _():
        lax.fori_loop(0, pl.num_programs(0), finish_block, 0)
        moves(
            [
                (functools.partial(lambda dst, p, s: pltpu.make_async_copy(g_ref.at[p], dst, s), dst), j)
                for j, dst in enumerate(sends)
            ]
        )


def attend_back(heads, info, q_parts, k, v, do_parts, o_parts, cos, sin, begins, block):
    n = len(q_parts)
    rows = q_parts[0].shape[0]
    length = n * rows
    ext = heads * LANES
    width = o_parts[0].shape[1]
    whole = lambda i, info, b: (0, 0)
    anywhere = pl.BlockSpec(memory_space=pl.ANY)
    columns = 4 * LANES + width
    return pl.pallas_call(
        functools.partial(attend_back_kernel, heads, block, n),
        name="attend_back",
        grid_spec=pltpu.PrefetchScalarGridSpec(
            num_scalar_prefetch=2,
            grid=(length // block,),
            in_specs=[anywhere] * (3 * n)
            + [
                pl.BlockSpec((length, ext), whole),
                pl.BlockSpec((length, ext), whole),
                pl.BlockSpec((length, LANES), whole),
                pl.BlockSpec((length, LANES), whole),
            ],
            out_specs=[pl.BlockSpec((length, columns), whole)] + [anywhere] * n,
            scratch_shapes=[
                pltpu.VMEM((length, ext), bf16),
                pltpu.VMEM((length, width), bf16),
                pltpu.VMEM((length, width), bf16),
                pltpu.VMEM((length, ext), f32),
                pltpu.VMEM((length, ext), f32),
                pltpu.VMEM((block, ext), f32),
                pltpu.VMEM((block, ext), bf16),
                pltpu.SemaphoreType.DMA((3 * n,)),
            ],
        ),
        out_shape=[jax.ShapeDtypeStruct((length, columns), bf16)]
        + [jax.ShapeDtypeStruct((rows, columns), bf16)] * n,
        compiler_params=pltpu.CompilerParams(vmem_limit_bytes=VMEM),
        cost_estimate=LARGE,
    )(info, begins, *q_parts, *do_parts, *o_parts, k, v, cos, sin)


def split_axis(n):
    low = 1 << ((n.bit_length() - 1) // 2)
    return n // low, low


def swap(axis, value, offset):
    n = lax.axis_size(axis)
    return lax.ppermute(value, axis, [(i, i ^ offset) for i in range(n)])


def gather_rows(value, n):
    high, low = split_axis(n)
    rows = value.shape[0]
    half = rows // 2
    parts = {0: value}
    for b in range(1, low):
        parts[b] = swap("tensor", value, b)
    for a in range(1, high):
        parts[a * low] = swap("tensor", value, a * low)
    listed = [(parts[j], j, 0) for j in sorted(parts)]
    for a in range(1, high):
        for b in range(1, low):
            j = a * low + b
            listed.append((swap("tensor", parts[b][:half], a * low), j, 0))
            listed.append((swap("tensor", parts[a * low][half:], b), j, half))
    return listed


def after(value, *others):
    return lax.optimization_barrier((value,) + others)[0]


def add_up(first, *others):
    total = first.astype(f32)
    for other in others:
        total = total + other.astype(f32)
    return total


def over_replicas(value):
    if value.shape[1] % LANES == 0:
        return lax.all_gather(value, "dp", axis=0)
    return lax.all_gather(value, "dp", axis=1, tiled=True)


def halve_over_z(parts, z, step, hold):
    pairs = parts.reshape((-1, 2) + parts.shape[1:])
    side = (z // step) % 2
    pick = lambda which: lax.dynamic_index_in_dim(pairs, which, 1, keepdims=False)
    parts = add_up(pick(side), hold(swap("dp", pick(1 - side), 2 * step)))
    return parts.astype(bf16) if parts.shape[0] > 1 else parts


def all_sum(axis, value, offsets):
    parts = [value] + [swap(axis, value, j) for j in offsets]
    while len(parts) > 1:
        parts = [a + b for a, b in zip(parts[::2], parts[1::2])]
    return parts[0]


def norm_kernel(x_ref, gain_ref, o_ref):
    x = x_ref[...].astype(f32)
    inverse = lax.rsqrt(jnp.mean(x * x, axis=-1, keepdims=True) + EPS)
    o_ref[...] = (x * inverse * gain_ref[...]).astype(bf16)


def norm_rows(x, gain):
    rows, depth = x.shape
    block = min(rows, 128)
    return pl.pallas_call(
        norm_kernel,
        name="norm_rows",
        grid=(rows // block,),
        in_specs=[
            pl.BlockSpec((block, depth), lambda i: (i, 0)),
            pl.BlockSpec((1, depth), lambda i: (0, 0)),
        ],
        out_specs=pl.BlockSpec((block, depth), lambda i: (i, 0)),
        out_shape=jax.ShapeDtypeStruct((rows, depth), bf16),
        compiler_params=pltpu.CompilerParams(vmem_limit_bytes=VMEM),
        cost_estimate=SMALL,
    )(x, gain)


def branch_kernel(n, parts, info_ref, *refs):
    att = refs[:n]
    slices_ref, tok_ref, gain_ref, mid_ref, h_ref, w_ref = refs[n : n + 6]
    h_parts = refs[n + 6 : n + 6 + parts]
    all_ref, sem, w_sem = refs[n + 6 + parts :]
    at = pl.program_id(0)
    size = tok_ref.shape[0]
    width = att[0].shape[1]

    @pl.when(at == 0)
    def _():
        copies = [
            pltpu.make_async_copy(
                att[j], all_ref.at[:, j * width : (j + 1) * width], sem.at[j]
            )
            for j in range(n)
        ]
        if len(slices_ref.shape) == 3:
            lanes = slices_ref.shape[2]
            copies += [
                pltpu.make_async_copy(
                    slices_ref.at[d], w_ref.at[:, d * lanes : (d + 1) * lanes], w_sem.at[d]
                )
                for d in range(slices_ref.shape[0])
            ]
        else:
            copies.append(pltpu.make_async_copy(slices_ref, w_ref, w_sem.at[0]))
        for copy in copies:
            copy.start()
        for copy in copies:
            copy.wait()

    here = pl.ds(pl.multiple_of(at * size, size), size)
    x = tok_ref[...].astype(f32) + dot_nn(all_ref[here, :], w_ref[...])
    mid_ref[...] = x
    inverse = lax.rsqrt(jnp.mean(x * x, axis=-1, keepdims=True) + EPS)
    h = (x * inverse * gain_ref[...]).astype(bf16)
    h_ref[...] = h
    for p in range(parts):

        @pl.when(at == p)
        def _():
            h_parts[p][...] = h


def branch(info, att, w_slices, tokens, gain, parts):
    n = len(att)
    rows, width = att[0].shape
    depth = tokens.shape[1]
    size = rows // parts
    whole = lambda i, info: (0, 0)
    row = lambda i, info: (i, 0)
    count = w_slices.shape[0] if w_slices.ndim == 3 else 1
    return pl.pallas_call(
        functools.partial(branch_kernel, n, parts),
        name="branch",
        grid_spec=pltpu.PrefetchScalarGridSpec(
            num_scalar_prefetch=1,
            grid=(parts,),
            in_specs=[anywhere()] * (n + 1)
            + [pl.BlockSpec((size, depth), row), pl.BlockSpec((1, depth), whole)],
            out_specs=[pl.BlockSpec((size, depth), row)] * 2
            + [pl.BlockSpec((n * width, depth), whole)]
            + [pl.BlockSpec((size, depth), whole)] * parts,
            scratch_shapes=[
                pltpu.VMEM((rows, n * width), bf16),
                pltpu.SemaphoreType.DMA((n,)),
                pltpu.SemaphoreType.DMA((count,)),
            ],
        ),
        out_shape=[
            jax.ShapeDtypeStruct((rows, depth), f32),
            jax.ShapeDtypeStruct((rows, depth), bf16),
            jax.ShapeDtypeStruct((n * width, depth), bf16),
        ]
        + [jax.ShapeDtypeStruct((size, depth), bf16)] * parts,
        compiler_params=pltpu.CompilerParams(vmem_limit_bytes=VMEM),
        cost_estimate=SMALL,
    )(info, *att, w_slices, tokens, gain)


def feed_kernel(shards_in, shared, send, act_first, info_ref, h_ref, g_ref, *refs):
    count = sum(shards_in)
    weights, refs = refs[:count], refs[count + shared :]
    out_ref, dh_ref, act_out, w_ref, sem, act_ref, act_sem = refs[:7]
    out_acc, dh_acc = refs[7:] if send else (out_ref, dh_ref)
    high, rows_w, depth = w_ref.shape
    units = rows_w // 3
    copies, at, used = [], 0, 0
    for a, pieces_in in enumerate(shards_in):
        groups = []
        for m in range(3):
            span = pl.ds(m * units, units)
            ref = weights[at + m] if pieces_in == 3 else weights[at]
            if pieces_in == 3:
                moves = [(ref, w_ref.at[a, span])]
            elif len(ref.shape) == 3:
                size = ref.shape[2]
                moves = [
                    (ref.at[d, span], w_ref.at[a, span, d * size : (d + 1) * size])
                    for d in range(ref.shape[0])
                ]
            else:
                moves = [(ref.at[span], w_ref.at[a, span])]
            groups.append(
                [
                    pltpu.make_async_copy(src, dst, sem.at[used + i])
                    for i, (src, dst) in enumerate(moves)
                ]
            )
            used += len(moves)
        at += pieces_in
        copies.append(groups)
    for groups in copies:
        for group in groups:
            for copy in group:
                copy.start()

    rows = h_ref.shape[0]
    out_acc[...] = jnp.zeros_like(out_acc)
    dh_acc[...] = jnp.zeros_like(dh_acc)

    def leave(a):
        to = act_out.at[a, :, act_first : act_first + rows]
        return pltpu.make_async_copy(act_ref.at[a], to, act_sem.at[a])

    def shard(a, carry):
        def weight(m):
            for k in range(high):

                @pl.when(a == k)
                def _():
                    for copy in copies[k][m]:
                        copy.wait()

            return w_ref[a, m * units : (m + 1) * units, :]

        gate = dot_nt(h_ref[...], weight(0))
        up = dot_nt(h_ref[...], weight(1))
        back = dot_nt(g_ref[...], weight(2))
        s = 0.5 * jnp.tanh(0.5 * gate) + 0.5
        gs = gate * s
        hidden = (gs * up).astype(bf16)
        d_up = (back * gs).astype(bf16)
        d_gate = (back * up * (s + gs * (1.0 - s))).astype(bf16)
        act_ref[a, 0] = d_gate
        act_ref[a, 1] = d_up
        act_ref[a, 2] = hidden
        leave(a).start()
        gate_w, up_w, down_w = (w_ref[a, m * units : (m + 1) * units, :] for m in range(3))
        dh_acc[...] += dot_nn(d_gate, gate_w) + dot_nn(d_up, up_w)
        out_acc[...] += dot_nn(hidden, down_w)
        return carry

    lax.fori_loop(0, high, shard, 0)
    if send:
        out_ref[...] = out_acc[...].astype(bf16)
        dh_ref[...] = dh_acc[...].astype(bf16)
    for a in range(high):
        leave(a).wait()


def feed(info, h, g, g_first, weights, act_first, act_rows, shared, out_first, out_rows, send):
    rows, depth = h.shape
    high = len(weights)
    flat = [w for shard in weights for w in shard]
    units = weights[0][0].shape[0] if len(weights[0]) == 3 else weights[0][0].shape[-2] // 3
    block = rows
    at, out_at = g_first // block, out_first // block
    row = lambda i, info: (i, 0)
    kind = bf16 if send else f32
    moves = sum(
        3 if len(shard) == 3 else 3 * (shard[0].shape[0] if shard[0].ndim == 3 else 1)
        for shard in weights
    )
    base = 3 + len(flat)
    aliases = {} if not shared else {base: 2} if len(shared) == 1 else {base: 0, base + 1: 2}
    return pl.pallas_call(
        functools.partial(
            feed_kernel, tuple(len(shard) for shard in weights), len(shared), send, act_first
        ),
        name="feed",
        grid_spec=pltpu.PrefetchScalarGridSpec(
            num_scalar_prefetch=1,
            grid=(1,),
            in_specs=[
                pl.BlockSpec((block, depth), row),
                pl.BlockSpec((block, depth), lambda i, info: (at, 0)),
            ]
            + [anywhere()] * (len(flat) + len(shared)),
            out_specs=[
                pl.BlockSpec((block, depth), lambda i, info: (out_at, 0)),
                pl.BlockSpec((block, depth), row),
                anywhere(),
            ],
            scratch_shapes=[
                pltpu.VMEM((high, 3 * units, depth), bf16),
                pltpu.SemaphoreType.DMA((moves,)),
                pltpu.VMEM((high, 3, block, units), bf16),
                pltpu.SemaphoreType.DMA((high,)),
            ]
            + ([pltpu.VMEM((block, depth), f32)] * 2 if send else []),
        ),
        out_shape=[
            jax.ShapeDtypeStruct((out_rows, depth), kind),
            jax.ShapeDtypeStruct((rows, depth), kind),
            jax.ShapeDtypeStruct((high, 3, act_rows, units), bf16),
        ],
        input_output_aliases=aliases,
        compiler_params=pltpu.CompilerParams(vmem_limit_bytes=VMEM),
        cost_estimate=SMALL,
    )(info, h, g, *flat, *shared)


def feed_grad_kernel(h_rows, g_rows, members, info_ref, list_ref, *refs):
    h, g = refs[: len(h_rows)], refs[len(h_rows) : len(h_rows) + len(g_rows)]
    act_ref, keep_ref, send_ref, h_ref, g_ref, h_sem, g_sem = refs[len(h_rows) + len(g_rows) :]
    core = info_ref[1]
    at = pl.program_id(0)
    depth = h_ref.shape[1]
    half = depth // 2
    size = half // members
    aligned = size % LANES == 0

    def copies(parts, rows, whole, sem):
        out = []
        for ref, first in zip(parts, rows):
            here = slice(first, first + ref.shape[0])
            if not aligned:
                out.append(pltpu.make_async_copy(ref, whole.at[here], sem.at[len(out)]))
                continue
            for side in range(2):
                for z in range(members):
                    lanes = pl.ds(pl.multiple_of((2 * z + (core ^ side)) * size, size), size)
                    to = slice(side * half + z * size, side * half + (z + 1) * size)
                    out.append(
                        pltpu.make_async_copy(ref.at[:, lanes], whole.at[here, to], sem.at[len(out)])
                    )
        return out

    h_copies, g_copies = copies(h, h_rows, h_ref, h_sem), copies(g, g_rows, g_ref, g_sem)

    @pl.when(at == 0)
    def _():
        for copy in h_copies + g_copies:
            copy.start()
        for copy in h_copies:
            copy.wait()

    @pl.when(at == 1)
    def _():
        for copy in g_copies:
            copy.wait()

    def work(source):
        if aligned:
            for ref, side in ((keep_ref, 0), (send_ref, 1)):
                g_side = dot_tn(act_ref[0, 0], source[:, side * half : (side + 1) * half])
                for z in range(members):
                    ref[0, z] = g_side[:, z * size : (z + 1) * size].astype(bf16)
            return
        g_all = dot_tn(act_ref[0, 0], source[...])
        for z in range(members):
            even = g_all[:, 2 * z * size : (2 * z + 1) * size]
            odd = g_all[:, (2 * z + 1) * size : (2 * z + 2) * size]
            keep_ref[0, z] = jnp.where(core == 0, even, odd).astype(bf16)
            send_ref[0, z] = jnp.where(core == 0, odd, even).astype(bf16)

    @pl.when(list_ref[at, 1] < 2)
    def _():
        work(h_ref)

    @pl.when(list_ref[at, 1] == 2)
    def _():
        work(g_ref)


def feed_grads(info, h, h_rows, g, g_rows, act, wanted, members):
    depth = h[0].shape[1]
    _, _, rows, units = act.shape
    size = depth // (2 * members)
    count = len(wanted)
    out = jax.ShapeDtypeStruct((count, members, units, size), bf16)
    return pl.pallas_call(
        functools.partial(feed_grad_kernel, tuple(h_rows), tuple(g_rows), members),
        name="feed_grads",
        grid_spec=pltpu.PrefetchScalarGridSpec(
            num_scalar_prefetch=2,
            grid=(count,),
            in_specs=[anywhere()] * (len(h) + len(g))
            + [pl.BlockSpec((1, 1, rows, units), lambda i, info, w: (w[i, 0], w[i, 1], 0, 0))],
            out_specs=[pl.BlockSpec((1, members, units, size), lambda i, info, w: (i, 0, 0, 0))]
            * 2,
            scratch_shapes=[
                pltpu.VMEM((rows, depth), bf16),
                pltpu.VMEM((rows, depth), bf16),
                pltpu.SemaphoreType.DMA((2 * members * len(h),)),
                pltpu.SemaphoreType.DMA((2 * members * len(g),)),
            ],
        ),
        out_shape=[out, out],
        compiler_params=pltpu.CompilerParams(vmem_limit_bytes=VMEM),
        cost_estimate=SMALL,
    )(info, jnp.asarray(wanted, jnp.int32), *h, *g, act)


def branch_back_kernel(n, parts, info_ref, dh_ref, mid_ref, g_ref, gain_ref, w_ref, *refs):
    far, refs = refs[:parts], refs[parts:]
    dm_ref, db_ref, gg_ref = refs[:3]
    da = refs[3:]
    at = pl.program_id(0)
    width = da[0].shape[1]
    x = mid_ref[...]
    inverse = lax.rsqrt(jnp.mean(x * x, axis=-1, keepdims=True) + EPS)
    unit = x * inverse
    received = far[0][...]
    for p in range(1, parts):
        received = jnp.where(at == p, far[p][...], received)
    cotangent = dh_ref[...] + received.astype(f32)
    e = cotangent * gain_ref[...]
    inner = jnp.mean(e * unit, axis=-1, keepdims=True)
    d_mid = g_ref[...].astype(f32) + inverse * (e - unit * inner)
    share = jnp.sum(cotangent * unit, axis=0, keepdims=True)

    @pl.when(at == 0)
    def _():
        gg_ref[...] = jnp.zeros_like(gg_ref)

    gg_ref[...] += share
    dm_ref[...] = d_mid
    rounded = d_mid.astype(bf16)
    db_ref[...] = rounded
    for j in range(n):
        da[j][...] = dot_nt(rounded, w_ref[j * width : (j + 1) * width, :]).astype(bf16)


def branch_back(info, d_h, d_far, middle, g, gain, w_all, width):
    n = w_all.shape[0] // width
    parts = len(d_far)
    rows, depth = middle.shape
    size = rows // parts
    whole = lambda i, info: (0, 0)
    row = lambda i, info: (i, 0)
    part = pl.BlockSpec((size, depth), row)
    return pl.pallas_call(
        functools.partial(branch_back_kernel, n, parts),
        name="branch_back",
        grid_spec=pltpu.PrefetchScalarGridSpec(
            num_scalar_prefetch=1,
            grid=(parts,),
            in_specs=[part, part, part]
            + [pl.BlockSpec(gain.shape, whole), pl.BlockSpec(w_all.shape, whole)]
            + [pl.BlockSpec((size, depth), whole)] * parts,
            out_specs=[part, part, pl.BlockSpec((1, depth), whole)]
            + [pl.BlockSpec((size, width), row)] * n,
        ),
        out_shape=[
            jax.ShapeDtypeStruct((rows, depth), f32),
            jax.ShapeDtypeStruct((rows, depth), bf16),
            jax.ShapeDtypeStruct((1, depth), f32),
        ]
        + [jax.ShapeDtypeStruct((rows, width), bf16)] * n,
        compiler_params=pltpu.CompilerParams(vmem_limit_bytes=VMEM),
        cost_estimate=SMALL,
    )(info, d_h, middle, g, gain, w_all, *d_far)


def out_grad_kernel(n, info_ref, *refs):
    db_ref = refs[0]
    att = refs[1 : 1 + n]
    o_ref = refs[1 + n]
    for j in range(n):
        o_ref[info_ref[0] ^ j] = dot_tn(db_ref[...], att[j][...]).astype(bf16)


def out_grads(info, d_branch, att):
    n = len(att)
    rows, depth = d_branch.shape
    width = att[0].shape[1]
    whole = lambda i, info: (0, 0)
    return pl.pallas_call(
        functools.partial(out_grad_kernel, n),
        name="out_grads",
        grid_spec=pltpu.PrefetchScalarGridSpec(
            num_scalar_prefetch=1,
            grid=(1,),
            in_specs=[pl.BlockSpec(d_branch.shape, whole)]
            + [pl.BlockSpec(a.shape, whole) for a in att],
            out_specs=pl.BlockSpec((n, depth, width), lambda i, info: (0, 0, 0)),
        ),
        out_shape=jax.ShapeDtypeStruct((n, depth, width), bf16),
        compiler_params=pltpu.CompilerParams(vmem_limit_bytes=VMEM),
        cost_estimate=SMALL,
    )(info, d_branch, *att)


def qkv_grad_kernel(rows, placed, info_ref, *refs):
    count = len(placed)
    pieces = refs[:count]
    d_ref, w_ref, sel_ref, out_ref, o_ref, share_ref, x_ref, sem = refs[count:]
    columns = sel_ref.shape[0]
    at = pl.program_id(0)
    block = o_ref.shape[0]

    @pl.when(at == 0)
    def _():
        copies = []
        for i, (ref, (j, first)) in enumerate(zip(pieces, placed)):
            size = ref.shape[0]
            place = pl.ds(pl.multiple_of((info_ref[0] ^ j) * rows + first, size), size)
            copies.append(pltpu.make_async_copy(ref, x_ref.at[place], sem.at[i]))
        for copy in copies:
            copy.start()
        for copy in copies:
            copy.wait()

    lanes = pl.ds(pl.multiple_of(at * block, block), block)
    g = dot_tn(x_ref[:, lanes], d_ref[...])
    share_ref[...] = jnp.sum(g * w_ref[...].astype(f32), axis=1, keepdims=True)
    o_ref[:, :columns] = dot_nt(g.astype(bf16), sel_ref[...]).astype(bf16)
    o_ref[:, columns:] = out_ref[...]


def qkv_grads(info, parts, d, w, select, beside, rows):
    length = d.shape[0]
    depth = w.shape[0]
    columns = select.shape[0]
    total = columns + beside.shape[1]
    block = 512
    placed = tuple((j, first) for _, j, first in parts)
    whole = lambda i, info: (0, 0)
    row = lambda i, info: (i, 0)
    return pl.pallas_call(
        functools.partial(qkv_grad_kernel, rows, placed),
        name="qkv_grads",
        grid_spec=pltpu.PrefetchScalarGridSpec(
            num_scalar_prefetch=1,
            grid=(depth // block,),
            in_specs=[anywhere()] * len(parts)
            + [
                pl.BlockSpec(d.shape, whole),
                pl.BlockSpec((block, w.shape[1]), row),
                pl.BlockSpec(select.shape, whole),
                pl.BlockSpec((block, beside.shape[1]), row),
            ],
            out_specs=[pl.BlockSpec((block, total), row), pl.BlockSpec((block, 1), row)],
            scratch_shapes=[
                pltpu.VMEM((length, depth), bf16),
                pltpu.SemaphoreType.DMA((len(parts),)),
            ],
        ),
        out_shape=[
            jax.ShapeDtypeStruct((depth, total), bf16),
            jax.ShapeDtypeStruct((depth, 1), f32),
        ],
        compiler_params=pltpu.CompilerParams(vmem_limit_bytes=VMEM),
        cost_estimate=SMALL,
    )(info, *[p for p, _, _ in parts], d, w, select, beside)


def finish_kernel(n, wide, info_ref, *refs):
    d = refs[:n]
    own_ref, cols_ref, tok_ref, gain_ref, dm_ref, o_ref = refs[n : n + 6]
    w_ref, sem = refs[-2:]
    t = info_ref[0]
    members, _, size, columns = cols_ref.shape
    depth = members * size
    first = pl.program_id(0) == 0
    copies = [
        pltpu.make_async_copy(cols_ref.at[:, j], w_ref.at[j], sem.at[j]) for j in range(n - 1)
    ]

    @pl.when(first)
    def _():
        for copy in copies:
            copy.start()

    o_ref[...] = dot_nt(d[0][...], own_ref[...])
    for j in range(n - 1):

        @pl.when(first)
        def _():
            copies[j].wait()

        o_ref[...] += dot_nt(d[j + 1][...], w_ref[j].reshape(depth, columns))
    x = tok_ref[...].astype(f32)
    inverse = lax.rsqrt(jnp.mean(x * x, axis=-1, keepdims=True) + EPS)
    unit = x * inverse
    e = o_ref[...] * gain_ref[...]
    inner = jnp.mean(e * unit, axis=-1, keepdims=True)
    o_ref[...] = dm_ref[...] + inverse * (e - unit * inner)
    if wide:
        first_ref = refs[n + 6]
        width = depth // n
        for j in range(n):
            at = pl.ds(pl.multiple_of((t ^ j) * width, width), width)
            first_ref[:, at] = d[j][:, 4 * LANES :].astype(f32)


def finish(info, d_parts, own, cols, tokens, gain, d_middle):
    n = len(d_parts)
    rows, depth = tokens.shape
    block = min(rows, 512)
    wide = (depth // n) % LANES == 0
    row = lambda i, info: (i, 0)
    whole = lambda i, info: (0, 0)
    count = 2 if wide else 1
    members, _, size, columns = cols.shape
    out = pl.pallas_call(
        functools.partial(finish_kernel, n, wide),
        name="finish",
        grid_spec=pltpu.PrefetchScalarGridSpec(
            num_scalar_prefetch=1,
            grid=(rows // block,),
            in_specs=[pl.BlockSpec((block, d.shape[1]), row) for d in d_parts]
            + [
                pl.BlockSpec(own.shape, whole),
                anywhere(),
                pl.BlockSpec((block, depth), row),
                pl.BlockSpec((1, depth), whole),
                pl.BlockSpec((block, depth), row),
            ],
            out_specs=[pl.BlockSpec((block, depth), row)] * count,
            scratch_shapes=[
                pltpu.VMEM((n - 1, members, size, columns), bf16),
                pltpu.SemaphoreType.DMA((n - 1,)),
            ],
        ),
        out_shape=[jax.ShapeDtypeStruct((rows, depth), f32)] * count,
        compiler_params=pltpu.CompilerParams(vmem_limit_bytes=VMEM),
        cost_estimate=LARGE,
    )(info, *d_parts, own, cols, tokens, gain, d_middle)
    if wide:
        return out
    heads_width = depth // n
    pieces_ = jnp.stack([d[:, 4 * LANES : 4 * LANES + heads_width] for d in d_parts])
    ordered = jnp.take(pieces_, info[0] ^ jnp.arange(n), axis=0)
    return out[0], ordered.transpose(1, 0, 2).reshape(rows, depth).astype(f32)


def shards(
    tokens,
    first_values,
    doc_lengths,
    attention_norm_gain,
    w_qkv,
    w_out,
    feedforward_norm_gain,
    w_gate,
    w_up,
    w_down,
    out_grad,
):
    n = lax.axis_size("tensor")
    high, low = split_axis(n)
    members = lax.axis_size("dp") // 2
    t = lax.axis_index("tensor")
    z, core = lax.axis_index("dp") // 2, lax.axis_index("dp") % 2
    info = jnp.stack([t, core]).astype(jnp.int32)
    rows, depth = tokens.shape
    heads = w_out.shape[0] // HD
    own_width = heads * HD
    width = max(LANES, own_width)
    length = rows * n
    block = min(256, rows)
    gain_one = attention_norm_gain[None, :]
    gain_two = feedforward_norm_gain[None, :]
    missing = width - own_width
    widen = lambda v: jnp.pad(v, ((0, 0), (0, missing))) if missing else v
    replicas = 2 * members
    size_d = depth // replicas
    mine = lambda w, axis: lax.dynamic_slice_in_dim(w, lax.axis_index("dp") * size_d, size_d, axis)

    together = lax.optimization_barrier
    cosine, sine_table = rope_tables(length)
    ends = jnp.cumsum(doc_lengths[0])
    starts = ends - doc_lengths[0]
    docs = doc_lengths.shape[1]
    limits = jnp.pad(jnp.stack([starts, ends]), ((0, 6), (HD, LANES - HD - docs)))
    heads_at = jnp.arange(length // block, dtype=jnp.int32) * block
    begins = jnp.max(jnp.where(starts[None, :] <= heads_at[:, None], starts[None, :], 0), axis=1)
    begins = (begins // block).astype(jnp.int32)
    select = column_selector(heads)
    w_cols = jnp.dot(w_qkv, select, preferred_element_type=f32).astype(bf16)

    own_weights = (w_gate.T, w_up.T, w_down)
    weight_slice = jnp.concatenate([mine(w, 1) for w in own_weights])
    value_parts = [
        widen(lax.dynamic_slice_in_dim(first_values, (t ^ j) * own_width, own_width, 1))
        for j in range(n)
    ]
    w_out_wide = jnp.pad(w_out, ((0, missing), (0, 0))) if missing else w_out
    out_slice = mine(w_out_wide, 1)
    normed = norm_rows(tokens, gain_one)
    value_parts, normed = together((value_parts, normed))
    normed_parts = gather_rows(normed, n)
    out_slices = [out_slice] + [swap("tensor", out_slice, j) for j in range(1, n)]
    w_out_all = over_replicas(jnp.concatenate(after(out_slices, normed)))
    value_parts = [value_parts[0]] + [swap("tensor", value_parts[j], j) for j in range(1, n)]
    placed = [(j, first) for _, j, first in normed_parts]
    pieces_in = [piece for piece, _, _ in normed_parts]
    cols_slice = mine(w_cols, 0)
    (
        pieces_in, value_parts, weight_slice, w_cols, cols_slice, cosine, sine_table, limits,
        grad_late, select,
    ) = together(
        (
            pieces_in, value_parts, weight_slice, w_cols, cols_slice, cosine, sine_table, limits,
            out_grad, select,
        )
    )

    far_slices = [swap("tensor", weight_slice, a * low) for a in range(1, high)]
    grad_rows = [out_grad] + [swap("tensor", grad_late, b) for b in range(1, low)]
    normed_parts = [(piece, j, first) for piece, (j, first) in zip(pieces_in, placed)]
    q, k, v, squares = project(
        heads, info, normed_parts, value_parts, w_cols, cosine, sine_table, limits, rows
    )
    q, far_slices, w_out_all = together((q, far_slices, w_out_all))
    seen = {}
    for j in range(n - 1, -1, -1):
        seen[j] = attend(heads, info, j, q, k, v, begins, block, rows)
        if j == 1:
            q, *grad_rows = together((q, *grad_rows))
    feed_far = [(over_replicas(w),) for w in far_slices]
    heads_rows = [seen[0][0]] + [swap("tensor", seen[j][0], j) for j in range(1, n)]
    heads_rows, cols_slice = together((heads_rows, cols_slice))

    parts = 2 if rows >= 512 else 1
    size = rows // parts
    middle, second, w_out_all, *second_parts = branch(
        info, heads_rows, w_out_all, tokens, gain_two, parts
    )
    second_parts, cols_slice = together((second_parts, cols_slice))
    far_keys = [(b, p) for b in range(1, low) for p in range(parts)]
    inputs = {(b, p): swap("tensor", second_parts[p], b) for b, p in far_keys}
    cols_far = [swap("tensor", cols_slice, j) for j in range(1, n)]
    shards_held = [own_weights] + feed_far
    own_out, own_back, act = feed(
        info, second, out_grad, 0, shards_held, 0, low * rows, [], 0, rows, False
    )
    shared, backs = [act], {}
    for b, p in far_keys:
        if (b, p) == far_keys[0]:
            inputs, shared = together((inputs, shared))
        if (b, p) == far_keys[-1]:
            cols_far, shared = together((cols_far, shared))
        arrived = inputs[b, p]
        to_send, backs[b, p], act = feed(
            info, arrived, grad_rows[b], p * size, shards_held, b * rows + p * size, low * rows,
            shared, (b - 1) * rows + p * size, (low - 1) * rows, True,
        )
        shared = [to_send, act]
    d_far = [[swap("tensor", backs[b, p], b) for b in range(1, low)] for p in range(parts)]
    d_far = [d[0] if low == 2 else add_up(*d) for d in d_far]
    sources = (
        [second] + [inputs[key] for key in far_keys],
        [0] + [b * rows + p * size for b, p in far_keys],
        grad_rows,
        [b * rows for b in range(low)],
    )
    d_far[0], act = together((d_far[0], act))
    cols = lax.all_gather(jnp.stack(cols_far), "dp", axis=0)
    wanted = [(a, m) for a in range(1, high) for m in range(3)] + [(0, 0), (0, 1), (0, 2)]
    keep, send = feed_grads(info, *sources, act, wanted, members)
    d_far, keep, send, to_send = together((d_far, keep, send, to_send))

    got = swap("dp", send, 1)
    d_middle, d_branch, feed_share, *d_att = branch_back(
        info, own_back, d_far, middle, out_grad, gain_two, w_out_all, width
    )
    d_att = [d_att[0]] + [swap("tensor", d_att[j], j) for j in range(1, n)]
    add_two = lambda lo, hi: add_up(keep[lo:hi], got[lo:hi]).astype(bf16)
    rest_sums = [add_two(3 * a + 1, 3 * a + 3) for a in range(high - 1)]
    rest_sums, got = together((rest_sums, got))
    gate_sums = jnp.stack(
        [add_two(i, i + 1)[0] for i in [3 * (high - 1)] + [3 * a for a in range(high - 1)]], axis=1
    )
    out_grad_w = out_grads(info, d_branch, heads_rows)
    d_att, to_send, out_grad_w, keep, got, cols = together(
        (d_att, to_send, out_grad_w, keep, got, cols)
    )

    gate_z = [
        swap("dp", lax.dynamic_index_in_dim(gate_sums, z ^ k, 0, keepdims=False), 2 * k)
        for k in range(1, members)
    ]
    rest_got = [swap("tensor", rest_sums[a - 1], a * low) for a in range(1, high)]
    out_got = [swap("tensor", to_send[(b - 1) * rows : b * rows], b) for b in range(1, low)]
    out_sum = lax.psum_scatter(out_grad_w, "tensor", scatter_dimension=0, tiled=False)
    d_cols = attend_back(
        heads, info, [seen[j][1] for j in range(n)], k, v, d_att, [seen[j][0] for j in range(n)],
        cosine, sine_table, begins, block,
    )
    d_cols, gate_z, out_got, keep = together((d_cols, gate_z, out_got, keep))

    d_all, *d_parts = d_cols
    rest_sum = add_up(keep[-2:], got[-2:], *rest_got).astype(bf16).swapaxes(0, 1)
    d_all, rest_sum = together((d_all, rest_sum))
    d_parts = [d_parts[0]] + [swap("tensor", d_parts[j], j) for j in range(1, n)]
    grads, share = qkv_grads(info, normed_parts, d_all, w_cols, select, out_sum, rows)
    grads = lax.psum_scatter(grads, "dp", scatter_dimension=0, tiled=True)
    gate_z, out_got, share = together((gate_z, out_got, share))
    step = 1
    if members > 1:
        rest_sum = halve_over_z(rest_sum, z, step, lambda half: after(half, share))
    gate_sum = add_up(
        lax.dynamic_index_in_dim(gate_sums, z, 0, keepdims=False), *gate_z
    ).astype(bf16)
    gate_sum = add_up(
        gate_sum[0], *[swap("tensor", gate_sum[a], a * low) for a in range(1, high)]
    )
    out = add_up(middle, own_out, *out_got).astype(bf16)
    totals = jnp.sum(squares[:2], axis=1)
    scalars = jnp.pad(totals[None, :], ((0, 0), (0, depth - 2)))
    shares = jnp.concatenate([share.reshape(1, depth) / gain_one, feed_share, scalars])
    d_parts, out, rest_sum = together((d_parts, out, rest_sum))
    while 2 * step < members:
        step *= 2
        rest_sum = halve_over_z(rest_sum, z, step, lambda half: half)
    rest_sum = rest_sum[0].astype(f32)
    tokens_grad, first_grad = finish(
        info, d_parts, w_cols, cols, tokens, gain_one, d_middle
    )
    shares, tokens_grad, rest_sum = together((shares, tokens_grad, rest_sum))
    sums = all_sum("dp", shares, [1])
    sums = all_sum("dp", sums, range(2, 2 * members, 2))
    sums = all_sum("tensor", sums, range(1, n))
    columns = 3 * own_width
    entry_count = first_values.size * lax.axis_size("dp") * n
    return (
        out,
        tokens_grad,
        first_grad,
        sums[0],
        grads[:, :columns].astype(f32),
        grads[:, columns : columns + own_width].T.astype(f32),
        sums[1],
        gate_sum.T,
        rest_sum[0].T,
        rest_sum[1],
        jnp.sqrt(sums[2, 1] / entry_count),
        jnp.sqrt(sums[2, 0] / entry_count),
    )


def solution(mesh):
    token_spec = P(("dp", "tensor"), None)
    return jax.shard_map(
        shards,
        mesh=mesh,
        in_specs=(
            token_spec,
            token_spec,
            P("dp", None),
            P(),
            P(None, "tensor"),
            P("tensor", None),
            P(),
            P(None, "tensor"),
            P(None, "tensor"),
            P("tensor", None),
            token_spec,
        ),
        out_specs=(
            token_spec,
            token_spec,
            token_spec,
            P(),
            P("dp", "tensor"),
            P("tensor", "dp"),
            P(),
            P("dp", "tensor"),
            P("dp", "tensor"),
            P("tensor", "dp"),
            P(),
            P(),
        ),
        check_vma=False,
    )
```

```python
import functools
import math

import jax
import jax.numpy as jnp
import numpy as np
from jax import lax
from jax.experimental import pallas as pl
from jax.experimental.pallas import tpu as pltpu
from jax.sharding import PartitionSpec as P

HD = 64
HALF = HD // 2
LANES = 128
GROUP = LANES // HALF
EPS = 1e-06
NEG = -1e30
VMEM = 60 << 20
SMALL = pl.CostEstimate(flops=1, bytes_accessed=1, transcendentals=0)
LARGE = pl.CostEstimate(flops=10**11, bytes_accessed=1, transcendentals=0)
f32 = jnp.float32
bf16 = jnp.bfloat16


def rope_tables(length):
    inverse = jnp.exp(-math.log(10000.0) * jnp.arange(HALF, dtype=f32) / HALF)
    angles = jnp.arange(length, dtype=f32)[:, None] * inverse[None, :]
    tile = lambda t: jnp.concatenate([t] * GROUP, axis=1)
    return tile(jnp.cos(angles)), tile(jnp.sin(angles))


def column_order(heads):
    value_width = max(LANES, heads * HD)
    order = np.full((4 * LANES + value_width,), -1, np.int32)
    for h in range(heads):
        for part in range(2):
            for half in range(2):
                at = (2 * part + half) * LANES + h * HALF
                src = h * 3 * HD + part * HD + half * HALF
                order[at : at + HALF] = np.arange(src, src + HALF)
        order[4 * LANES + h * HD : 4 * LANES + (h + 1) * HD] = np.arange(
            h * 3 * HD + 2 * HD, (h + 1) * 3 * HD
        )
    return order


def column_selector(heads):
    order = jnp.asarray(column_order(heads))
    rows = jnp.arange(3 * heads * HD, dtype=jnp.int32)
    return (rows[:, None] == order[None, :]).astype(bf16)


def dot_nt(a, b):
    return lax.dot_general(a, b, (((1,), (1,)), ((), ())), preferred_element_type=f32)


def dot_tn(a, b):
    return lax.dot_general(a, b, (((0,), (0,)), ((), ())), preferred_element_type=f32)


def dot_nn(a, b):
    return jnp.dot(a, b, preferred_element_type=f32)


def anywhere():
    return pl.BlockSpec(memory_space=pl.ANY)


def project_kernel(heads, placed, info_ref, *refs):
    count = len(placed)
    n = len({j for j, _ in placed})
    pieces, values = refs[:count], refs[count : count + n]
    w_ref, cos_ref, sin_ref, lim_ref = refs[count + n : count + n + 4]
    q_ref, k_ref, v_ref, sq_ref, x_ref, fv_ref, sem = refs[count + n + 4 :]
    at = pl.program_id(0)
    block = q_ref.shape[0]
    copies = []
    for i, (ref, (j, first)) in enumerate(zip(pieces, placed)):
        into = x_ref.at[j, first : first + ref.shape[0]]
        copies.append((j, pltpu.make_async_copy(ref, into, sem.at[i])))
    for j, ref in enumerate(values):
        copies.append((j, pltpu.make_async_copy(ref, fv_ref.at[j], sem.at[count + j])))

    @pl.when(at == 0)
    def _():
        sq_ref[...] = jnp.zeros_like(sq_ref)
        for _, copy in copies:
            copy.start()

    for j in range(n):

        @pl.when(at == j)
        def _():
            for owner, copy in copies:
                if owner == j:
                    copy.wait()

    acc = dot_nn(x_ref[at], w_ref[...])
    c, s = cos_ref[...], sin_ref[...]
    lane = lax.broadcasted_iota(jnp.int32, (block, LANES), 1)
    place = (info_ref[0] ^ at) * block + lax.broadcasted_iota(jnp.int32, (block, LANES), 0)
    inside = (place >= lim_ref[0:1, :]) & (place < lim_ref[1:2, :])
    doc_lane = (lane >= HD) & (lane < HD + 8)
    q_extra = jnp.where(doc_lane & jnp.logical_not(inside), NEG, 0.0)
    k_extra = jnp.where(inside, 1.0, jnp.where((lane >= HD + 8) & (lane < HD + 11), 1.0, 0.0))
    for ref, base, extra, scale in ((q_ref, 0, q_extra, HD**-0.5), (k_ref, 2, k_extra, 1.0)):
        u1 = acc[:, base * LANES : (base + 1) * LANES]
        u2 = acc[:, (base + 1) * LANES : (base + 2) * LANES]
        r1 = (u1 * c - u2 * s) * scale
        r2 = (u1 * s + u2 * c) * scale
        for h in range(heads):
            a = r1 if h == 0 else pltpu.roll(r1, LANES - HALF * h, 1)
            b = r2 if h == 1 else pltpu.roll(r2, (LANES + HALF - HALF * h) % LANES, 1)
            both = jnp.where(lane < HALF, a, jnp.where(lane < HD, b, extra))
            ref[:, h * LANES : (h + 1) * LANES] = both.astype(bf16)
    first = fv_ref[at].astype(f32)
    mixed = 0.5 * acc[:, 4 * LANES :] + 0.5 * first
    sq_ref[0:1, :] += jnp.sum(mixed * mixed, axis=0, keepdims=True)
    sq_ref[1:2, :] += jnp.sum(first * first, axis=0, keepdims=True)
    for h in range(heads):
        t = (h // 2) * LANES
        own = (lane < HD) if h % 2 == 0 else (lane >= HD)
        v_ref[:, h * LANES : (h + 1) * LANES] = jnp.where(
            own, mixed[:, t : t + LANES], 1.0
        ).astype(bf16)


def project(heads, info, parts, values, w, cos, sin, limits, rows):
    n = len(values)
    length = rows * n
    depth = parts[0][0].shape[1]
    width = values[0].shape[1]
    row = lambda i, info: (info[0] ^ i, 0)
    whole = lambda i, info: (0, 0)
    ext = heads * LANES
    placed = tuple((j, first) for _, j, first in parts)
    return pl.pallas_call(
        functools.partial(project_kernel, heads, placed),
        name="project",
        grid_spec=pltpu.PrefetchScalarGridSpec(
            num_scalar_prefetch=1,
            grid=(n,),
            in_specs=[anywhere()] * (len(parts) + n)
            + [
                pl.BlockSpec(w.shape, whole),
                pl.BlockSpec((rows, LANES), row),
                pl.BlockSpec((rows, LANES), row),
                pl.BlockSpec((8, LANES), whole),
            ],
            out_specs=[
                pl.BlockSpec((rows, ext), row),
                pl.BlockSpec((rows, ext), row),
                pl.BlockSpec((rows, ext), row),
                pl.BlockSpec((8, width), whole),
            ],
            scratch_shapes=[
                pltpu.VMEM((n, rows, depth), bf16),
                pltpu.VMEM((n, rows, width), bf16),
                pltpu.SemaphoreType.DMA((len(parts) + n,)),
            ],
        ),
        out_shape=[jax.ShapeDtypeStruct((length, ext), bf16)] * 3
        + [jax.ShapeDtypeStruct((8, width), f32)],
        compiler_params=pltpu.CompilerParams(vmem_limit_bytes=VMEM),
        cost_estimate=SMALL,
    )(info, *[p for p, _, _ in parts], *values, w, cos, sin, limits)


def pieces(x):
    hi = x.astype(bf16).astype(f32)
    mid = (x - hi).astype(bf16).astype(f32)
    return hi, mid, x - hi - mid


def attend_kernel(
    heads, offset, bk, info_ref, begin_ref, q_ref, k_ref, v_ref, o_ref, qo_ref, m_ref, acc_ref
):
    bq = q_ref.shape[0]
    at = info_ref[0] ^ offset
    lane = lax.broadcasted_iota(jnp.int32, (bq, LANES), 1)
    r = lax.broadcasted_iota(jnp.int32, (bq, bk), 0)
    c = lax.broadcasted_iota(jnp.int32, (bq, bk), 1)
    col = [slice(h * LANES, (h + 1) * LANES) for h in range(heads)]
    spread = lambda m: jnp.concatenate([m] * (bk // LANES), axis=1)

    def visit(kb, mask, first):
        there = pl.ds(pl.multiple_of(kb * bk, bk), bk)
        for h in range(heads):
            s = dot_nt(q_ref[:, col[h]], k_ref[there, col[h]])
            if mask is not None:
                s = jnp.where(mask, s, NEG)
            new = jnp.broadcast_to(jnp.max(s, axis=1, keepdims=True), (bq, LANES))
            if not first:
                old = m_ref[:, col[h]]
                new = jnp.maximum(old, new)
            p = jnp.exp(s - spread(new)).astype(bf16)
            part = dot_nn(p, v_ref[there, col[h]])
            m_ref[:, col[h]] = new
            acc_ref[:, col[h]] = part if first else acc_ref[:, col[h]] * jnp.exp(old - new) + part

    for d in range(bq // bk):
        visit(at * (bq // bk) + d, c + d * bk <= r, d == 0)

    def step(kb, carry):
        visit(kb, None, False)
        return carry

    lax.fori_loop(begin_ref[at * (bq // bk)], at * (bq // bk), step, 0)
    low = lane < HD
    for t in range((heads + 1) // 2):
        a = acc_ref[:, col[2 * t]]
        b = acc_ref[:, col[2 * t + 1]] if 2 * t + 1 < heads else a
        total = pltpu.roll(jnp.where(low, b, a), HD, 1)
        result = jnp.where(low, a, b) / total
        if 2 * t + 1 >= heads:
            result = jnp.where(low, result, 0.0)
        o_ref[:, t * LANES : (t + 1) * LANES] = result.astype(bf16)
    for h in range(heads):
        a = acc_ref[:, col[h]]
        total = a if h % 2 == 0 else pltpu.roll(a, HD, 1)
        hi, mid, lo = pieces(-(m_ref[:, col[h]] + jnp.log(jnp.where(low, 1.0, total))))
        extra = jnp.where(
            lane == HD + 8, hi, jnp.where(lane == HD + 9, mid, jnp.where(lane == HD + 10, lo, 0.0))
        )
        fill = (lane >= HD + 8) & (lane < HD + 11)
        qo_ref[:, col[h]] = jnp.where(fill, extra, q_ref[:, col[h]].astype(f32)).astype(bf16)


def attend(heads, info, offset, q, k, v, begins, block, rows):
    length = q.shape[0]
    ext = heads * LANES
    width = max(LANES, heads * HD)
    whole = lambda i, info, b: (0, 0)
    return pl.pallas_call(
        functools.partial(attend_kernel, heads, offset, block),
        name="attend",
        grid_spec=pltpu.PrefetchScalarGridSpec(
            num_scalar_prefetch=2,
            grid=(1,),
            in_specs=[
                pl.BlockSpec((rows, ext), lambda i, info, b: (info[0] ^ offset, 0)),
                pl.BlockSpec((length, ext), whole),
                pl.BlockSpec((length, ext), whole),
            ],
            out_specs=[pl.BlockSpec((rows, width), whole), pl.BlockSpec((rows, ext), whole)],
            scratch_shapes=[pltpu.VMEM((rows, ext), f32), pltpu.VMEM((rows, ext), f32)],
        ),
        out_shape=[
            jax.ShapeDtypeStruct((rows, width), bf16),
            jax.ShapeDtypeStruct((rows, ext), bf16),
        ],
        compiler_params=pltpu.CompilerParams(vmem_limit_bytes=VMEM),
        cost_estimate=SMALL,
    )(info, begins, q, k, v)


def attend_back_kernel(heads, block, n, info_ref, begin_ref, *refs):
    q_parts, do_parts, o_parts = refs[:n], refs[n : 2 * n], refs[2 * n : 3 * n]
    k_ref, v_ref, cos_ref, sin_ref, g_ref = refs[3 * n : 3 * n + 5]
    sends = refs[3 * n + 5 : 4 * n + 5]
    q_all, do_all, o_all, dk_ref, dv_ref, dq_ref, de_ref, sem = refs[4 * n + 5 :]
    at = pl.program_id(0)
    rows = q_parts[0].shape[0]

    def moves(pairs):
        copies = []
        for i, (make, j) in enumerate(pairs):
            place = pl.ds(pl.multiple_of((info_ref[0] ^ j) * rows, rows), rows)
            copies.append(make(place, sem.at[i]))
        for copy in copies:
            copy.start()
        for copy in copies:
            copy.wait()

    @pl.when(at == 0)
    def _():
        moves(
            [
                (functools.partial(lambda src, dst, p, s: pltpu.make_async_copy(src, dst.at[p], s), part, whole), j)
                for parts, whole in ((q_parts, q_all), (do_parts, do_all), (o_parts, o_all))
                for j, part in enumerate(parts)
            ]
        )

    lane = lax.broadcasted_iota(jnp.int32, (block, LANES), 1)
    r = lax.broadcasted_iota(jnp.int32, (block, block), 0)
    c = lax.broadcasted_iota(jnp.int32, (block, block), 1)
    causal = r <= c
    low = lane < HD
    here = pl.ds(pl.multiple_of(at * block, block), block)
    col = [slice(h * LANES, (h + 1) * LANES) for h in range(heads)]

    for h in range(heads):
        t = slice((h // 2) * LANES, (h // 2 + 1) * LANES)
        own = low if h % 2 == 0 else jnp.logical_not(low)
        grad = do_all[here, t].astype(f32)
        product = grad * o_all[here, t].astype(f32)
        centre = jnp.sum(jnp.where(own, product, 0.0), axis=1, keepdims=True)
        hi, mid, lo = pieces(-jnp.broadcast_to(centre, (block, LANES)))
        spot = lane - (HD if h % 2 == 0 else 0)
        extra = jnp.where(spot == 0, hi, jnp.where(spot == 1, mid, jnp.where(spot == 2, lo, 0.0)))
        de_ref[:, col[h]] = jnp.where(own, grad, extra).astype(bf16)

    def visit(there, mask, first):
        st = [dot_nt(k_ref[there, c_], q_all[here, c_]) for c_ in col]
        dpt = [dot_nt(v_ref[there, c_], de_ref[:, c_]) for c_ in col]
        p = [jnp.exp(s) for s in st]
        if mask is not None:
            p = [jnp.where(mask, x, 0.0) for x in p]
        ds = [(x * y).astype(bf16) for x, y in zip(p, dpt)]
        p = [x.astype(bf16) for x in p]
        for h, c_ in enumerate(col):
            dv = dot_nn(p[h], de_ref[:, c_])
            dk = dot_nn(ds[h], q_all[here, c_])
            dq = dot_tn(ds[h], k_ref[there, c_])
            if first:
                dv_ref[there, c_] = dv
                dk_ref[there, c_] = dk
                dq_ref[:, c_] = dq
            else:
                dv_ref[there, c_] += dv
                dk_ref[there, c_] += dk
                dq_ref[:, c_] += dq

    visit(here, causal, True)

    def step(kb, carry):
        visit(pl.ds(pl.multiple_of(kb * block, block), block), None, False)
        return carry

    lax.fori_loop(begin_ref[at], at, step, 0)

    def turn_back(ref, rows, scale):
        u1 = u2 = None
        quarter = lane // HALF
        for h in range(heads):
            u = ref[rows, col[h]]
            a = u if h == 0 else pltpu.roll(u, HALF * h, 1)
            b = u if h == 1 else pltpu.roll(u, (LANES + HALF * h - HALF) % LANES, 1)
            u1 = a if h == 0 else jnp.where(quarter == h, a, u1)
            u2 = b if h == 0 else jnp.where(quarter == h, b, u2)
        if heads < GROUP:
            u1 = jnp.where(quarter < heads, u1, 0.0)
            u2 = jnp.where(quarter < heads, u2, 0.0)
        u1, u2 = u1 * scale, u2 * scale
        cs, sn = cos_ref[rows, :], sin_ref[rows, :]
        return (u1 * cs + u2 * sn).astype(bf16), (u2 * cs - u1 * sn).astype(bf16)

    def finish_block(i, carry):
        rows = pl.ds(pl.multiple_of(i * block, block), block)
        d1, d2 = turn_back(dk_ref, rows, 1.0)
        g_ref[rows, 2 * LANES : 3 * LANES] = d1
        g_ref[rows, 3 * LANES : 4 * LANES] = d2
        for t in range((heads + 1) // 2):
            a = dv_ref[rows, col[2 * t]]
            b = dv_ref[rows, col[2 * t + 1]] if 2 * t + 1 < heads else jnp.zeros_like(a)
            d_mix = jnp.where(low, a, b).astype(bf16)
            g_ref[rows, (4 + t) * LANES : (5 + t) * LANES] = (d_mix.astype(f32) * 0.5).astype(bf16)
        return carry

    u1 = u2 = None
    quarter = lane // HALF
    for h in range(heads):
        u = dq_ref[:, col[h]]
        a = u if h == 0 else pltpu.roll(u, HALF * h, 1)
        b = u if h == 1 else pltpu.roll(u, (LANES + HALF * h - HALF) % LANES, 1)
        u1 = a if h == 0 else jnp.where(quarter == h, a, u1)
        u2 = b if h == 0 else jnp.where(quarter == h, b, u2)
    if heads < GROUP:
        u1 = jnp.where(quarter < heads, u1, 0.0)
        u2 = jnp.where(quarter < heads, u2, 0.0)
    u1, u2 = u1 * HD**-0.5, u2 * HD**-0.5
    cs, sn = cos_ref[here, :], sin_ref[here, :]
    g_ref[here, 0:LANES] = (u1 * cs + u2 * sn).astype(bf16)
    g_ref[here, LANES : 2 * LANES] = (u2 * cs - u1 * sn).astype(bf16)

    @pl.when(at == pl.num_programs(0) - 1)
    def _():
        lax.fori_loop(0, pl.num_programs(0), finish_block, 0)
        moves(
            [
                (functools.partial(lambda dst, p, s: pltpu.make_async_copy(g_ref.at[p], dst, s), dst), j)
                for j, dst in enumerate(sends)
            ]
        )


def attend_back(heads, info, q_parts, k, v, do_parts, o_parts, cos, sin, begins, block):
    n = len(q_parts)
    rows = q_parts[0].shape[0]
    length = n * rows
    ext = heads * LANES
    width = o_parts[0].shape[1]
    whole = lambda i, info, b: (0, 0)
    anywhere = pl.BlockSpec(memory_space=pl.ANY)
    columns = 4 * LANES + width
    return pl.pallas_call(
        functools.partial(attend_back_kernel, heads, block, n),
        name="attend_back",
        grid_spec=pltpu.PrefetchScalarGridSpec(
            num_scalar_prefetch=2,
            grid=(length // block,),
            in_specs=[anywhere] * (3 * n)
            + [
                pl.BlockSpec((length, ext), whole),
                pl.BlockSpec((length, ext), whole),
                pl.BlockSpec((length, LANES), whole),
                pl.BlockSpec((length, LANES), whole),
            ],
            out_specs=[pl.BlockSpec((length, columns), whole)] + [anywhere] * n,
            scratch_shapes=[
                pltpu.VMEM((length, ext), bf16),
                pltpu.VMEM((length, width), bf16),
                pltpu.VMEM((length, width), bf16),
                pltpu.VMEM((length, ext), f32),
                pltpu.VMEM((length, ext), f32),
                pltpu.VMEM((block, ext), f32),
                pltpu.VMEM((block, ext), bf16),
                pltpu.SemaphoreType.DMA((3 * n,)),
            ],
        ),
        out_shape=[jax.ShapeDtypeStruct((length, columns), bf16)]
        + [jax.ShapeDtypeStruct((rows, columns), bf16)] * n,
        compiler_params=pltpu.CompilerParams(vmem_limit_bytes=VMEM),
        cost_estimate=LARGE,
    )(info, begins, *q_parts, *do_parts, *o_parts, k, v, cos, sin)


def split_axis(n):
    low = 1 << ((n.bit_length() - 1) // 2)
    return n // low, low


def swap(axis, value, offset):
    n = lax.axis_size(axis)
    return lax.ppermute(value, axis, [(i, i ^ offset) for i in range(n)])


def gather_rows(value, n):
    high, low = split_axis(n)
    rows = value.shape[0]
    half = rows // 2
    parts = {0: value}
    for b in range(1, low):
        parts[b] = swap("tensor", value, b)
    for a in range(1, high):
        parts[a * low] = swap("tensor", value, a * low)
    listed = [(parts[j], j, 0) for j in sorted(parts)]
    for a in range(1, high):
        for b in range(1, low):
            j = a * low + b
            listed.append((swap("tensor", parts[b][:half], a * low), j, 0))
            listed.append((swap("tensor", parts[a * low][half:], b), j, half))
    return listed


def after(value, *others):
    return lax.optimization_barrier((value,) + others)[0]


def add_up(first, *others):
    total = first.astype(f32)
    for other in others:
        total = total + other.astype(f32)
    return total


def over_replicas(value):
    if value.shape[1] % LANES == 0:
        return lax.all_gather(value, "dp", axis=0)
    return lax.all_gather(value, "dp", axis=1, tiled=True)


def halve_over_z(parts, z, step, hold):
    pairs = parts.reshape((-1, 2) + parts.shape[1:])
    side = (z // step) % 2
    pick = lambda which: lax.dynamic_index_in_dim(pairs, which, 1, keepdims=False)
    parts = add_up(pick(side), hold(swap("dp", pick(1 - side), 2 * step)))
    return parts.astype(bf16) if parts.shape[0] > 1 else parts


def all_sum(axis, value, offsets):
    parts = [value] + [swap(axis, value, j) for j in offsets]
    while len(parts) > 1:
        parts = [a + b for a, b in zip(parts[::2], parts[1::2])]
    return parts[0]


def norm_kernel(x_ref, gain_ref, o_ref):
    x = x_ref[...].astype(f32)
    inverse = lax.rsqrt(jnp.mean(x * x, axis=-1, keepdims=True) + EPS)
    o_ref[...] = (x * inverse * gain_ref[...]).astype(bf16)


def norm_rows(x, gain):
    rows, depth = x.shape
    block = min(rows, 128)
    return pl.pallas_call(
        norm_kernel,
        name="norm_rows",
        grid=(rows // block,),
        in_specs=[
            pl.BlockSpec((block, depth), lambda i: (i, 0)),
            pl.BlockSpec((1, depth), lambda i: (0, 0)),
        ],
        out_specs=pl.BlockSpec((block, depth), lambda i: (i, 0)),
        out_shape=jax.ShapeDtypeStruct((rows, depth), bf16),
        compiler_params=pltpu.CompilerParams(vmem_limit_bytes=VMEM),
        cost_estimate=SMALL,
    )(x, gain)


def branch_kernel(n, parts, info_ref, *refs):
    att = refs[:n]
    slices_ref, tok_ref, gain_ref, mid_ref, h_ref, w_ref = refs[n : n + 6]
    h_parts = refs[n + 6 : n + 6 + parts]
    all_ref, sem, w_sem = refs[n + 6 + parts :]
    at = pl.program_id(0)
    size = tok_ref.shape[0]
    width = att[0].shape[1]

    @pl.when(at == 0)
    def _():
        copies = [
            pltpu.make_async_copy(
                att[j], all_ref.at[:, j * width : (j + 1) * width], sem.at[j]
            )
            for j in range(n)
        ]
        if len(slices_ref.shape) == 3:
            lanes = slices_ref.shape[2]
            copies += [
                pltpu.make_async_copy(
                    slices_ref.at[d], w_ref.at[:, d * lanes : (d + 1) * lanes], w_sem.at[d]
                )
                for d in range(slices_ref.shape[0])
            ]
        else:
            copies.append(pltpu.make_async_copy(slices_ref, w_ref, w_sem.at[0]))
        for copy in copies:
            copy.start()
        for copy in copies:
            copy.wait()

    here = pl.ds(pl.multiple_of(at * size, size), size)
    x = tok_ref[...].astype(f32) + dot_nn(all_ref[here, :], w_ref[...])
    mid_ref[...] = x
    inverse = lax.rsqrt(jnp.mean(x * x, axis=-1, keepdims=True) + EPS)
    h = (x * inverse * gain_ref[...]).astype(bf16)
    h_ref[...] = h
    for p in range(parts):

        @pl.when(at == p)
        def _():
            h_parts[p][...] = h


def branch(info, att, w_slices, tokens, gain, parts):
    n = len(att)
    rows, width = att[0].shape
    depth = tokens.shape[1]
    size = rows // parts
    whole = lambda i, info: (0, 0)
    row = lambda i, info: (i, 0)
    count = w_slices.shape[0] if w_slices.ndim == 3 else 1
    return pl.pallas_call(
        functools.partial(branch_kernel, n, parts),
        name="branch",
        grid_spec=pltpu.PrefetchScalarGridSpec(
            num_scalar_prefetch=1,
            grid=(parts,),
            in_specs=[anywhere()] * (n + 1)
            + [pl.BlockSpec((size, depth), row), pl.BlockSpec((1, depth), whole)],
            out_specs=[pl.BlockSpec((size, depth), row)] * 2
            + [pl.BlockSpec((n * width, depth), whole)]
            + [pl.BlockSpec((size, depth), whole)] * parts,
            scratch_shapes=[
                pltpu.VMEM((rows, n * width), bf16),
                pltpu.SemaphoreType.DMA((n,)),
                pltpu.SemaphoreType.DMA((count,)),
            ],
        ),
        out_shape=[
            jax.ShapeDtypeStruct((rows, depth), f32),
            jax.ShapeDtypeStruct((rows, depth), bf16),
            jax.ShapeDtypeStruct((n * width, depth), bf16),
        ]
        + [jax.ShapeDtypeStruct((size, depth), bf16)] * parts,
        compiler_params=pltpu.CompilerParams(vmem_limit_bytes=VMEM),
        cost_estimate=SMALL,
    )(info, *att, w_slices, tokens, gain)


def feed_kernel(shards_in, shared, send, act_first, info_ref, h_ref, g_ref, *refs):
    count = sum(shards_in)
    weights, refs = refs[:count], refs[count + shared :]
    out_ref, dh_ref, act_out, w_ref, sem, act_ref, act_sem = refs[:7]
    out_acc, dh_acc = refs[7:] if send else (out_ref, dh_ref)
    high, rows_w, depth = w_ref.shape
    units = rows_w // 3
    copies, at, used = [], 0, 0
    for a, pieces_in in enumerate(shards_in):
        groups = []
        for m in range(3):
            span = pl.ds(m * units, units)
            ref = weights[at + m] if pieces_in == 3 else weights[at]
            if pieces_in == 3:
                moves = [(ref, w_ref.at[a, span])]
            elif len(ref.shape) == 3:
                size = ref.shape[2]
                moves = [
                    (ref.at[d, span], w_ref.at[a, span, d * size : (d + 1) * size])
                    for d in range(ref.shape[0])
                ]
            else:
                moves = [(ref.at[span], w_ref.at[a, span])]
            groups.append(
                [
                    pltpu.make_async_copy(src, dst, sem.at[used + i])
                    for i, (src, dst) in enumerate(moves)
                ]
            )
            used += len(moves)
        at += pieces_in
        copies.append(groups)
    for groups in copies:
        for group in groups:
            for copy in group:
                copy.start()

    rows = h_ref.shape[0]
    out_acc[...] = jnp.zeros_like(out_acc)
    dh_acc[...] = jnp.zeros_like(dh_acc)

    def leave(a):
        to = act_out.at[a, :, act_first : act_first + rows]
        return pltpu.make_async_copy(act_ref.at[a], to, act_sem.at[a])

    def shard(a, carry):
        def weight(m):
            for k in range(high):

                @pl.when(a == k)
                def _():
                    for copy in copies[k][m]:
                        copy.wait()

            return w_ref[a, m * units : (m + 1) * units, :]

        gate = dot_nt(h_ref[...], weight(0))
        up = dot_nt(h_ref[...], weight(1))
        back = dot_nt(g_ref[...], weight(2))
        s = 0.5 * jnp.tanh(0.5 * gate) + 0.5
        gs = gate * s
        hidden = (gs * up).astype(bf16)
        d_up = (back * gs).astype(bf16)
        d_gate = (back * up * (s + gs * (1.0 - s))).astype(bf16)
        act_ref[a, 0] = d_gate
        act_ref[a, 1] = d_up
        act_ref[a, 2] = hidden
        leave(a).start()
        gate_w, up_w, down_w = (w_ref[a, m * units : (m + 1) * units, :] for m in range(3))
        dh_acc[...] += dot_nn(d_gate, gate_w) + dot_nn(d_up, up_w)
        out_acc[...] += dot_nn(hidden, down_w)
        return carry

    lax.fori_loop(0, high, shard, 0)
    if send:
        out_ref[...] = out_acc[...].astype(bf16)
        dh_ref[...] = dh_acc[...].astype(bf16)
    for a in range(high):
        leave(a).wait()


def feed(info, h, g, g_first, weights, act_first, act_rows, shared, out_first, out_rows, send):
    rows, depth = h.shape
    high = len(weights)
    flat = [w for shard in weights for w in shard]
    units = weights[0][0].shape[0] if len(weights[0]) == 3 else weights[0][0].shape[-2] // 3
    block = rows
    at, out_at = g_first // block, out_first // block
    row = lambda i, info: (i, 0)
    kind = bf16 if send else f32
    moves = sum(
        3 if len(shard) == 3 else 3 * (shard[0].shape[0] if shard[0].ndim == 3 else 1)
        for shard in weights
    )
    base = 3 + len(flat)
    aliases = {} if not shared else {base: 2} if len(shared) == 1 else {base: 0, base + 1: 2}
    return pl.pallas_call(
        functools.partial(
            feed_kernel, tuple(len(shard) for shard in weights), len(shared), send, act_first
        ),
        name="feed",
        grid_spec=pltpu.PrefetchScalarGridSpec(
            num_scalar_prefetch=1,
            grid=(1,),
            in_specs=[
                pl.BlockSpec((block, depth), row),
                pl.BlockSpec((block, depth), lambda i, info: (at, 0)),
            ]
            + [anywhere()] * (len(flat) + len(shared)),
            out_specs=[
                pl.BlockSpec((block, depth), lambda i, info: (out_at, 0)),
                pl.BlockSpec((block, depth), row),
                anywhere(),
            ],
            scratch_shapes=[
                pltpu.VMEM((high, 3 * units, depth), bf16),
                pltpu.SemaphoreType.DMA((moves,)),
                pltpu.VMEM((high, 3, block, units), bf16),
                pltpu.SemaphoreType.DMA((high,)),
            ]
            + ([pltpu.VMEM((block, depth), f32)] * 2 if send else []),
        ),
        out_shape=[
            jax.ShapeDtypeStruct((out_rows, depth), kind),
            jax.ShapeDtypeStruct((rows, depth), kind),
            jax.ShapeDtypeStruct((high, 3, act_rows, units), bf16),
        ],
        input_output_aliases=aliases,
        compiler_params=pltpu.CompilerParams(vmem_limit_bytes=VMEM),
        cost_estimate=SMALL,
    )(info, h, g, *flat, *shared)


def feed_grad_kernel(h_rows, g_rows, members, info_ref, list_ref, *refs):
    h, g = refs[: len(h_rows)], refs[len(h_rows) : len(h_rows) + len(g_rows)]
    act_ref, keep_ref, send_ref, h_ref, g_ref, h_sem, g_sem = refs[len(h_rows) + len(g_rows) :]
    core = info_ref[1]
    at = pl.program_id(0)
    depth = h_ref.shape[1]
    half = depth // 2
    size = half // members
    aligned = size % LANES == 0

    def copies(parts, rows, whole, sem):
        out = []
        for ref, first in zip(parts, rows):
            here = slice(first, first + ref.shape[0])
            if not aligned:
                out.append(pltpu.make_async_copy(ref, whole.at[here], sem.at[len(out)]))
                continue
            for side in range(2):
                for z in range(members):
                    lanes = pl.ds(pl.multiple_of((2 * z + (core ^ side)) * size, size), size)
                    to = slice(side * half + z * size, side * half + (z + 1) * size)
                    out.append(
                        pltpu.make_async_copy(ref.at[:, lanes], whole.at[here, to], sem.at[len(out)])
                    )
        return out

    h_copies, g_copies = copies(h, h_rows, h_ref, h_sem), copies(g, g_rows, g_ref, g_sem)

    @pl.when(at == 0)
    def _():
        for copy in h_copies + g_copies:
            copy.start()
        for copy in h_copies:
            copy.wait()

    @pl.when(at == 1)
    def _():
        for copy in g_copies:
            copy.wait()

    def work(source):
        if aligned:
            for ref, side in ((keep_ref, 0), (send_ref, 1)):
                g_side = dot_tn(act_ref[0, 0], source[:, side * half : (side + 1) * half])
                for z in range(members):
                    ref[0, z] = g_side[:, z * size : (z + 1) * size].astype(bf16)
            return
        g_all = dot_tn(act_ref[0, 0], source[...])
        for z in range(members):
            even = g_all[:, 2 * z * size : (2 * z + 1) * size]
            odd = g_all[:, (2 * z + 1) * size : (2 * z + 2) * size]
            keep_ref[0, z] = jnp.where(core == 0, even, odd).astype(bf16)
            send_ref[0, z] = jnp.where(core == 0, odd, even).astype(bf16)

    @pl.when(list_ref[at, 1] < 2)
    def _():
        work(h_ref)

    @pl.when(list_ref[at, 1] == 2)
    def _():
        work(g_ref)


def feed_grads(info, h, h_rows, g, g_rows, act, wanted, members):
    depth = h[0].shape[1]
    _, _, rows, units = act.shape
    size = depth // (2 * members)
    count = len(wanted)
    out = jax.ShapeDtypeStruct((count, members, units, size), bf16)
    return pl.pallas_call(
        functools.partial(feed_grad_kernel, tuple(h_rows), tuple(g_rows), members),
        name="feed_grads",
        grid_spec=pltpu.PrefetchScalarGridSpec(
            num_scalar_prefetch=2,
            grid=(count,),
            in_specs=[anywhere()] * (len(h) + len(g))
            + [pl.BlockSpec((1, 1, rows, units), lambda i, info, w: (w[i, 0], w[i, 1], 0, 0))],
            out_specs=[pl.BlockSpec((1, members, units, size), lambda i, info, w: (i, 0, 0, 0))]
            * 2,
            scratch_shapes=[
                pltpu.VMEM((rows, depth), bf16),
                pltpu.VMEM((rows, depth), bf16),
                pltpu.SemaphoreType.DMA((2 * members * len(h),)),
                pltpu.SemaphoreType.DMA((2 * members * len(g),)),
            ],
        ),
        out_shape=[out, out],
        compiler_params=pltpu.CompilerParams(vmem_limit_bytes=VMEM),
        cost_estimate=SMALL,
    )(info, jnp.asarray(wanted, jnp.int32), *h, *g, act)


def branch_back_kernel(n, parts, info_ref, dh_ref, mid_ref, g_ref, gain_ref, w_ref, *refs):
    far, refs = refs[:parts], refs[parts:]
    dm_ref, db_ref, gg_ref = refs[:3]
    da = refs[3:]
    at = pl.program_id(0)
    width = da[0].shape[1]
    x = mid_ref[...]
    inverse = lax.rsqrt(jnp.mean(x * x, axis=-1, keepdims=True) + EPS)
    unit = x * inverse
    received = far[0][...]
    for p in range(1, parts):
        received = jnp.where(at == p, far[p][...], received)
    cotangent = dh_ref[...] + received.astype(f32)
    e = cotangent * gain_ref[...]
    inner = jnp.mean(e * unit, axis=-1, keepdims=True)
    d_mid = g_ref[...].astype(f32) + inverse * (e - unit * inner)
    share = jnp.sum(cotangent * unit, axis=0, keepdims=True)

    @pl.when(at == 0)
    def _():
        gg_ref[...] = jnp.zeros_like(gg_ref)

    gg_ref[...] += share
    dm_ref[...] = d_mid
    rounded = d_mid.astype(bf16)
    db_ref[...] = rounded
    for j in range(n):
        da[j][...] = dot_nt(rounded, w_ref[j * width : (j + 1) * width, :]).astype(bf16)


def branch_back(info, d_h, d_far, middle, g, gain, w_all, width):
    n = w_all.shape[0] // width
    parts = len(d_far)
    rows, depth = middle.shape
    size = rows // parts
    whole = lambda i, info: (0, 0)
    row = lambda i, info: (i, 0)
    part = pl.BlockSpec((size, depth), row)
    return pl.pallas_call(
        functools.partial(branch_back_kernel, n, parts),
        name="branch_back",
        grid_spec=pltpu.PrefetchScalarGridSpec(
            num_scalar_prefetch=1,
            grid=(parts,),
            in_specs=[part, part, part]
            + [pl.BlockSpec(gain.shape, whole), pl.BlockSpec(w_all.shape, whole)]
            + [pl.BlockSpec((size, depth), whole)] * parts,
            out_specs=[part, part, pl.BlockSpec((1, depth), whole)]
            + [pl.BlockSpec((size, width), row)] * n,
        ),
        out_shape=[
            jax.ShapeDtypeStruct((rows, depth), f32),
            jax.ShapeDtypeStruct((rows, depth), bf16),
            jax.ShapeDtypeStruct((1, depth), f32),
        ]
        + [jax.ShapeDtypeStruct((rows, width), bf16)] * n,
        compiler_params=pltpu.CompilerParams(vmem_limit_bytes=VMEM),
        cost_estimate=SMALL,
    )(info, d_h, middle, g, gain, w_all, *d_far)


def out_grad_kernel(n, info_ref, *refs):
    db_ref = refs[0]
    att = refs[1 : 1 + n]
    o_ref = refs[1 + n]
    for j in range(n):
        o_ref[info_ref[0] ^ j] = dot_tn(db_ref[...], att[j][...]).astype(bf16)


def out_grads(info, d_branch, att):
    n = len(att)
    rows, depth = d_branch.shape
    width = att[0].shape[1]
    whole = lambda i, info: (0, 0)
    return pl.pallas_call(
        functools.partial(out_grad_kernel, n),
        name="out_grads",
        grid_spec=pltpu.PrefetchScalarGridSpec(
            num_scalar_prefetch=1,
            grid=(1,),
            in_specs=[pl.BlockSpec(d_branch.shape, whole)]
            + [pl.BlockSpec(a.shape, whole) for a in att],
            out_specs=pl.BlockSpec((n, depth, width), lambda i, info: (0, 0, 0)),
        ),
        out_shape=jax.ShapeDtypeStruct((n, depth, width), bf16),
        compiler_params=pltpu.CompilerParams(vmem_limit_bytes=VMEM),
        cost_estimate=SMALL,
    )(info, d_branch, *att)


def qkv_grad_kernel(rows, placed, info_ref, *refs):
    count = len(placed)
    pieces = refs[:count]
    d_ref, w_ref, sel_ref, out_ref, o_ref, share_ref, x_ref, sem = refs[count:]
    columns = sel_ref.shape[0]
    at = pl.program_id(0)
    block = o_ref.shape[0]

    @pl.when(at == 0)
    def _():
        copies = []
        for i, (ref, (j, first)) in enumerate(zip(pieces, placed)):
            size = ref.shape[0]
            place = pl.ds(pl.multiple_of((info_ref[0] ^ j) * rows + first, size), size)
            copies.append(pltpu.make_async_copy(ref, x_ref.at[place], sem.at[i]))
        for copy in copies:
            copy.start()
        for copy in copies:
            copy.wait()

    lanes = pl.ds(pl.multiple_of(at * block, block), block)
    g = dot_tn(x_ref[:, lanes], d_ref[...])
    share_ref[...] = jnp.sum(g * w_ref[...].astype(f32), axis=1, keepdims=True)
    o_ref[:, :columns] = dot_nt(g.astype(bf16), sel_ref[...]).astype(bf16)
    o_ref[:, columns:] = out_ref[...]


def qkv_grads(info, parts, d, w, select, beside, rows):
    length = d.shape[0]
    depth = w.shape[0]
    columns = select.shape[0]
    total = columns + beside.shape[1]
    block = 512
    placed = tuple((j, first) for _, j, first in parts)
    whole = lambda i, info: (0, 0)
    row = lambda i, info: (i, 0)
    return pl.pallas_call(
        functools.partial(qkv_grad_kernel, rows, placed),
        name="qkv_grads",
        grid_spec=pltpu.PrefetchScalarGridSpec(
            num_scalar_prefetch=1,
            grid=(depth // block,),
            in_specs=[anywhere()] * len(parts)
            + [
                pl.BlockSpec(d.shape, whole),
                pl.BlockSpec((block, w.shape[1]), row),
                pl.BlockSpec(select.shape, whole),
                pl.BlockSpec((block, beside.shape[1]), row),
            ],
            out_specs=[pl.BlockSpec((block, total), row), pl.BlockSpec((block, 1), row)],
            scratch_shapes=[
                pltpu.VMEM((length, depth), bf16),
                pltpu.SemaphoreType.DMA((len(parts),)),
            ],
        ),
        out_shape=[
            jax.ShapeDtypeStruct((depth, total), bf16),
            jax.ShapeDtypeStruct((depth, 1), f32),
        ],
        compiler_params=pltpu.CompilerParams(vmem_limit_bytes=VMEM),
        cost_estimate=SMALL,
    )(info, *[p for p, _, _ in parts], d, w, select, beside)


def finish_kernel(n, wide, info_ref, *refs):
    d = refs[:n]
    own_ref, cols_ref, tok_ref, gain_ref, dm_ref, o_ref = refs[n : n + 6]
    w_ref, sem = refs[-2:]
    t = info_ref[0]
    members, _, size, columns = cols_ref.shape
    depth = members * size
    first = pl.program_id(0) == 0
    copies = [
        pltpu.make_async_copy(cols_ref.at[:, j], w_ref.at[j], sem.at[j]) for j in range(n - 1)
    ]

    @pl.when(first)
    def _():
        for copy in copies:
            copy.start()

    o_ref[...] = dot_nt(d[0][...], own_ref[...])
    for j in range(n - 1):

        @pl.when(first)
        def _():
            copies[j].wait()

        o_ref[...] += dot_nt(d[j + 1][...], w_ref[j].reshape(depth, columns))
    x = tok_ref[...].astype(f32)
    inverse = lax.rsqrt(jnp.mean(x * x, axis=-1, keepdims=True) + EPS)
    unit = x * inverse
    e = o_ref[...] * gain_ref[...]
    inner = jnp.mean(e * unit, axis=-1, keepdims=True)
    o_ref[...] = dm_ref[...] + inverse * (e - unit * inner)
    if wide:
        first_ref = refs[n + 6]
        width = depth // n
        for j in range(n):
            at = pl.ds(pl.multiple_of((t ^ j) * width, width), width)
            first_ref[:, at] = d[j][:, 4 * LANES :].astype(f32)


def finish(info, d_parts, own, cols, tokens, gain, d_middle):
    n = len(d_parts)
    rows, depth = tokens.shape
    block = min(rows, 512)
    wide = (depth // n) % LANES == 0
    row = lambda i, info: (i, 0)
    whole = lambda i, info: (0, 0)
    count = 2 if wide else 1
    members, _, size, columns = cols.shape
    out = pl.pallas_call(
        functools.partial(finish_kernel, n, wide),
        name="finish",
        grid_spec=pltpu.PrefetchScalarGridSpec(
            num_scalar_prefetch=1,
            grid=(rows // block,),
            in_specs=[pl.BlockSpec((block, d.shape[1]), row) for d in d_parts]
            + [
                pl.BlockSpec(own.shape, whole),
                anywhere(),
                pl.BlockSpec((block, depth), row),
                pl.BlockSpec((1, depth), whole),
                pl.BlockSpec((block, depth), row),
            ],
            out_specs=[pl.BlockSpec((block, depth), row)] * count,
            scratch_shapes=[
                pltpu.VMEM((n - 1, members, size, columns), bf16),
                pltpu.SemaphoreType.DMA((n - 1,)),
            ],
        ),
        out_shape=[jax.ShapeDtypeStruct((rows, depth), f32)] * count,
        compiler_params=pltpu.CompilerParams(vmem_limit_bytes=VMEM),
        cost_estimate=LARGE,
    )(info, *d_parts, own, cols, tokens, gain, d_middle)
    if wide:
        return out
    heads_width = depth // n
    pieces_ = jnp.stack([d[:, 4 * LANES : 4 * LANES + heads_width] for d in d_parts])
    ordered = jnp.take(pieces_, info[0] ^ jnp.arange(n), axis=0)
    return out[0], ordered.transpose(1, 0, 2).reshape(rows, depth).astype(f32)


def shards(
    tokens,
    first_values,
    doc_lengths,
    attention_norm_gain,
    w_qkv,
    w_out,
    feedforward_norm_gain,
    w_gate,
    w_up,
    w_down,
    out_grad,
):
    n = lax.axis_size("tensor")
    high, low = split_axis(n)
    members = lax.axis_size("dp") // 2
    t = lax.axis_index("tensor")
    z, core = lax.axis_index("dp") // 2, lax.axis_index("dp") % 2
    info = jnp.stack([t, core]).astype(jnp.int32)
    rows, depth = tokens.shape
    heads = w_out.shape[0] // HD
    own_width = heads * HD
    width = max(LANES, own_width)
    length = rows * n
    block = min(256, rows)
    gain_one = attention_norm_gain[None, :]
    gain_two = feedforward_norm_gain[None, :]
    missing = width - own_width
    widen = lambda v: jnp.pad(v, ((0, 0), (0, missing))) if missing else v
    replicas = 2 * members
    size_d = depth // replicas
    mine = lambda w, axis: lax.dynamic_slice_in_dim(w, lax.axis_index("dp") * size_d, size_d, axis)

    together = lax.optimization_barrier
    cosine, sine_table = rope_tables(length)
    ends = jnp.cumsum(doc_lengths[0])
    starts = ends - doc_lengths[0]
    docs = doc_lengths.shape[1]
    limits = jnp.pad(jnp.stack([starts, ends]), ((0, 6), (HD, LANES - HD - docs)))
    heads_at = jnp.arange(length // block, dtype=jnp.int32) * block
    begins = jnp.max(jnp.where(starts[None, :] <= heads_at[:, None], starts[None, :], 0), axis=1)
    begins = (begins // block).astype(jnp.int32)
    select = column_selector(heads)
    w_cols = jnp.dot(w_qkv, select, preferred_element_type=f32).astype(bf16)

    own_weights = (w_gate.T, w_up.T, w_down)
    weight_slice = jnp.concatenate([mine(w, 1) for w in own_weights])
    value_parts = [
        widen(lax.dynamic_slice_in_dim(first_values, (t ^ j) * own_width, own_width, 1))
        for j in range(n)
    ]
    w_out_wide = jnp.pad(w_out, ((0, missing), (0, 0))) if missing else w_out
    out_slice = mine(w_out_wide, 1)
    normed = norm_rows(tokens, gain_one)
    value_parts, normed = together((value_parts, normed))
    normed_parts = gather_rows(normed, n)
    out_slices = [out_slice] + [swap("tensor", out_slice, j) for j in range(1, n)]
    w_out_all = over_replicas(jnp.concatenate(after(out_slices, normed)))
    value_parts = [value_parts[0]] + [swap("tensor", value_parts[j], j) for j in range(1, n)]
    placed = [(j, first) for _, j, first in normed_parts]
    pieces_in = [piece for piece, _, _ in normed_parts]
    cols_slice = mine(w_cols, 0)
    (
        pieces_in, value_parts, weight_slice, w_cols, cols_slice, cosine, sine_table, limits,
        grad_late, select,
    ) = together(
        (
            pieces_in, value_parts, weight_slice, w_cols, cols_slice, cosine, sine_table, limits,
            out_grad, select,
        )
    )

    far_slices = [swap("tensor", weight_slice, a * low) for a in range(1, high)]
    grad_rows = [out_grad] + [swap("tensor", grad_late, b) for b in range(1, low)]
    normed_parts = [(piece, j, first) for piece, (j, first) in zip(pieces_in, placed)]
    q, k, v, squares = project(
        heads, info, normed_parts, value_parts, w_cols, cosine, sine_table, limits, rows
    )
    q, far_slices, w_out_all = together((q, far_slices, w_out_all))
    seen = {}
    for j in range(n - 1, -1, -1):
        seen[j] = attend(heads, info, j, q, k, v, begins, block, rows)
        if j == 1:
            q, *grad_rows = together((q, *grad_rows))
    feed_far = [(over_replicas(w),) for w in far_slices]
    heads_rows = [seen[0][0]] + [swap("tensor", seen[j][0], j) for j in range(1, n)]
    heads_rows, cols_slice = together((heads_rows, cols_slice))

    parts = 2 if rows >= 512 else 1
    size = rows // parts
    middle, second, w_out_all, *second_parts = branch(
        info, heads_rows, w_out_all, tokens, gain_two, parts
    )
    second_parts, cols_slice = together((second_parts, cols_slice))
    far_keys = [(b, p) for b in range(1, low) for p in range(parts)]
    inputs = {(b, p): swap("tensor", second_parts[p], b) for b, p in far_keys}
    cols_far = [swap("tensor", cols_slice, j) for j in range(1, n)]
    shards_held = [own_weights] + feed_far
    own_out, own_back, act = feed(
        info, second, out_grad, 0, shards_held, 0, low * rows, [], 0, rows, False
    )
    shared, backs = [act], {}
    for b, p in far_keys:
        if (b, p) == far_keys[0]:
            inputs, shared = together((inputs, shared))
        if (b, p) == far_keys[-1]:
            cols_far, shared = together((cols_far, shared))
        arrived = inputs[b, p]
        to_send, backs[b, p], act = feed(
            info, arrived, grad_rows[b], p * size, shards_held, b * rows + p * size, low * rows,
            shared, (b - 1) * rows + p * size, (low - 1) * rows, True,
        )
        shared = [to_send, act]
    d_far = [[swap("tensor", backs[b, p], b) for b in range(1, low)] for p in range(parts)]
    d_far = [d[0] if low == 2 else add_up(*d) for d in d_far]
    sources = (
        [second] + [inputs[key] for key in far_keys],
        [0] + [b * rows + p * size for b, p in far_keys],
        grad_rows,
        [b * rows for b in range(low)],
    )
    d_far[0], act = together((d_far[0], act))
    cols = lax.all_gather(jnp.stack(cols_far), "dp", axis=0)
    wanted = [(a, m) for a in range(1, high) for m in range(3)] + [(0, 0), (0, 1), (0, 2)]
    keep, send = feed_grads(info, *sources, act, wanted, members)
    d_far, keep, send, to_send = together((d_far, keep, send, to_send))

    got = swap("dp", send, 1)
    d_middle, d_branch, feed_share, *d_att = branch_back(
        info, own_back, d_far, middle, out_grad, gain_two, w_out_all, width
    )
    d_att = [d_att[0]] + [swap("tensor", d_att[j], j) for j in range(1, n)]
    add_two = lambda lo, hi: add_up(keep[lo:hi], got[lo:hi]).astype(bf16)
    rest_sums = [add_two(3 * a + 1, 3 * a + 3) for a in range(high - 1)]
    rest_sums, got = together((rest_sums, got))
    gate_sums = jnp.stack(
        [add_two(i, i + 1)[0] for i in [3 * (high - 1)] + [3 * a for a in range(high - 1)]], axis=1
    )
    out_grad_w = out_grads(info, d_branch, heads_rows)
    d_att, to_send, out_grad_w, keep, got, cols = together(
        (d_att, to_send, out_grad_w, keep, got, cols)
    )

    gate_z = [
        swap("dp", lax.dynamic_index_in_dim(gate_sums, z ^ k, 0, keepdims=False), 2 * k)
        for k in range(1, members)
    ]
    rest_got = [swap("tensor", rest_sums[a - 1], a * low) for a in range(1, high)]
    out_got = [swap("tensor", to_send[(b - 1) * rows : b * rows], b) for b in range(1, low)]
    out_sum = lax.psum_scatter(out_grad_w, "tensor", scatter_dimension=0, tiled=False)
    d_cols = attend_back(
        heads, info, [seen[j][1] for j in range(n)], k, v, d_att, [seen[j][0] for j in range(n)],
        cosine, sine_table, begins, block,
    )
    d_cols, gate_z, out_got, keep = together((d_cols, gate_z, out_got, keep))

    d_all, *d_parts = d_cols
    rest_sum = add_up(keep[-2:], got[-2:], *rest_got).astype(bf16).swapaxes(0, 1)
    d_all, rest_sum = together((d_all, rest_sum))
    d_parts = [d_parts[0]] + [swap("tensor", d_parts[j], j) for j in range(1, n)]
    grads, share = qkv_grads(info, normed_parts, d_all, w_cols, select, out_sum, rows)
    grads = lax.psum_scatter(grads, "dp", scatter_dimension=0, tiled=True)
    gate_z, out_got, share = together((gate_z, out_got, share))
    step = 1
    if members > 1:
        rest_sum = halve_over_z(rest_sum, z, step, lambda half: after(half, share))
    gate_sum = add_up(
        lax.dynamic_index_in_dim(gate_sums, z, 0, keepdims=False), *gate_z
    ).astype(bf16)
    gate_sum = add_up(
        gate_sum[0], *[swap("tensor", gate_sum[a], a * low) for a in range(1, high)]
    )
    out = add_up(middle, own_out, *out_got).astype(bf16)
    totals = jnp.sum(squares[:2], axis=1)
    scalars = jnp.pad(totals[None, :], ((0, 0), (0, depth - 2)))
    shares = jnp.concatenate([share.reshape(1, depth) / gain_one, feed_share, scalars])
    reach = 1
    while reach < replicas:
        shares = all_sum("dp", shares, [reach])
        reach *= 2
    d_parts, out, rest_sum, shares = together((d_parts, out, rest_sum, shares))
    while 2 * step < members:
        step *= 2
        rest_sum = halve_over_z(rest_sum, z, step, lambda half: half)
    rest_sum = rest_sum[0].astype(f32)
    tokens_grad, first_grad = finish(
        info, d_parts, w_cols, cols, tokens, gain_one, d_middle
    )
    shares, tokens_grad, rest_sum = together((shares, tokens_grad, rest_sum))
    sums = all_sum("tensor", shares, range(1, n))
    columns = 3 * own_width
    entry_count = first_values.size * lax.axis_size("dp") * n
    return (
        out,
        tokens_grad,
        first_grad,
        sums[0],
        grads[:, :columns].astype(f32),
        grads[:, columns : columns + own_width].T.astype(f32),
        sums[1],
        gate_sum.T,
        rest_sum[0].T,
        rest_sum[1],
        jnp.sqrt(sums[2, 1] / entry_count),
        jnp.sqrt(sums[2, 0] / entry_count),
    )


def solution(mesh):
    token_spec = P(("dp", "tensor"), None)
    return jax.shard_map(
        shards,
        mesh=mesh,
        in_specs=(
            token_spec,
            token_spec,
            P("dp", None),
            P(),
            P(None, "tensor"),
            P("tensor", None),
            P(),
            P(None, "tensor"),
            P(None, "tensor"),
            P("tensor", None),
            token_spec,
        ),
        out_specs=(
            token_spec,
            token_spec,
            token_spec,
            P(),
            P("dp", "tensor"),
            P("tensor", "dp"),
            P(),
            P("dp", "tensor"),
            P("dp", "tensor"),
            P("tensor", "dp"),
            P(),
            P(),
        ),
        check_vma=False,
    )
```

```python
import functools
import math

import jax
import jax.numpy as jnp
import numpy as np
from jax import lax
from jax.experimental import pallas as pl
from jax.experimental.pallas import tpu as pltpu
from jax.sharding import PartitionSpec as P

HD = 64
HALF = HD // 2
LANES = 128
GROUP = LANES // HALF
EPS = 1e-06
NEG = -1e30
VMEM = 60 << 20
SMALL = pl.CostEstimate(flops=1, bytes_accessed=1, transcendentals=0)
LARGE = pl.CostEstimate(flops=10**11, bytes_accessed=1, transcendentals=0)
f32 = jnp.float32
bf16 = jnp.bfloat16


def rope_tables(length):
    inverse = jnp.exp(-math.log(10000.0) * jnp.arange(HALF, dtype=f32) / HALF)
    angles = jnp.arange(length, dtype=f32)[:, None] * inverse[None, :]
    tile = lambda t: jnp.concatenate([t] * GROUP, axis=1)
    return tile(jnp.cos(angles)), tile(jnp.sin(angles))


def column_order(heads):
    value_width = max(LANES, heads * HD)
    order = np.full((4 * LANES + value_width,), -1, np.int32)
    for h in range(heads):
        for part in range(2):
            for half in range(2):
                at = (2 * part + half) * LANES + h * HALF
                src = h * 3 * HD + part * HD + half * HALF
                order[at : at + HALF] = np.arange(src, src + HALF)
        order[4 * LANES + h * HD : 4 * LANES + (h + 1) * HD] = np.arange(
            h * 3 * HD + 2 * HD, (h + 1) * 3 * HD
        )
    return order


def column_selector(heads):
    order = jnp.asarray(column_order(heads))
    rows = jnp.arange(3 * heads * HD, dtype=jnp.int32)
    return (rows[:, None] == order[None, :]).astype(bf16)


def dot_nt(a, b):
    return lax.dot_general(a, b, (((1,), (1,)), ((), ())), preferred_element_type=f32)


def dot_tn(a, b):
    return lax.dot_general(a, b, (((0,), (0,)), ((), ())), preferred_element_type=f32)


def dot_nn(a, b):
    return jnp.dot(a, b, preferred_element_type=f32)


def anywhere():
    return pl.BlockSpec(memory_space=pl.ANY)


def project_kernel(heads, placed, info_ref, *refs):
    count = len(placed)
    n = len({j for j, _ in placed})
    pieces, values = refs[:count], refs[count : count + n]
    w_ref, cos_ref, sin_ref, lim_ref = refs[count + n : count + n + 4]
    q_ref, k_ref, v_ref, sq_ref, x_ref, fv_ref, sem = refs[count + n + 4 :]
    at = pl.program_id(0)
    block = q_ref.shape[0]
    copies = []
    for i, (ref, (j, first)) in enumerate(zip(pieces, placed)):
        into = x_ref.at[j, first : first + ref.shape[0]]
        copies.append((j, pltpu.make_async_copy(ref, into, sem.at[i])))
    for j, ref in enumerate(values):
        copies.append((j, pltpu.make_async_copy(ref, fv_ref.at[j], sem.at[count + j])))

    @pl.when(at == 0)
    def _():
        sq_ref[...] = jnp.zeros_like(sq_ref)
        for _, copy in copies:
            copy.start()

    for j in range(n):

        @pl.when(at == j)
        def _():
            for owner, copy in copies:
                if owner == j:
                    copy.wait()

    acc = dot_nn(x_ref[at], w_ref[...])
    c, s = cos_ref[...], sin_ref[...]
    lane = lax.broadcasted_iota(jnp.int32, (block, LANES), 1)
    place = (info_ref[0] ^ at) * block + lax.broadcasted_iota(jnp.int32, (block, LANES), 0)
    inside = (place >= lim_ref[0:1, :]) & (place < lim_ref[1:2, :])
    doc_lane = (lane >= HD) & (lane < HD + 8)
    q_extra = jnp.where(doc_lane & jnp.logical_not(inside), NEG, 0.0)
    k_extra = jnp.where(inside, 1.0, jnp.where((lane >= HD + 8) & (lane < HD + 11), 1.0, 0.0))
    for ref, base, extra, scale in ((q_ref, 0, q_extra, HD**-0.5), (k_ref, 2, k_extra, 1.0)):
        u1 = acc[:, base * LANES : (base + 1) * LANES]
        u2 = acc[:, (base + 1) * LANES : (base + 2) * LANES]
        r1 = (u1 * c - u2 * s) * scale
        r2 = (u1 * s + u2 * c) * scale
        for h in range(heads):
            a = r1 if h == 0 else pltpu.roll(r1, LANES - HALF * h, 1)
            b = r2 if h == 1 else pltpu.roll(r2, (LANES + HALF - HALF * h) % LANES, 1)
            both = jnp.where(lane < HALF, a, jnp.where(lane < HD, b, extra))
            ref[:, h * LANES : (h + 1) * LANES] = both.astype(bf16)
    first = fv_ref[at].astype(f32)
    mixed = 0.5 * acc[:, 4 * LANES :] + 0.5 * first
    sq_ref[0:1, :] += jnp.sum(mixed * mixed, axis=0, keepdims=True)
    sq_ref[1:2, :] += jnp.sum(first * first, axis=0, keepdims=True)
    for h in range(heads):
        t = (h // 2) * LANES
        own = (lane < HD) if h % 2 == 0 else (lane >= HD)
        v_ref[:, h * LANES : (h + 1) * LANES] = jnp.where(
            own, mixed[:, t : t + LANES], 1.0
        ).astype(bf16)


def project(heads, info, parts, values, w, cos, sin, limits, rows):
    n = len(values)
    length = rows * n
    depth = parts[0][0].shape[1]
    width = values[0].shape[1]
    row = lambda i, info: (info[0] ^ i, 0)
    whole = lambda i, info: (0, 0)
    ext = heads * LANES
    placed = tuple((j, first) for _, j, first in parts)
    return pl.pallas_call(
        functools.partial(project_kernel, heads, placed),
        name="project",
        grid_spec=pltpu.PrefetchScalarGridSpec(
            num_scalar_prefetch=1,
            grid=(n,),
            in_specs=[anywhere()] * (len(parts) + n)
            + [
                pl.BlockSpec(w.shape, whole),
                pl.BlockSpec((rows, LANES), row),
                pl.BlockSpec((rows, LANES), row),
                pl.BlockSpec((8, LANES), whole),
            ],
            out_specs=[
                pl.BlockSpec((rows, ext), row),
                pl.BlockSpec((rows, ext), row),
                pl.BlockSpec((rows, ext), row),
                pl.BlockSpec((8, width), whole),
            ],
            scratch_shapes=[
                pltpu.VMEM((n, rows, depth), bf16),
                pltpu.VMEM((n, rows, width), bf16),
                pltpu.SemaphoreType.DMA((len(parts) + n,)),
            ],
        ),
        out_shape=[jax.ShapeDtypeStruct((length, ext), bf16)] * 3
        + [jax.ShapeDtypeStruct((8, width), f32)],
        compiler_params=pltpu.CompilerParams(vmem_limit_bytes=VMEM),
        cost_estimate=SMALL,
    )(info, *[p for p, _, _ in parts], *values, w, cos, sin, limits)


def pieces(x):
    hi = x.astype(bf16).astype(f32)
    mid = (x - hi).astype(bf16).astype(f32)
    return hi, mid, x - hi - mid


def attend_kernel(
    heads, offset, bk, info_ref, begin_ref, q_ref, k_ref, v_ref, o_ref, qo_ref, m_ref, acc_ref
):
    bq = q_ref.shape[0]
    at = info_ref[0] ^ offset
    lane = lax.broadcasted_iota(jnp.int32, (bq, LANES), 1)
    r = lax.broadcasted_iota(jnp.int32, (bq, bk), 0)
    c = lax.broadcasted_iota(jnp.int32, (bq, bk), 1)
    col = [slice(h * LANES, (h + 1) * LANES) for h in range(heads)]
    spread = lambda m: jnp.concatenate([m] * (bk // LANES), axis=1)

    def visit(kb, mask, first):
        there = pl.ds(pl.multiple_of(kb * bk, bk), bk)
        for h in range(heads):
            s = dot_nt(q_ref[:, col[h]], k_ref[there, col[h]])
            if mask is not None:
                s = jnp.where(mask, s, NEG)
            new = jnp.broadcast_to(jnp.max(s, axis=1, keepdims=True), (bq, LANES))
            if not first:
                old = m_ref[:, col[h]]
                new = jnp.maximum(old, new)
            p = jnp.exp(s - spread(new)).astype(bf16)
            part = dot_nn(p, v_ref[there, col[h]])
            m_ref[:, col[h]] = new
            acc_ref[:, col[h]] = part if first else acc_ref[:, col[h]] * jnp.exp(old - new) + part

    for d in range(bq // bk):
        visit(at * (bq // bk) + d, c + d * bk <= r, d == 0)

    def step(kb, carry):
        visit(kb, None, False)
        return carry

    lax.fori_loop(begin_ref[at * (bq // bk)], at * (bq // bk), step, 0)
    low = lane < HD
    for t in range((heads + 1) // 2):
        a = acc_ref[:, col[2 * t]]
        b = acc_ref[:, col[2 * t + 1]] if 2 * t + 1 < heads else a
        total = pltpu.roll(jnp.where(low, b, a), HD, 1)
        result = jnp.where(low, a, b) / total
        if 2 * t + 1 >= heads:
            result = jnp.where(low, result, 0.0)
        o_ref[:, t * LANES : (t + 1) * LANES] = result.astype(bf16)
    for h in range(heads):
        a = acc_ref[:, col[h]]
        total = a if h % 2 == 0 else pltpu.roll(a, HD, 1)
        hi, mid, lo = pieces(-(m_ref[:, col[h]] + jnp.log(jnp.where(low, 1.0, total))))
        extra = jnp.where(
            lane == HD + 8, hi, jnp.where(lane == HD + 9, mid, jnp.where(lane == HD + 10, lo, 0.0))
        )
        fill = (lane >= HD + 8) & (lane < HD + 11)
        qo_ref[:, col[h]] = jnp.where(fill, extra, q_ref[:, col[h]].astype(f32)).astype(bf16)


def attend(heads, info, offset, q, k, v, begins, block, rows):
    length = q.shape[0]
    ext = heads * LANES
    width = max(LANES, heads * HD)
    whole = lambda i, info, b: (0, 0)
    return pl.pallas_call(
        functools.partial(attend_kernel, heads, offset, block),
        name="attend",
        grid_spec=pltpu.PrefetchScalarGridSpec(
            num_scalar_prefetch=2,
            grid=(1,),
            in_specs=[
                pl.BlockSpec((rows, ext), lambda i, info, b: (info[0] ^ offset, 0)),
                pl.BlockSpec((length, ext), whole),
                pl.BlockSpec((length, ext), whole),
            ],
            out_specs=[pl.BlockSpec((rows, width), whole), pl.BlockSpec((rows, ext), whole)],
            scratch_shapes=[pltpu.VMEM((rows, ext), f32), pltpu.VMEM((rows, ext), f32)],
        ),
        out_shape=[
            jax.ShapeDtypeStruct((rows, width), bf16),
            jax.ShapeDtypeStruct((rows, ext), bf16),
        ],
        compiler_params=pltpu.CompilerParams(vmem_limit_bytes=VMEM),
        cost_estimate=SMALL,
    )(info, begins, q, k, v)


def attend_back_kernel(heads, block, n, info_ref, begin_ref, *refs):
    q_parts, do_parts, o_parts = refs[:n], refs[n : 2 * n], refs[2 * n : 3 * n]
    k_ref, v_ref, cos_ref, sin_ref, g_ref = refs[3 * n : 3 * n + 5]
    sends = refs[3 * n + 5 : 4 * n + 5]
    q_all, do_all, o_all, dk_ref, dv_ref, dq_ref, de_ref, sem = refs[4 * n + 5 :]
    at = pl.program_id(0)
    rows = q_parts[0].shape[0]

    def moves(pairs):
        copies = []
        for i, (make, j) in enumerate(pairs):
            place = pl.ds(pl.multiple_of((info_ref[0] ^ j) * rows, rows), rows)
            copies.append(make(place, sem.at[i]))
        for copy in copies:
            copy.start()
        for copy in copies:
            copy.wait()

    @pl.when(at == 0)
    def _():
        moves(
            [
                (functools.partial(lambda src, dst, p, s: pltpu.make_async_copy(src, dst.at[p], s), part, whole), j)
                for parts, whole in ((q_parts, q_all), (do_parts, do_all), (o_parts, o_all))
                for j, part in enumerate(parts)
            ]
        )

    lane = lax.broadcasted_iota(jnp.int32, (block, LANES), 1)
    r = lax.broadcasted_iota(jnp.int32, (block, block), 0)
    c = lax.broadcasted_iota(jnp.int32, (block, block), 1)
    causal = r <= c
    low = lane < HD
    here = pl.ds(pl.multiple_of(at * block, block), block)
    col = [slice(h * LANES, (h + 1) * LANES) for h in range(heads)]

    for h in range(heads):
        t = slice((h // 2) * LANES, (h // 2 + 1) * LANES)
        own = low if h % 2 == 0 else jnp.logical_not(low)
        grad = do_all[here, t].astype(f32)
        product = grad * o_all[here, t].astype(f32)
        centre = jnp.sum(jnp.where(own, product, 0.0), axis=1, keepdims=True)
        hi, mid, lo = pieces(-jnp.broadcast_to(centre, (block, LANES)))
        spot = lane - (HD if h % 2 == 0 else 0)
        extra = jnp.where(spot == 0, hi, jnp.where(spot == 1, mid, jnp.where(spot == 2, lo, 0.0)))
        de_ref[:, col[h]] = jnp.where(own, grad, extra).astype(bf16)

    def visit(there, mask, first):
        st = [dot_nt(k_ref[there, c_], q_all[here, c_]) for c_ in col]
        dpt = [dot_nt(v_ref[there, c_], de_ref[:, c_]) for c_ in col]
        p = [jnp.exp(s) for s in st]
        if mask is not None:
            p = [jnp.where(mask, x, 0.0) for x in p]
        ds = [(x * y).astype(bf16) for x, y in zip(p, dpt)]
        p = [x.astype(bf16) for x in p]
        for h, c_ in enumerate(col):
            dv = dot_nn(p[h], de_ref[:, c_])
            dk = dot_nn(ds[h], q_all[here, c_])
            dq = dot_tn(ds[h], k_ref[there, c_])
            if first:
                dv_ref[there, c_] = dv
                dk_ref[there, c_] = dk
                dq_ref[:, c_] = dq
            else:
                dv_ref[there, c_] += dv
                dk_ref[there, c_] += dk
                dq_ref[:, c_] += dq

    visit(here, causal, True)

    def step(kb, carry):
        visit(pl.ds(pl.multiple_of(kb * block, block), block), None, False)
        return carry

    lax.fori_loop(begin_ref[at], at, step, 0)

    def turn_back(ref, rows, scale):
        u1 = u2 = None
        quarter = lane // HALF
        for h in range(heads):
            u = ref[rows, col[h]]
            a = u if h == 0 else pltpu.roll(u, HALF * h, 1)
            b = u if h == 1 else pltpu.roll(u, (LANES + HALF * h - HALF) % LANES, 1)
            u1 = a if h == 0 else jnp.where(quarter == h, a, u1)
            u2 = b if h == 0 else jnp.where(quarter == h, b, u2)
        if heads < GROUP:
            u1 = jnp.where(quarter < heads, u1, 0.0)
            u2 = jnp.where(quarter < heads, u2, 0.0)
        u1, u2 = u1 * scale, u2 * scale
        cs, sn = cos_ref[rows, :], sin_ref[rows, :]
        return (u1 * cs + u2 * sn).astype(bf16), (u2 * cs - u1 * sn).astype(bf16)

    def finish_block(i, carry):
        rows = pl.ds(pl.multiple_of(i * block, block), block)
        d1, d2 = turn_back(dk_ref, rows, 1.0)
        g_ref[rows, 2 * LANES : 3 * LANES] = d1
        g_ref[rows, 3 * LANES : 4 * LANES] = d2
        for t in range((heads + 1) // 2):
            a = dv_ref[rows, col[2 * t]]
            b = dv_ref[rows, col[2 * t + 1]] if 2 * t + 1 < heads else jnp.zeros_like(a)
            d_mix = jnp.where(low, a, b).astype(bf16)
            g_ref[rows, (4 + t) * LANES : (5 + t) * LANES] = (d_mix.astype(f32) * 0.5).astype(bf16)
        return carry

    u1 = u2 = None
    quarter = lane // HALF
    for h in range(heads):
        u = dq_ref[:, col[h]]
        a = u if h == 0 else pltpu.roll(u, HALF * h, 1)
        b = u if h == 1 else pltpu.roll(u, (LANES + HALF * h - HALF) % LANES, 1)
        u1 = a if h == 0 else jnp.where(quarter == h, a, u1)
        u2 = b if h == 0 else jnp.where(quarter == h, b, u2)
    if heads < GROUP:
        u1 = jnp.where(quarter < heads, u1, 0.0)
        u2 = jnp.where(quarter < heads, u2, 0.0)
    u1, u2 = u1 * HD**-0.5, u2 * HD**-0.5
    cs, sn = cos_ref[here, :], sin_ref[here, :]
    g_ref[here, 0:LANES] = (u1 * cs + u2 * sn).astype(bf16)
    g_ref[here, LANES : 2 * LANES] = (u2 * cs - u1 * sn).astype(bf16)

    @pl.when(at == pl.num_programs(0) - 1)
    def _():
        lax.fori_loop(0, pl.num_programs(0), finish_block, 0)
        moves(
            [
                (functools.partial(lambda dst, p, s: pltpu.make_async_copy(g_ref.at[p], dst, s), dst), j)
                for j, dst in enumerate(sends)
            ]
        )


def attend_back(heads, info, q_parts, k, v, do_parts, o_parts, cos, sin, begins, block):
    n = len(q_parts)
    rows = q_parts[0].shape[0]
    length = n * rows
    ext = heads * LANES
    width = o_parts[0].shape[1]
    whole = lambda i, info, b: (0, 0)
    anywhere = pl.BlockSpec(memory_space=pl.ANY)
    columns = 4 * LANES + width
    return pl.pallas_call(
        functools.partial(attend_back_kernel, heads, block, n),
        name="attend_back",
        grid_spec=pltpu.PrefetchScalarGridSpec(
            num_scalar_prefetch=2,
            grid=(length // block,),
            in_specs=[anywhere] * (3 * n)
            + [
                pl.BlockSpec((length, ext), whole),
                pl.BlockSpec((length, ext), whole),
                pl.BlockSpec((length, LANES), whole),
                pl.BlockSpec((length, LANES), whole),
            ],
            out_specs=[pl.BlockSpec((length, columns), whole)] + [anywhere] * n,
            scratch_shapes=[
                pltpu.VMEM((length, ext), bf16),
                pltpu.VMEM((length, width), bf16),
                pltpu.VMEM((length, width), bf16),
                pltpu.VMEM((length, ext), f32),
                pltpu.VMEM((length, ext), f32),
                pltpu.VMEM((block, ext), f32),
                pltpu.VMEM((block, ext), bf16),
                pltpu.SemaphoreType.DMA((3 * n,)),
            ],
        ),
        out_shape=[jax.ShapeDtypeStruct((length, columns), bf16)]
        + [jax.ShapeDtypeStruct((rows, columns), bf16)] * n,
        compiler_params=pltpu.CompilerParams(vmem_limit_bytes=VMEM),
        cost_estimate=LARGE,
    )(info, begins, *q_parts, *do_parts, *o_parts, k, v, cos, sin)


def split_axis(n):
    low = 1 << ((n.bit_length() - 1) // 2)
    return n // low, low


def swap(axis, value, offset):
    n = lax.axis_size(axis)
    return lax.ppermute(value, axis, [(i, i ^ offset) for i in range(n)])


def gather_rows(value, n):
    high, low = split_axis(n)
    rows = value.shape[0]
    half = rows // 2
    parts = {0: value}
    for b in range(1, low):
        parts[b] = swap("tensor", value, b)
    for a in range(1, high):
        parts[a * low] = swap("tensor", value, a * low)
    listed = [(parts[j], j, 0) for j in sorted(parts)]
    for a in range(1, high):
        for b in range(1, low):
            j = a * low + b
            listed.append((swap("tensor", parts[b][:half], a * low), j, 0))
            listed.append((swap("tensor", parts[a * low][half:], b), j, half))
    return listed


def after(value, *others):
    return lax.optimization_barrier((value,) + others)[0]


def add_up(first, *others):
    total = first.astype(f32)
    for other in others:
        total = total + other.astype(f32)
    return total


def over_replicas(value):
    if value.shape[1] % LANES == 0:
        return lax.all_gather(value, "dp", axis=0)
    return lax.all_gather(value, "dp", axis=1, tiled=True)


def halve_over_z(parts, z, step, hold):
    pairs = parts.reshape((-1, 2) + parts.shape[1:])
    side = (z // step) % 2
    pick = lambda which: lax.dynamic_index_in_dim(pairs, which, 1, keepdims=False)
    parts = add_up(pick(side), hold(swap("dp", pick(1 - side), 2 * step)))
    return parts.astype(bf16) if parts.shape[0] > 1 else parts


def all_sum(axis, value, offsets):
    parts = [value] + [swap(axis, value, j) for j in offsets]
    while len(parts) > 1:
        parts = [a + b for a, b in zip(parts[::2], parts[1::2])]
    return parts[0]


def norm_kernel(x_ref, gain_ref, o_ref):
    x = x_ref[...].astype(f32)
    inverse = lax.rsqrt(jnp.mean(x * x, axis=-1, keepdims=True) + EPS)
    o_ref[...] = (x * inverse * gain_ref[...]).astype(bf16)


def norm_rows(x, gain):
    rows, depth = x.shape
    block = min(rows, 128)
    return pl.pallas_call(
        norm_kernel,
        name="norm_rows",
        grid=(rows // block,),
        in_specs=[
            pl.BlockSpec((block, depth), lambda i: (i, 0)),
            pl.BlockSpec((1, depth), lambda i: (0, 0)),
        ],
        out_specs=pl.BlockSpec((block, depth), lambda i: (i, 0)),
        out_shape=jax.ShapeDtypeStruct((rows, depth), bf16),
        compiler_params=pltpu.CompilerParams(vmem_limit_bytes=VMEM),
        cost_estimate=SMALL,
    )(x, gain)


def branch_kernel(n, parts, info_ref, *refs):
    att = refs[:n]
    slices_ref, tok_ref, gain_ref, mid_ref, h_ref, w_ref = refs[n : n + 6]
    h_parts = refs[n + 6 : n + 6 + parts]
    all_ref, sem, w_sem = refs[n + 6 + parts :]
    at = pl.program_id(0)
    size = tok_ref.shape[0]
    width = att[0].shape[1]

    @pl.when(at == 0)
    def _():
        copies = [
            pltpu.make_async_copy(
                att[j], all_ref.at[:, j * width : (j + 1) * width], sem.at[j]
            )
            for j in range(n)
        ]
        if len(slices_ref.shape) == 3:
            lanes = slices_ref.shape[2]
            copies += [
                pltpu.make_async_copy(
                    slices_ref.at[d], w_ref.at[:, d * lanes : (d + 1) * lanes], w_sem.at[d]
                )
                for d in range(slices_ref.shape[0])
            ]
        else:
            copies.append(pltpu.make_async_copy(slices_ref, w_ref, w_sem.at[0]))
        for copy in copies:
            copy.start()
        for copy in copies:
            copy.wait()

    here = pl.ds(pl.multiple_of(at * size, size), size)
    x = tok_ref[...].astype(f32) + dot_nn(all_ref[here, :], w_ref[...])
    mid_ref[...] = x
    inverse = lax.rsqrt(jnp.mean(x * x, axis=-1, keepdims=True) + EPS)
    h = (x * inverse * gain_ref[...]).astype(bf16)
    h_ref[...] = h
    for p in range(parts):

        @pl.when(at == p)
        def _():
            h_parts[p][...] = h


def branch(info, att, w_slices, tokens, gain, parts):
    n = len(att)
    rows, width = att[0].shape
    depth = tokens.shape[1]
    size = rows // parts
    whole = lambda i, info: (0, 0)
    row = lambda i, info: (i, 0)
    count = w_slices.shape[0] if w_slices.ndim == 3 else 1
    return pl.pallas_call(
        functools.partial(branch_kernel, n, parts),
        name="branch",
        grid_spec=pltpu.PrefetchScalarGridSpec(
            num_scalar_prefetch=1,
            grid=(parts,),
            in_specs=[anywhere()] * (n + 1)
            + [pl.BlockSpec((size, depth), row), pl.BlockSpec((1, depth), whole)],
            out_specs=[pl.BlockSpec((size, depth), row)] * 2
            + [pl.BlockSpec((n * width, depth), whole)]
            + [pl.BlockSpec((size, depth), whole)] * parts,
            scratch_shapes=[
                pltpu.VMEM((rows, n * width), bf16),
                pltpu.SemaphoreType.DMA((n,)),
                pltpu.SemaphoreType.DMA((count,)),
            ],
        ),
        out_shape=[
            jax.ShapeDtypeStruct((rows, depth), f32),
            jax.ShapeDtypeStruct((rows, depth), bf16),
            jax.ShapeDtypeStruct((n * width, depth), bf16),
        ]
        + [jax.ShapeDtypeStruct((size, depth), bf16)] * parts,
        compiler_params=pltpu.CompilerParams(vmem_limit_bytes=VMEM),
        cost_estimate=SMALL,
    )(info, *att, w_slices, tokens, gain)


def feed_kernel(shards_in, shared, send, act_first, info_ref, h_ref, g_ref, *refs):
    count = sum(shards_in)
    weights, refs = refs[:count], refs[count + shared :]
    out_ref, dh_ref, act_out, w_ref, sem, act_ref, act_sem = refs[:7]
    out_acc, dh_acc = refs[7:] if send else (out_ref, dh_ref)
    high, rows_w, depth = w_ref.shape
    units = rows_w // 3
    copies, at, used = [], 0, 0
    for a, pieces_in in enumerate(shards_in):
        groups = []
        for m in range(3):
            span = pl.ds(m * units, units)
            ref = weights[at + m] if pieces_in == 3 else weights[at]
            if pieces_in == 3:
                moves = [(ref, w_ref.at[a, span])]
            elif len(ref.shape) == 3:
                size = ref.shape[2]
                moves = [
                    (ref.at[d, span], w_ref.at[a, span, d * size : (d + 1) * size])
                    for d in range(ref.shape[0])
                ]
            else:
                moves = [(ref.at[span], w_ref.at[a, span])]
            groups.append(
                [
                    pltpu.make_async_copy(src, dst, sem.at[used + i])
                    for i, (src, dst) in enumerate(moves)
                ]
            )
            used += len(moves)
        at += pieces_in
        copies.append(groups)
    for groups in copies:
        for group in groups:
            for copy in group:
                copy.start()

    rows = h_ref.shape[0]
    out_acc[...] = jnp.zeros_like(out_acc)
    dh_acc[...] = jnp.zeros_like(dh_acc)

    def leave(a):
        to = act_out.at[a, :, act_first : act_first + rows]
        return pltpu.make_async_copy(act_ref.at[a], to, act_sem.at[a])

    def shard(a, carry):
        def weight(m):
            for k in range(high):

                @pl.when(a == k)
                def _():
                    for copy in copies[k][m]:
                        copy.wait()

            return w_ref[a, m * units : (m + 1) * units, :]

        gate = dot_nt(h_ref[...], weight(0))
        up = dot_nt(h_ref[...], weight(1))
        back = dot_nt(g_ref[...], weight(2))
        s = 0.5 * jnp.tanh(0.5 * gate) + 0.5
        gs = gate * s
        hidden = (gs * up).astype(bf16)
        d_up = (back * gs).astype(bf16)
        d_gate = (back * up * (s + gs * (1.0 - s))).astype(bf16)
        act_ref[a, 0] = d_gate
        act_ref[a, 1] = d_up
        act_ref[a, 2] = hidden
        leave(a).start()
        gate_w, up_w, down_w = (w_ref[a, m * units : (m + 1) * units, :] for m in range(3))
        dh_acc[...] += dot_nn(d_gate, gate_w) + dot_nn(d_up, up_w)
        out_acc[...] += dot_nn(hidden, down_w)
        return carry

    lax.fori_loop(0, high, shard, 0)
    if send:
        out_ref[...] = out_acc[...].astype(bf16)
        dh_ref[...] = dh_acc[...].astype(bf16)
    for a in range(high):
        leave(a).wait()


def feed(info, h, g, g_first, weights, act_first, act_rows, shared, out_first, out_rows, send):
    rows, depth = h.shape
    high = len(weights)
    flat = [w for shard in weights for w in shard]
    units = weights[0][0].shape[0] if len(weights[0]) == 3 else weights[0][0].shape[-2] // 3
    block = rows
    at, out_at = g_first // block, out_first // block
    row = lambda i, info: (i, 0)
    kind = bf16 if send else f32
    moves = sum(
        3 if len(shard) == 3 else 3 * (shard[0].shape[0] if shard[0].ndim == 3 else 1)
        for shard in weights
    )
    base = 3 + len(flat)
    aliases = {} if not shared else {base: 2} if len(shared) == 1 else {base: 0, base + 1: 2}
    return pl.pallas_call(
        functools.partial(
            feed_kernel, tuple(len(shard) for shard in weights), len(shared), send, act_first
        ),
        name="feed",
        grid_spec=pltpu.PrefetchScalarGridSpec(
            num_scalar_prefetch=1,
            grid=(1,),
            in_specs=[
                pl.BlockSpec((block, depth), row),
                pl.BlockSpec((block, depth), lambda i, info: (at, 0)),
            ]
            + [anywhere()] * (len(flat) + len(shared)),
            out_specs=[
                pl.BlockSpec((block, depth), lambda i, info: (out_at, 0)),
                pl.BlockSpec((block, depth), row),
                anywhere(),
            ],
            scratch_shapes=[
                pltpu.VMEM((high, 3 * units, depth), bf16),
                pltpu.SemaphoreType.DMA((moves,)),
                pltpu.VMEM((high, 3, block, units), bf16),
                pltpu.SemaphoreType.DMA((high,)),
            ]
            + ([pltpu.VMEM((block, depth), f32)] * 2 if send else []),
        ),
        out_shape=[
            jax.ShapeDtypeStruct((out_rows, depth), kind),
            jax.ShapeDtypeStruct((rows, depth), kind),
            jax.ShapeDtypeStruct((high, 3, act_rows, units), bf16),
        ],
        input_output_aliases=aliases,
        compiler_params=pltpu.CompilerParams(vmem_limit_bytes=VMEM),
        cost_estimate=SMALL,
    )(info, h, g, *flat, *shared)


def feed_grad_kernel(h_rows, g_rows, members, info_ref, list_ref, *refs):
    h, g = refs[: len(h_rows)], refs[len(h_rows) : len(h_rows) + len(g_rows)]
    act_ref, keep_ref, send_ref, h_ref, g_ref, h_sem, g_sem = refs[len(h_rows) + len(g_rows) :]
    core = info_ref[1]
    at = pl.program_id(0)
    depth = h_ref.shape[1]
    half = depth // 2
    size = half // members
    aligned = size % LANES == 0

    def copies(parts, rows, whole, sem):
        out = []
        for ref, first in zip(parts, rows):
            here = slice(first, first + ref.shape[0])
            if not aligned:
                out.append(pltpu.make_async_copy(ref, whole.at[here], sem.at[len(out)]))
                continue
            for side in range(2):
                for z in range(members):
                    lanes = pl.ds(pl.multiple_of((2 * z + (core ^ side)) * size, size), size)
                    to = slice(side * half + z * size, side * half + (z + 1) * size)
                    out.append(
                        pltpu.make_async_copy(ref.at[:, lanes], whole.at[here, to], sem.at[len(out)])
                    )
        return out

    h_copies, g_copies = copies(h, h_rows, h_ref, h_sem), copies(g, g_rows, g_ref, g_sem)

    @pl.when(at == 0)
    def _():
        for copy in h_copies + g_copies:
            copy.start()
        for copy in h_copies:
            copy.wait()

    @pl.when(at == 1)
    def _():
        for copy in g_copies:
            copy.wait()

    def work(source):
        if aligned:
            for ref, side in ((keep_ref, 0), (send_ref, 1)):
                g_side = dot_tn(act_ref[0, 0], source[:, side * half : (side + 1) * half])
                for z in range(members):
                    ref[0, z] = g_side[:, z * size : (z + 1) * size].astype(bf16)
            return
        g_all = dot_tn(act_ref[0, 0], source[...])
        for z in range(members):
            even = g_all[:, 2 * z * size : (2 * z + 1) * size]
            odd = g_all[:, (2 * z + 1) * size : (2 * z + 2) * size]
            keep_ref[0, z] = jnp.where(core == 0, even, odd).astype(bf16)
            send_ref[0, z] = jnp.where(core == 0, odd, even).astype(bf16)

    @pl.when(list_ref[at, 1] < 2)
    def _():
        work(h_ref)

    @pl.when(list_ref[at, 1] == 2)
    def _():
        work(g_ref)


def feed_grads(info, h, h_rows, g, g_rows, act, wanted, members):
    depth = h[0].shape[1]
    _, _, rows, units = act.shape
    size = depth // (2 * members)
    count = len(wanted)
    out = jax.ShapeDtypeStruct((count, members, units, size), bf16)
    return pl.pallas_call(
        functools.partial(feed_grad_kernel, tuple(h_rows), tuple(g_rows), members),
        name="feed_grads",
        grid_spec=pltpu.PrefetchScalarGridSpec(
            num_scalar_prefetch=2,
            grid=(count,),
            in_specs=[anywhere()] * (len(h) + len(g))
            + [pl.BlockSpec((1, 1, rows, units), lambda i, info, w: (w[i, 0], w[i, 1], 0, 0))],
            out_specs=[pl.BlockSpec((1, members, units, size), lambda i, info, w: (i, 0, 0, 0))]
            * 2,
            scratch_shapes=[
                pltpu.VMEM((rows, depth), bf16),
                pltpu.VMEM((rows, depth), bf16),
                pltpu.SemaphoreType.DMA((2 * members * len(h),)),
                pltpu.SemaphoreType.DMA((2 * members * len(g),)),
            ],
        ),
        out_shape=[out, out],
        compiler_params=pltpu.CompilerParams(vmem_limit_bytes=VMEM),
        cost_estimate=SMALL,
    )(info, jnp.asarray(wanted, jnp.int32), *h, *g, act)


def branch_back_kernel(n, parts, info_ref, dh_ref, mid_ref, g_ref, gain_ref, w_ref, *refs):
    far, refs = refs[:parts], refs[parts:]
    dm_ref, db_ref, gg_ref = refs[:3]
    da = refs[3:]
    at = pl.program_id(0)
    width = da[0].shape[1]
    x = mid_ref[...]
    inverse = lax.rsqrt(jnp.mean(x * x, axis=-1, keepdims=True) + EPS)
    unit = x * inverse
    received = far[0][...]
    for p in range(1, parts):
        received = jnp.where(at == p, far[p][...], received)
    cotangent = dh_ref[...] + received.astype(f32)
    e = cotangent * gain_ref[...]
    inner = jnp.mean(e * unit, axis=-1, keepdims=True)
    d_mid = g_ref[...].astype(f32) + inverse * (e - unit * inner)
    share = jnp.sum(cotangent * unit, axis=0, keepdims=True)

    @pl.when(at == 0)
    def _():
        gg_ref[...] = jnp.zeros_like(gg_ref)

    gg_ref[...] += share
    dm_ref[...] = d_mid
    rounded = d_mid.astype(bf16)
    db_ref[...] = rounded
    for j in range(n):
        da[j][...] = dot_nt(rounded, w_ref[j * width : (j + 1) * width, :]).astype(bf16)


def branch_back(info, d_h, d_far, middle, g, gain, w_all, width):
    n = w_all.shape[0] // width
    parts = len(d_far)
    rows, depth = middle.shape
    size = rows // parts
    whole = lambda i, info: (0, 0)
    row = lambda i, info: (i, 0)
    part = pl.BlockSpec((size, depth), row)
    return pl.pallas_call(
        functools.partial(branch_back_kernel, n, parts),
        name="branch_back",
        grid_spec=pltpu.PrefetchScalarGridSpec(
            num_scalar_prefetch=1,
            grid=(parts,),
            in_specs=[part, part, part]
            + [pl.BlockSpec(gain.shape, whole), pl.BlockSpec(w_all.shape, whole)]
            + [pl.BlockSpec((size, depth), whole)] * parts,
            out_specs=[part, part, pl.BlockSpec((1, depth), whole)]
            + [pl.BlockSpec((size, width), row)] * n,
        ),
        out_shape=[
            jax.ShapeDtypeStruct((rows, depth), f32),
            jax.ShapeDtypeStruct((rows, depth), bf16),
            jax.ShapeDtypeStruct((1, depth), f32),
        ]
        + [jax.ShapeDtypeStruct((rows, width), bf16)] * n,
        compiler_params=pltpu.CompilerParams(vmem_limit_bytes=VMEM),
        cost_estimate=SMALL,
    )(info, d_h, middle, g, gain, w_all, *d_far)


def out_grad_kernel(n, info_ref, *refs):
    db_ref = refs[0]
    att = refs[1 : 1 + n]
    o_ref = refs[1 + n]
    for j in range(n):
        o_ref[info_ref[0] ^ j] = dot_tn(db_ref[...], att[j][...]).astype(bf16)


def out_grads(info, d_branch, att):
    n = len(att)
    rows, depth = d_branch.shape
    width = att[0].shape[1]
    whole = lambda i, info: (0, 0)
    return pl.pallas_call(
        functools.partial(out_grad_kernel, n),
        name="out_grads",
        grid_spec=pltpu.PrefetchScalarGridSpec(
            num_scalar_prefetch=1,
            grid=(1,),
            in_specs=[pl.BlockSpec(d_branch.shape, whole)]
            + [pl.BlockSpec(a.shape, whole) for a in att],
            out_specs=pl.BlockSpec((n, depth, width), lambda i, info: (0, 0, 0)),
        ),
        out_shape=jax.ShapeDtypeStruct((n, depth, width), bf16),
        compiler_params=pltpu.CompilerParams(vmem_limit_bytes=VMEM),
        cost_estimate=SMALL,
    )(info, d_branch, *att)


def qkv_grad_kernel(rows, placed, info_ref, *refs):
    count = len(placed)
    pieces = refs[:count]
    d_ref, w_ref, sel_ref, out_ref, o_ref, share_ref, x_ref, sem = refs[count:]
    columns = sel_ref.shape[0]
    at = pl.program_id(0)
    block = o_ref.shape[0]

    @pl.when(at == 0)
    def _():
        copies = []
        for i, (ref, (j, first)) in enumerate(zip(pieces, placed)):
            size = ref.shape[0]
            place = pl.ds(pl.multiple_of((info_ref[0] ^ j) * rows + first, size), size)
            copies.append(pltpu.make_async_copy(ref, x_ref.at[place], sem.at[i]))
        for copy in copies:
            copy.start()
        for copy in copies:
            copy.wait()

    lanes = pl.ds(pl.multiple_of(at * block, block), block)
    g = dot_tn(x_ref[:, lanes], d_ref[...])
    share_ref[...] = jnp.sum(g * w_ref[...].astype(f32), axis=1, keepdims=True)
    o_ref[:, :columns] = dot_nt(g.astype(bf16), sel_ref[...]).astype(bf16)
    o_ref[:, columns:] = out_ref[...]


def qkv_grads(info, parts, d, w, select, beside, rows):
    length = d.shape[0]
    depth = w.shape[0]
    columns = select.shape[0]
    total = columns + beside.shape[1]
    block = 512
    placed = tuple((j, first) for _, j, first in parts)
    whole = lambda i, info: (0, 0)
    row = lambda i, info: (i, 0)
    return pl.pallas_call(
        functools.partial(qkv_grad_kernel, rows, placed),
        name="qkv_grads",
        grid_spec=pltpu.PrefetchScalarGridSpec(
            num_scalar_prefetch=1,
            grid=(depth // block,),
            in_specs=[anywhere()] * len(parts)
            + [
                pl.BlockSpec(d.shape, whole),
                pl.BlockSpec((block, w.shape[1]), row),
                pl.BlockSpec(select.shape, whole),
                pl.BlockSpec((block, beside.shape[1]), row),
            ],
            out_specs=[pl.BlockSpec((block, total), row), pl.BlockSpec((block, 1), row)],
            scratch_shapes=[
                pltpu.VMEM((length, depth), bf16),
                pltpu.SemaphoreType.DMA((len(parts),)),
            ],
        ),
        out_shape=[
            jax.ShapeDtypeStruct((depth, total), bf16),
            jax.ShapeDtypeStruct((depth, 1), f32),
        ],
        compiler_params=pltpu.CompilerParams(vmem_limit_bytes=VMEM),
        cost_estimate=SMALL,
    )(info, *[p for p, _, _ in parts], d, w, select, beside)


def finish_kernel(n, wide, info_ref, *refs):
    d = refs[:n]
    own_ref, cols_ref, tok_ref, gain_ref, dm_ref, o_ref = refs[n : n + 6]
    w_ref, sem = refs[-2:]
    t = info_ref[0]
    members, _, size, columns = cols_ref.shape
    depth = members * size
    first = pl.program_id(0) == 0
    copies = [
        pltpu.make_async_copy(cols_ref.at[:, j], w_ref.at[j], sem.at[j]) for j in range(n - 1)
    ]

    @pl.when(first)
    def _():
        for copy in copies:
            copy.start()

    o_ref[...] = dot_nt(d[0][...], own_ref[...])
    for j in range(n - 1):

        @pl.when(first)
        def _():
            copies[j].wait()

        o_ref[...] += dot_nt(d[j + 1][...], w_ref[j].reshape(depth, columns))
    x = tok_ref[...].astype(f32)
    inverse = lax.rsqrt(jnp.mean(x * x, axis=-1, keepdims=True) + EPS)
    unit = x * inverse
    e = o_ref[...] * gain_ref[...]
    inner = jnp.mean(e * unit, axis=-1, keepdims=True)
    o_ref[...] = dm_ref[...] + inverse * (e - unit * inner)
    if wide:
        first_ref = refs[n + 6]
        width = depth // n
        for j in range(n):
            at = pl.ds(pl.multiple_of((t ^ j) * width, width), width)
            first_ref[:, at] = d[j][:, 4 * LANES :].astype(f32)


def finish(info, d_parts, own, cols, tokens, gain, d_middle):
    n = len(d_parts)
    rows, depth = tokens.shape
    block = min(rows, 512)
    wide = (depth // n) % LANES == 0
    row = lambda i, info: (i, 0)
    whole = lambda i, info: (0, 0)
    count = 2 if wide else 1
    members, _, size, columns = cols.shape
    out = pl.pallas_call(
        functools.partial(finish_kernel, n, wide),
        name="finish",
        grid_spec=pltpu.PrefetchScalarGridSpec(
            num_scalar_prefetch=1,
            grid=(rows // block,),
            in_specs=[pl.BlockSpec((block, d.shape[1]), row) for d in d_parts]
            + [
                pl.BlockSpec(own.shape, whole),
                anywhere(),
                pl.BlockSpec((block, depth), row),
                pl.BlockSpec((1, depth), whole),
                pl.BlockSpec((block, depth), row),
            ],
            out_specs=[pl.BlockSpec((block, depth), row)] * count,
            scratch_shapes=[
                pltpu.VMEM((n - 1, members, size, columns), bf16),
                pltpu.SemaphoreType.DMA((n - 1,)),
            ],
        ),
        out_shape=[jax.ShapeDtypeStruct((rows, depth), f32)] * count,
        compiler_params=pltpu.CompilerParams(vmem_limit_bytes=VMEM),
        cost_estimate=LARGE,
    )(info, *d_parts, own, cols, tokens, gain, d_middle)
    if wide:
        return out
    heads_width = depth // n
    pieces_ = jnp.stack([d[:, 4 * LANES : 4 * LANES + heads_width] for d in d_parts])
    ordered = jnp.take(pieces_, info[0] ^ jnp.arange(n), axis=0)
    return out[0], ordered.transpose(1, 0, 2).reshape(rows, depth).astype(f32)


def shards(
    tokens,
    first_values,
    doc_lengths,
    attention_norm_gain,
    w_qkv,
    w_out,
    feedforward_norm_gain,
    w_gate,
    w_up,
    w_down,
    out_grad,
):
    n = lax.axis_size("tensor")
    high, low = split_axis(n)
    members = lax.axis_size("dp") // 2
    t = lax.axis_index("tensor")
    z, core = lax.axis_index("dp") // 2, lax.axis_index("dp") % 2
    info = jnp.stack([t, core]).astype(jnp.int32)
    rows, depth = tokens.shape
    heads = w_out.shape[0] // HD
    own_width = heads * HD
    width = max(LANES, own_width)
    length = rows * n
    block = min(256, rows)
    gain_one = attention_norm_gain[None, :]
    gain_two = feedforward_norm_gain[None, :]
    missing = width - own_width
    widen = lambda v: jnp.pad(v, ((0, 0), (0, missing))) if missing else v
    replicas = 2 * members
    size_d = depth // replicas
    mine = lambda w, axis: lax.dynamic_slice_in_dim(w, lax.axis_index("dp") * size_d, size_d, axis)

    together = lax.optimization_barrier
    cosine, sine_table = rope_tables(length)
    ends = jnp.cumsum(doc_lengths[0])
    starts = ends - doc_lengths[0]
    docs = doc_lengths.shape[1]
    limits = jnp.pad(jnp.stack([starts, ends]), ((0, 6), (HD, LANES - HD - docs)))
    heads_at = jnp.arange(length // block, dtype=jnp.int32) * block
    begins = jnp.max(jnp.where(starts[None, :] <= heads_at[:, None], starts[None, :], 0), axis=1)
    begins = (begins // block).astype(jnp.int32)
    select = column_selector(heads)
    w_cols = jnp.dot(w_qkv, select, preferred_element_type=f32).astype(bf16)

    own_weights = (w_gate.T, w_up.T, w_down)
    weight_slice = jnp.concatenate([mine(w, 1) for w in own_weights])
    value_parts = [
        widen(lax.dynamic_slice_in_dim(first_values, (t ^ j) * own_width, own_width, 1))
        for j in range(n)
    ]
    w_out_wide = jnp.pad(w_out, ((0, missing), (0, 0))) if missing else w_out
    out_slice = mine(w_out_wide, 1)
    normed = norm_rows(tokens, gain_one)
    value_parts, normed = together((value_parts, normed))
    normed_parts = gather_rows(normed, n)
    out_slices = [out_slice] + [swap("tensor", out_slice, j) for j in range(1, n)]
    w_out_all = over_replicas(jnp.concatenate(after(out_slices, normed)))
    value_parts = [value_parts[0]] + [swap("tensor", value_parts[j], j) for j in range(1, n)]
    placed = [(j, first) for _, j, first in normed_parts]
    pieces_in = [piece for piece, _, _ in normed_parts]
    cols_slice = mine(w_cols, 0)
    (
        pieces_in, value_parts, weight_slice, w_cols, cols_slice, cosine, sine_table, limits,
        grad_late, select,
    ) = together(
        (
            pieces_in, value_parts, weight_slice, w_cols, cols_slice, cosine, sine_table, limits,
            out_grad, select,
        )
    )

    far_slices = [swap("tensor", weight_slice, a * low) for a in range(1, high)]
    grad_rows = [out_grad] + [swap("tensor", grad_late, b) for b in range(1, low)]
    normed_parts = [(piece, j, first) for piece, (j, first) in zip(pieces_in, placed)]
    q, k, v, squares = project(
        heads, info, normed_parts, value_parts, w_cols, cosine, sine_table, limits, rows
    )
    q, far_slices, w_out_all = together((q, far_slices, w_out_all))
    seen = {}
    for j in range(n - 1, -1, -1):
        seen[j] = attend(heads, info, j, q, k, v, begins, block, rows)
        if j == 1:
            q, *grad_rows = together((q, *grad_rows))
    feed_far = [(over_replicas(w),) for w in far_slices]
    heads_rows = [seen[0][0]] + [swap("tensor", seen[j][0], j) for j in range(1, n)]
    heads_rows, cols_slice = together((heads_rows, cols_slice))

    parts = 2 if rows >= 512 else 1
    size = rows // parts
    middle, second, w_out_all, *second_parts = branch(
        info, heads_rows, w_out_all, tokens, gain_two, parts
    )
    second_parts, cols_slice = together((second_parts, cols_slice))
    far_keys = [(b, p) for b in range(1, low) for p in range(parts)]
    inputs = {(b, p): swap("tensor", second_parts[p], b) for b, p in far_keys}
    cols_far = [swap("tensor", cols_slice, j) for j in range(1, n)]
    shards_held = [own_weights] + feed_far
    own_out, own_back, act = feed(
        info, second, out_grad, 0, shards_held, 0, low * rows, [], 0, rows, False
    )
    shared, backs = [act], {}
    for b, p in far_keys:
        if (b, p) == far_keys[0]:
            inputs, shared = together((inputs, shared))
        if (b, p) == far_keys[-1]:
            cols_far, shared = together((cols_far, shared))
        arrived = inputs[b, p]
        to_send, backs[b, p], act = feed(
            info, arrived, grad_rows[b], p * size, shards_held, b * rows + p * size, low * rows,
            shared, (b - 1) * rows + p * size, (low - 1) * rows, True,
        )
        shared = [to_send, act]
    d_far = [[swap("tensor", backs[b, p], b) for b in range(1, low)] for p in range(parts)]
    d_far = [d[0] if low == 2 else add_up(*d) for d in d_far]
    sources = (
        [second] + [inputs[key] for key in far_keys],
        [0] + [b * rows + p * size for b, p in far_keys],
        grad_rows,
        [b * rows for b in range(low)],
    )
    d_far[0], act = together((d_far[0], act))
    cols = lax.all_gather(jnp.stack(cols_far), "dp", axis=0)
    wanted = [(a, m) for a in range(1, high) for m in range(3)] + [(0, 0), (0, 1), (0, 2)]
    keep, send = feed_grads(info, *sources, act, wanted, members)
    d_far, keep, send, to_send = together((d_far, keep, send, to_send))

    got = swap("dp", send, 1)
    d_middle, d_branch, feed_share, *d_att = branch_back(
        info, own_back, d_far, middle, out_grad, gain_two, w_out_all, width
    )
    d_att = [d_att[0]] + [swap("tensor", d_att[j], j) for j in range(1, n)]
    add_two = lambda lo, hi: add_up(keep[lo:hi], got[lo:hi]).astype(bf16)
    rest_sums = [add_two(3 * a + 1, 3 * a + 3) for a in range(high - 1)]
    rest_sums, got = together((rest_sums, got))
    gate_sums = jnp.stack(
        [add_two(i, i + 1)[0] for i in [3 * (high - 1)] + [3 * a for a in range(high - 1)]], axis=1
    )
    out_grad_w = out_grads(info, d_branch, heads_rows)
    d_att, to_send, out_grad_w, keep, got, cols = together(
        (d_att, to_send, out_grad_w, keep, got, cols)
    )

    gate_z = [
        swap("dp", lax.dynamic_index_in_dim(gate_sums, z ^ k, 0, keepdims=False), 2 * k)
        for k in range(1, members)
    ]
    rest_got = [swap("tensor", rest_sums[a - 1], a * low) for a in range(1, high)]
    out_got = [swap("tensor", to_send[(b - 1) * rows : b * rows], b) for b in range(1, low)]
    out_sum = lax.psum_scatter(out_grad_w, "tensor", scatter_dimension=0, tiled=False)
    d_cols = attend_back(
        heads, info, [seen[j][1] for j in range(n)], k, v, d_att, [seen[j][0] for j in range(n)],
        cosine, sine_table, begins, block,
    )
    d_cols, gate_z, out_got, keep = together((d_cols, gate_z, out_got, keep))

    d_all, *d_parts = d_cols
    rest_sum = add_up(keep[-2:], got[-2:], *rest_got).astype(bf16).swapaxes(0, 1)
    d_all, rest_sum = together((d_all, rest_sum))
    d_parts = [d_parts[0]] + [swap("tensor", d_parts[j], j) for j in range(1, n)]
    grads, share = qkv_grads(info, normed_parts, d_all, w_cols, select, out_sum, rows)
    grads = lax.psum_scatter(grads, "dp", scatter_dimension=0, tiled=True)
    gate_z, out_got, share = together((gate_z, out_got, share))
    step = 1
    if members > 1:
        rest_sum = halve_over_z(rest_sum, z, step, lambda half: after(half, share))
    gate_sum = add_up(
        lax.dynamic_index_in_dim(gate_sums, z, 0, keepdims=False), *gate_z
    ).astype(bf16)
    gate_sum = add_up(
        gate_sum[0], *[swap("tensor", gate_sum[a], a * low) for a in range(1, high)]
    )
    out = add_up(middle, own_out, *out_got).astype(bf16)
    totals = jnp.sum(squares[:2], axis=1)
    scalars = jnp.pad(totals[None, :], ((0, 0), (0, depth - 2)))
    shares = jnp.concatenate([share.reshape(1, depth) / gain_one, feed_share, scalars])
    reach = 1
    while reach < replicas:
        shares = all_sum("dp", shares, [reach])
        reach *= 2
    sums = all_sum("tensor", shares, range(1, n))
    d_parts, out, rest_sum, sums = together((d_parts, out, rest_sum, sums))
    while 2 * step < members:
        step *= 2
        rest_sum = halve_over_z(rest_sum, z, step, lambda half: half)
    rest_sum = rest_sum[0].astype(f32)
    tokens_grad, first_grad = finish(
        info, d_parts, w_cols, cols, tokens, gain_one, d_middle
    )
    tokens_grad, rest_sum = together((tokens_grad, rest_sum))
    columns = 3 * own_width
    entry_count = first_values.size * lax.axis_size("dp") * n
    return (
        out,
        tokens_grad,
        first_grad,
        sums[0],
        grads[:, :columns].astype(f32),
        grads[:, columns : columns + own_width].T.astype(f32),
        sums[1],
        gate_sum.T,
        rest_sum[0].T,
        rest_sum[1],
        jnp.sqrt(sums[2, 1] / entry_count),
        jnp.sqrt(sums[2, 0] / entry_count),
    )


def solution(mesh):
    token_spec = P(("dp", "tensor"), None)
    return jax.shard_map(
        shards,
        mesh=mesh,
        in_specs=(
            token_spec,
            token_spec,
            P("dp", None),
            P(),
            P(None, "tensor"),
            P("tensor", None),
            P(),
            P(None, "tensor"),
            P(None, "tensor"),
            P("tensor", None),
            token_spec,
        ),
        out_specs=(
            token_spec,
            token_spec,
            token_spec,
            P(),
            P("dp", "tensor"),
            P("tensor", "dp"),
            P(),
            P("dp", "tensor"),
            P("dp", "tensor"),
            P("tensor", "dp"),
            P(),
            P(),
        ),
        check_vma=False,
    )
```
